32 devices in a mesh: dp: 16 (over z, y, core), mp: 2 (over x).
Axes of the slice: x: 2, y: 2, z: 4, core: 2. Of those that a mesh axis runs over, the one named last changes fastest.
Arguments:
- activations: bfloat16 [2, 16384, 512], P(None, 'dp'), may hold values from -6 to 6
- cotangent: bfloat16 [2, 16384, 512], P(None, 'dp'), may hold values from -6 to 6
- w_qkv: bfloat16 [3, 512, 512], P(None, 'dp', 'mp'), may hold values from -0.25 to 0.25
- w_o: bfloat16 [512, 512], P('mp', 'dp'), may hold values from -0.75 to 0.75
- w_up: bfloat16 [512, 2048], P('dp', 'mp'), may hold values from -0.25 to 0.25
- w_down: bfloat16 [2048, 512], P('mp', 'dp'), may hold values from -0.125 to 0.125
- b_qv: bfloat16 [2, 8, 64], P(None, 'mp', 'dp'), may hold values from -3 to 3
- b_up: bfloat16 [32, 64], P('mp', 'dp'), may hold values from -3 to 3
- out_bias: bfloat16 [2, 512], P(None, 'dp'), may hold values from -3 to 3
- norm_gain: bfloat16 [2, 512], P(None, 'dp'), may hold values from 0.25 to 1.75
- norm_bias: bfloat16 [2, 512], P(None, 'dp'), may hold values from -2 to 2
- chain_ids: int32 [2, 16384], P(None, 'dp'), may hold values from -1 to 1023, as said below
- key_keep: int32 [2, 16384], P(None, 'dp'), may hold values 0 or 1
Outputs:
- output: float32 [2, 16384, 512], P(None, 'dp')
- grad_x: float32 [2, 16384, 512], P(None, 'dp')
- grad_w_qkv: float32 [3, 512, 512], P(None, 'dp', 'mp')
- grad_w_o: float32 [512, 512], P('mp', 'dp')
- grad_w_up: float32 [512, 2048], P('dp', 'mp')
- grad_w_down: float32 [2048, 512], P('mp', 'dp')
- grad_b_qv: float32 [2, 8, 64], P(None, 'mp', 'dp')
- grad_b_up: float32 [32, 64], P('mp', 'dp')
- grad_out_bias: float32 [2, 512], P(None, 'dp')
- grad_norm_gain: float32 [2, 512], P(None, 'dp')
- grad_norm_bias: float32 [2, 512], P(None, 'dp')
The draws below stay inside these ranges and needn't reach their ends.
Inputs may be any that keep to these rules, and one draw needn't show every extreme that they name: `chain_ids`: in each aligned block of 1024 slots along the last dimension, a live slot carries the index within the block of the first slot of its chain, chains are contiguous runs of live slots, the first slot of every block is live, and padding slots (-1) come after all live slots of their block; how many slots are live differs from block to block.
All inputs are finite; a program needn't handle non-finite values. No bound on the sum of `key_keep` on one device may be relied on, other than what follows from the above.
Results may differ from the reference program's by a relative error of at most 0.018.
Values may be sent and summed in bfloat16 or wider, within the bound.
A program may use at most 192 MiB of HBM per device.

```python
import math
import jax
import jax.numpy as jnp
from jax import lax

D = 512
H = 8
HD = 64
FF = 2048
SLOTS = 1024
MB = 2
TOKENS = 16384


def draw_chain_ids(key, part):
    blocks = MB * (TOKENS // SLOTS)
    key_fill, key_rate, key_flag = jax.random.split(key, 3)
    fill_count = jax.random.randint(key_fill, (blocks, 1), SLOTS // 2, SLOTS + 1)
    block_row = lax.broadcasted_iota(jnp.int32, (blocks, 1), 0)
    fill_count = jnp.where(block_row == 0, SLOTS, jnp.where(block_row == blocks - 1, SLOTS // 2, fill_count))
    start_rate = jax.random.randint(key_rate, (blocks, 1), 2, SLOTS // 4 + 3)
    coin_draw = jax.random.randint(key_flag, (blocks, SLOTS), 0, 65536)
    slot_index = lax.broadcasted_iota(jnp.int32, (blocks, SLOTS), 1)
    starts = (coin_draw * start_rate < 65536) | (slot_index == 0) | (block_row == 0) & (slot_index == SLOTS - 1)
    labels = lax.cummax(jnp.where(starts, slot_index, 0), axis=1)
    labels = jnp.where(slot_index < fill_count, labels, -1)
    return labels.reshape(MB, TOKENS).astype(jnp.int32)


def touch_ends(drawn, stream_key, least, largest):
    longest = drawn.shape.index(max(drawn.shape))
    spots = []
    for shift in (0, 1):
        where = [jax.random.randint(jax.random.fold_in(stream_key, axis), (), 0, length) for axis, length in enumerate(drawn.shape)]
        where[longest] = (where[longest] + shift) % drawn.shape[longest]
        spots.append(tuple(where))
    return drawn.at[spots[0]].set(least).at[spots[1]].set(largest)


def levels(key, shape, pieces, low, high):
    loudness, own = 1.0, jax.random.fold_in(key, 6)
    for position, blocks in pieces:
        heights = jnp.exp(jax.random.uniform(jax.random.fold_in(own, position), (blocks,), jnp.float32, low / len(pieces), high / len(pieces)))
        loudness = loudness * jnp.repeat(heights, shape[position] // blocks).reshape([-1 if axis == position else 1 for axis in range(len(shape))])
    return loudness


def normal_values(rng, shape, deviation, reach, cuts=(), held_as=jnp.bfloat16):
    level = levels(rng, shape, cuts, -0.22, 0.18) if cuts else 1.0
    values = jax.random.normal(rng, shape, jnp.float32) * deviation * level
    return jnp.minimum(jnp.maximum(values, -reach), reach).astype(held_as)


def setup_inputs(seed: int = 0) -> dict:
    streams_of = jax.random.split(jax.random.key(seed), 14)
    return {
        "activations": normal_values(streams_of[0], (MB, TOKENS, D), 1.0, 6.0, ((1, 16),)),
        "cotangent": normal_values(streams_of[1], (MB, TOKENS, D), 1.0, 6.0, ((1, 16),)),
        "w_qkv": normal_values(streams_of[2], (3, D, D), D ** -0.5, 0.25, ((1, 16), (2, 2))),
        "w_o": normal_values(streams_of[3], (D, D), HD ** -0.5, 0.75, ((0, 2), (1, 16))),
        "w_up": normal_values(streams_of[4], (D, FF), D ** -0.5, 0.25, ((0, 16), (1, 2))),
        "w_down": normal_values(streams_of[5], (FF, D), FF ** -0.5, 0.125, ((0, 2), (1, 16))),
        "b_qv": normal_values(streams_of[6], (2, H, HD), 0.5, 3.0, ((1, 2), (2, 16))),
        "b_up": normal_values(streams_of[7], (FF // 64, 64), 0.5, 3.0, ((0, 2), (1, 16))),
        "out_bias": normal_values(streams_of[8], (2, D), 0.5, 3.0, ((1, 16),)),
        "norm_gain": jnp.clip(1.0 + 0.15 * jax.random.normal(streams_of[9], (2, D), jnp.float32), 0.25, 1.75).astype(jnp.bfloat16),
        "norm_bias": normal_values(streams_of[10], (2, D), 0.3, 2.0, ((1, 16),)),
        "chain_ids": draw_chain_ids(jax.random.fold_in(streams_of[13], 71), 0),
        "key_keep": touch_ends((jax.random.randint(streams_of[12], (MB, TOKENS), 0, 10) < 9).astype(jnp.int32), jax.random.fold_in(streams_of[12], 1), 0, 1),
    }


@jax.custom_vjp
def low(v):
    return lax.optimization_barrier(v.astype(jnp.bfloat16)).astype(jnp.float32)

@jax.custom_vjp
def low_back(v):
    return v

def low_keep(v):
    return (low(v), None)

def low_pass(kept, grad):
    return (grad,)

def back_keep(v):
    return (v, None)

def back_low(kept, grad):
    return (low(grad),)
low.defvjp(low_keep, low_pass)
low_back.defvjp(back_keep, back_low)
epsilon = 1e-05
masked_value = -1e+30

def matmul(left, right):
    return jnp.dot(left, right, precision=lax.Precision.HIGHEST, preferred_element_type=jnp.float32)

def normalize(values, scale_row, shift_row):
    row_mean = lax.optimization_barrier(jnp.mean(values, axis=-1, keepdims=True))
    centred = values - row_mean
    inverse = lax.rsqrt(lax.optimization_barrier(jnp.mean(centred * centred, axis=-1, keepdims=True)) + epsilon)
    return centred * inverse * scale_row + shift_row

def attend_block(operands):
    query, key_rows, value_rows, chain_rows, keep_rows = operands
    slot_count = chain_rows.shape[0]
    same_chain = chain_rows[:, None] == chain_rows[None, :]
    diagonal = lax.broadcasted_iota(jnp.int32, (slot_count, slot_count), 0) == lax.broadcasted_iota(jnp.int32, (slot_count, slot_count), 1)
    allowed = same_chain & ((keep_rows[None, :] == 1) | diagonal)
    scores = jnp.einsum('qhd,khd->hqk', query, key_rows, precision=lax.Precision.HIGHEST) * (1.0 / math.sqrt(query.shape[2]))
    scores = low_back(scores)
    scores = jnp.where(allowed[None], scores, masked_value)
    row_top = lax.optimization_barrier(jnp.max(scores, axis=-1, keepdims=True))
    expo = jnp.exp(scores - row_top)
    probs = low(expo / lax.optimization_barrier(jnp.sum(expo, axis=-1, keepdims=True)))
    return jnp.einsum('hqk,khd->qhd', probs, value_rows, precision=lax.Precision.HIGHEST)

def reference(activations, cotangent, w_qkv, w_o, w_up, w_down, b_qv, b_up, out_bias, norm_gain, norm_bias, chain_ids, key_keep):
    row_count = MB * TOKENS
    chain_blocks = chain_ids.reshape(-1, SLOTS).astype(jnp.int32)
    keep_blocks = key_keep.reshape(-1, SLOTS).astype(jnp.int32)
    live_rows = (chain_ids >= 0).astype(jnp.float32)[:, :, None]

    def forward(inputs, qkv_full, out_full, up_full, down_full, bias_qv, bias_up, bias_out, gain_full, shift_full):
        rows_in = inputs.reshape(row_count, D)
        hidden_one = low(normalize(rows_in, gain_full[0], shift_full[0]))
        query = low_back(low(matmul(hidden_one, qkv_full[0]) + bias_qv[0].reshape(D)))
        key_rows = low_back(low(matmul(hidden_one, qkv_full[1])))
        value_rows = low_back(low(matmul(hidden_one, qkv_full[2]) + bias_qv[1].reshape(D)))
        block_shape = (-1, SLOTS, H, HD)
        mixed = lax.map(jax.checkpoint(attend_block), (query.reshape(block_shape), key_rows.reshape(block_shape), value_rows.reshape(block_shape), chain_blocks, keep_blocks))
        mixed = low_back(low(mixed.reshape(row_count, D)))
        resid = rows_in + low_back(matmul(mixed, out_full)) + bias_out[0]
        hidden_two = low(normalize(resid, gain_full[1], shift_full[1]))
        pre = low_back(matmul(hidden_two, up_full) + bias_up.reshape(FF))
        act = low(jax.nn.gelu(pre, approximate=False))
        result = resid + low_back(matmul(act, down_full)) + bias_out[1]
        return result.reshape(MB, TOKENS, D)
    output, pullback = jax.vjp(forward, activations.astype(jnp.float32), w_qkv.astype(jnp.float32), w_o.astype(jnp.float32), w_up.astype(jnp.float32), w_down.astype(jnp.float32), b_qv.astype(jnp.float32), b_up.astype(jnp.float32), out_bias.astype(jnp.float32), norm_gain.astype(jnp.float32), norm_bias.astype(jnp.float32))
    grad_x, grad_w_qkv, grad_w_o, grad_w_up, grad_w_down, grad_b_qv, grad_b_up, grad_out_bias, grad_norm_gain, grad_norm_bias = pullback(cotangent.astype(jnp.float32) * live_rows)
    return (output, grad_x, grad_w_qkv, grad_w_o, grad_w_up, grad_w_down, grad_b_qv, grad_b_up, grad_out_bias, grad_norm_gain, grad_norm_bias)
```

```python
import math

import jax
import jax.numpy as jnp
from jax import lax
from jax.sharding import PartitionSpec as P

epsilon = 1e-05
masked_value = -1e30


def product(left, right):
    return jnp.dot(left, right, preferred_element_type=jnp.float32)


def normalize(values, scale_row, shift_row):
    row_mean = jnp.mean(values, axis=-1, keepdims=True)
    centred = values - row_mean
    inverse = lax.rsqrt(jnp.mean(centred * centred, axis=-1, keepdims=True) + epsilon)
    scaled = centred * inverse
    return (scaled * scale_row + shift_row, scaled, inverse)


def normalize_back(grad_rows, scaled, inverse, scale_row):
    inner = grad_rows * scale_row
    return inverse * (
        inner
        - jnp.mean(inner, axis=-1, keepdims=True)
        - scaled * jnp.mean(inner * scaled, axis=-1, keepdims=True)
    )


def gelu_slope(values):
    normal_cdf = 0.5 * (1.0 + lax.erf(values * 0.7071067811865476))
    density = jnp.exp(-0.5 * values * values) * 0.3989422804014327
    return normal_cdf + values * density


def permitted(chain_rows, keep_rows):
    slot_count = chain_rows.shape[0]
    same_chain = chain_rows[:, None] == chain_rows[None, :]
    diagonal = lax.broadcasted_iota(jnp.int32, (slot_count, slot_count), 0) == lax.broadcasted_iota(
        jnp.int32, (slot_count, slot_count), 1
    )
    return same_chain & ((keep_rows[None, :] == 1) | diagonal)


def head_scores(query, key_rows, allowed, head_count, head_width):
    query_heads = query.reshape(-1, head_count, head_width)
    key_heads = key_rows.reshape(-1, head_count, head_width)
    scores = jnp.einsum(
        "qhd,khd->hqk", query_heads, key_heads, preferred_element_type=jnp.float32
    ) * (1.0 / math.sqrt(head_width))
    return jnp.where(allowed[None], scores, masked_value)


def forward(rows_in, chain_rows, keep_rows, weights, join=lambda a: a):
    qkv_full, out_full, up_full, down_full, bias_qv, bias_up, bias_out, gain_full, shift_full = (
        weights
    )
    head_count = bias_qv.shape[1]
    head_width = bias_qv.shape[2]
    row_count = rows_in.shape[0]
    bias_qv = bias_qv.astype(jnp.float32)
    bias_out = bias_out.astype(jnp.float32)
    gain_full = gain_full.astype(jnp.float32)
    shift_full = shift_full.astype(jnp.float32)
    allowed = permitted(chain_rows, keep_rows)
    normed_one, scaled_one, inverse_one = normalize(rows_in, gain_full[0], shift_full[0])
    hidden_one = normed_one.astype(jnp.bfloat16)
    query = (product(hidden_one, qkv_full[0]) + bias_qv[0].reshape(-1)).astype(jnp.bfloat16)
    key_rows = product(hidden_one, qkv_full[1]).astype(jnp.bfloat16)
    value_rows = (product(hidden_one, qkv_full[2]) + bias_qv[1].reshape(-1)).astype(jnp.bfloat16)
    scores = head_scores(query, key_rows, allowed, head_count, head_width)
    row_top = jnp.max(scores, axis=-1, keepdims=True)
    log_total = jnp.log(jnp.sum(jnp.exp(scores - row_top), axis=-1, keepdims=True)) + row_top
    probs_low = jnp.exp(scores - log_total).astype(jnp.bfloat16)
    mixed = jnp.einsum(
        "hqk,khd->qhd",
        probs_low,
        value_rows.reshape(row_count, head_count, head_width),
        preferred_element_type=jnp.float32,
    )
    mixed = mixed.reshape(row_count, -1).astype(jnp.bfloat16)
    partial_attn = product(mixed, out_full)
    resid = rows_in + join(partial_attn) + bias_out[0]
    normed_two, scaled_two, inverse_two = normalize(resid, gain_full[1], shift_full[1])
    hidden_two = normed_two.astype(jnp.bfloat16)
    pre = product(hidden_two, up_full) + bias_up.astype(jnp.float32).reshape(-1)
    act = jax.nn.gelu(pre, approximate=False).astype(jnp.bfloat16)
    partial_ffn = product(act, down_full)
    result = (
        resid + join(partial_ffn.astype(jnp.bfloat16)).astype(jnp.float32) + bias_out[1]
    )
    kept = (
        allowed,
        scaled_one,
        inverse_one,
        hidden_one,
        query,
        key_rows,
        value_rows,
        log_total,
        mixed,
        scaled_two,
        inverse_two,
        hidden_two,
        pre,
        act,
    )
    return (result, kept)


def backward(grad_out, result, kept, weights, join=lambda a: a):
    qkv_full, out_full, up_full, down_full, bias_qv, bias_up, bias_out, gain_full, shift_full = (
        weights
    )
    (
        allowed,
        scaled_one,
        inverse_one,
        hidden_one,
        query,
        key_rows,
        value_rows,
        log_total,
        mixed,
        scaled_two,
        inverse_two,
        hidden_two,
        pre,
        act,
    ) = kept
    head_count = bias_qv.shape[1]
    head_width = bias_qv.shape[2]
    row_count = grad_out.shape[0]
    gain_full = gain_full.astype(jnp.float32)
    grad_low = grad_out.astype(jnp.bfloat16)
    grad_down = product(act.T, grad_low)
    grad_pre = (product(grad_low, down_full.T) * gelu_slope(pre)).astype(jnp.bfloat16)
    grad_bup = jnp.sum(grad_pre, axis=0, dtype=jnp.float32).reshape(bias_up.shape)
    grad_up = product(hidden_two.T, grad_pre)
    partial_two = product(grad_pre, up_full.T)
    grad_two = join(partial_two.astype(jnp.bfloat16)).astype(jnp.float32)
    gain_two = jnp.sum(grad_two * scaled_two, axis=0)
    shift_two = jnp.sum(grad_two, axis=0)
    grad_resid = grad_out + normalize_back(grad_two, scaled_two, inverse_two, gain_full[1])
    resid_low = grad_resid.astype(jnp.bfloat16)
    grad_out_proj = product(mixed.T, resid_low)
    grad_mixed = (
        product(resid_low, out_full.T)
        .astype(jnp.bfloat16)
        .reshape(row_count, head_count, head_width)
    )
    scores = head_scores(query, key_rows, allowed, head_count, head_width)
    probs = jnp.exp(scores - log_total)
    probs_low = probs.astype(jnp.bfloat16)
    value_heads = value_rows.reshape(row_count, head_count, head_width)
    grad_value = jnp.einsum(
        "hqk,qhd->khd", probs_low, grad_mixed, preferred_element_type=jnp.float32
    ).astype(jnp.bfloat16)
    grad_probs = jnp.einsum(
        "qhd,khd->hqk", grad_mixed, value_heads, preferred_element_type=jnp.float32
    )
    grad_scores = (
        probs * (grad_probs - jnp.sum(grad_probs * probs, axis=-1, keepdims=True))
    ).astype(jnp.bfloat16)
    score_scale = 1.0 / math.sqrt(head_width)
    key_heads = key_rows.reshape(row_count, head_count, head_width)
    query_heads = query.reshape(row_count, head_count, head_width)
    grad_query = (
        jnp.einsum("hqk,khd->qhd", grad_scores, key_heads, preferred_element_type=jnp.float32)
        * score_scale
    ).astype(jnp.bfloat16)
    grad_key = (
        jnp.einsum("hqk,qhd->khd", grad_scores, query_heads, preferred_element_type=jnp.float32)
        * score_scale
    ).astype(jnp.bfloat16)
    stacked = jnp.stack(
        [
            grad_query.reshape(row_count, -1),
            grad_key.reshape(row_count, -1),
            grad_value.reshape(row_count, -1),
        ]
    )
    grad_qkv = jnp.einsum("rd,crk->cdk", hidden_one, stacked, preferred_element_type=jnp.float32)
    partial_one = jnp.einsum("crk,cdk->rd", stacked, qkv_full, preferred_element_type=jnp.float32)
    grad_one = join(partial_one.astype(jnp.bfloat16)).astype(jnp.float32)
    grad_bqv = jnp.stack(
        [
            jnp.sum(stacked[0], axis=0, dtype=jnp.float32),
            jnp.sum(stacked[2], axis=0, dtype=jnp.float32),
        ]
    ).reshape(2, head_count, head_width)
    gain_one = jnp.sum(grad_one * scaled_one, axis=0)
    shift_one = jnp.sum(grad_one, axis=0)
    grad_in = grad_resid + normalize_back(grad_one, scaled_one, inverse_one, gain_full[0])
    small_sums = jnp.stack(
        [
            jnp.sum(grad_resid, axis=0),
            jnp.sum(grad_out, axis=0),
            gain_one,
            gain_two,
            shift_one,
            shift_two,
        ]
    )
    local_grads = (
        grad_qkv,
        grad_out_proj,
        grad_up,
        grad_down,
        grad_bqv,
        grad_bup,
        small_sums[0:2],
        small_sums[2:4],
        small_sums[4:6],
    )
    return (result, grad_in, local_grads)


def body_generic(
    activations,
    cotangent,
    w_qkv,
    w_o,
    w_up,
    w_down,
    b_qv,
    b_up,
    out_bias,
    norm_gain,
    norm_bias,
    chain_ids,
    key_keep,
):
    batch_count = activations.shape[0]
    outputs = []
    input_grads = []
    running = None
    for batch_index in range(batch_count):
        weights = (
            lax.all_gather(w_qkv, "dp", axis=1, tiled=True),
            lax.all_gather(w_o, "dp", axis=1, tiled=True),
            lax.all_gather(w_up, "dp", axis=0, tiled=True),
            lax.all_gather(w_down, "dp", axis=1, tiled=True),
            lax.all_gather(b_qv, "dp", axis=2, tiled=True),
            lax.all_gather(b_up, "dp", axis=1, tiled=True),
            lax.all_gather(out_bias, "dp", axis=1, tiled=True),
            lax.all_gather(norm_gain, "dp", axis=1, tiled=True),
            lax.all_gather(norm_bias, "dp", axis=1, tiled=True),
        )
        result, kept = forward(
            activations[batch_index].astype(jnp.float32),
            chain_ids[batch_index],
            key_keep[batch_index],
            weights,
            lambda a: lax.psum(a, "mp"),
        )
        live_rows = (chain_ids[batch_index] >= 0).astype(jnp.float32)[:, None]
        output_rows, grad_in, local_grads = backward(
            cotangent[batch_index].astype(jnp.float32) * live_rows, result, kept, weights, lambda a: lax.psum(a, "mp")
        )
        outputs.append(output_rows)
        input_grads.append(grad_in)
        shares = (
            lax.psum_scatter(
                local_grads[0].astype(jnp.bfloat16), "dp", scatter_dimension=1, tiled=True
            ).astype(jnp.float32),
            lax.psum_scatter(
                local_grads[1].astype(jnp.bfloat16), "dp", scatter_dimension=1, tiled=True
            ).astype(jnp.float32),
            lax.psum_scatter(
                local_grads[2].astype(jnp.bfloat16), "dp", scatter_dimension=0, tiled=True
            ).astype(jnp.float32),
            lax.psum_scatter(
                local_grads[3].astype(jnp.bfloat16), "dp", scatter_dimension=1, tiled=True
            ).astype(jnp.float32),
            lax.psum_scatter(
                local_grads[4].astype(jnp.bfloat16), "dp", scatter_dimension=2, tiled=True
            ).astype(jnp.float32),
            lax.psum_scatter(
                local_grads[5].astype(jnp.bfloat16), "dp", scatter_dimension=1, tiled=True
            ).astype(jnp.float32),
            lax.psum_scatter(
                local_grads[6].astype(jnp.bfloat16), "dp", scatter_dimension=1, tiled=True
            ).astype(jnp.float32),
            lax.psum_scatter(
                local_grads[7].astype(jnp.bfloat16), "dp", scatter_dimension=1, tiled=True
            ).astype(jnp.float32),
            lax.psum_scatter(
                local_grads[8].astype(jnp.bfloat16), "dp", scatter_dimension=1, tiled=True
            ).astype(jnp.float32),
        )
        if running is None:
            running = tuple(shares)
        else:
            running = tuple(jax.tree.map(jnp.add, tuple(running), tuple(shares)))
    return (
        jnp.stack(outputs),
        jnp.stack(input_grads),
        running[0],
        running[1],
        running[2],
        running[3],
        running[4],
        running[5],
        running[6],
        running[7],
        running[8],
    )


def cat_weights(w_qkv, w_o, w_up, w_down):
    mixed_part = jnp.concatenate([w_qkv[0], w_qkv[1], w_qkv[2], w_o.T], axis=1)
    return jnp.stack([w_up, w_down.T, mixed_part])


def cat_small(b_qv, b_up, out_bias, norm_gain, norm_bias):
    parts = [b_qv.reshape(-1), b_up.reshape(-1), out_bias.reshape(-1), norm_gain.reshape(-1), norm_bias.reshape(-1)]
    return jnp.concatenate(parts)


def body_split(
    activations,
    cotangent,
    w_qkv,
    w_o,
    w_up,
    w_down,
    b_qv,
    b_up,
    out_bias,
    norm_gain,
    norm_bias,
    chain_ids,
    key_keep,
):
    own = lax.axis_index("mp")
    mp = lax.axis_size("mp")
    dp = lax.axis_size("dp")
    width = out_bias.shape[1] * dp
    local_heads, local_hd = b_qv.shape[1], b_qv.shape[2]
    packed = cat_weights(w_qkv, w_o, w_up, w_down)
    small = cat_small(b_qv, b_up, out_bias, norm_gain, norm_bias)
    full = lax.all_gather(packed, ("mp", "dp"), axis=0, tiled=False)
    full = full.reshape(mp, dp, 3, -1, packed.shape[2])
    full = full.transpose(2, 0, 1, 3, 4).reshape(3, mp, width, packed.shape[2])
    smalls = lax.all_gather(small, ("mp", "dp"), axis=0, tiled=False).reshape(mp, dp, -1)
    sizes = [b_qv.size, b_up.size, out_bias.size, norm_gain.size, norm_bias.size]
    offs = [0]
    for s in sizes:
        offs.append(offs[-1] + s)
    piece = lambda k: smalls[:, :, offs[k] : offs[k + 1]]
    bias_qv = piece(0).reshape(mp, dp, 2, local_heads, local_hd).transpose(2, 0, 3, 1, 4).reshape(2, mp * local_heads, dp * local_hd)
    bias_up = piece(1).reshape(mp, dp, b_up.shape[0], b_up.shape[1]).transpose(0, 2, 1, 3).reshape(mp * b_up.shape[0], -1)
    vec = lambda k: piece(k)[0].reshape(dp, 2, -1).transpose(1, 0, 2).reshape(2, width)
    bias_out, gain_full, shift_full = vec(2), vec(3), vec(4)
    q4 = packed.shape[2] // 4
    pick = lambda c: full[2, :, :, c * q4 : (c + 1) * q4].transpose(1, 0, 2).reshape(width, mp * q4)
    qkv_full = jnp.stack([pick(0), pick(1), pick(2)])
    out_full = pick(3).T
    up_full = full[0].transpose(1, 0, 2).reshape(width, -1)
    down_full = full[1].transpose(0, 2, 1).reshape(-1, width)
    weights = (qkv_full, out_full, up_full, down_full, bias_qv, bias_up, bias_out, gain_full, shift_full)
    take = lambda a: lax.dynamic_index_in_dim(a, own, 0, keepdims=False)
    chain_rows = take(chain_ids)
    result, kept = forward(take(activations).astype(jnp.float32), chain_rows, take(key_keep), weights)
    live_rows = (chain_rows >= 0).astype(jnp.float32)[:, None]
    output_rows, grad_in, grads = backward(take(cotangent).astype(jnp.float32) * live_rows, result, kept, weights)
    both = jnp.stack([output_rows, grad_in]).astype(jnp.bfloat16)
    gathered = lax.all_gather(both, "mp", axis=0, tiled=False).astype(jnp.float32)
    g_qkv, g_o, g_up, g_down, g_bqv, g_bup, g_bias, g_gain, g_shift = grads
    halves = lambda a: a.reshape(a.shape[0], mp, -1).transpose(1, 0, 2)
    g_mix = jnp.concatenate([halves(g_qkv[0]), halves(g_qkv[1]), halves(g_qkv[2]), halves(g_o.T)], axis=2)
    g_all = jnp.stack([halves(g_up), halves(g_down.T), g_mix]).astype(jnp.bfloat16)
    g_all = g_all.reshape(3, mp, dp, width // dp, -1).transpose(1, 2, 0, 3, 4)
    g_all = g_all.reshape(mp * dp, 3, width // dp, -1)
    g_own = lax.psum_scatter(g_all, ("mp", "dp"), scatter_dimension=0, tiled=False).astype(jnp.float32)
    s_qv = g_bqv.reshape(2, mp, local_heads, dp, local_hd).transpose(1, 3, 0, 2, 4).reshape(mp, dp, -1)
    s_up = g_bup.reshape(mp, b_up.shape[0], dp, b_up.shape[1]).transpose(0, 2, 1, 3).reshape(mp, dp, -1)
    rep = lambda a: jnp.broadcast_to(a.reshape(2, dp, -1).transpose(1, 0, 2).reshape(1, dp, -1), (mp, dp, 2 * width // dp))
    s_all = jnp.concatenate([s_qv, s_up, rep(g_bias), rep(g_gain), rep(g_shift)], axis=2)
    s_all = s_all.reshape(mp * dp, -1)
    s_sum = lax.psum(s_all, ("mp", "dp"))
    s_own = lax.dynamic_index_in_dim(s_sum, own * dp + lax.axis_index("dp"), 0, keepdims=False)
    part = lambda k, a: s_own[offs[k] : offs[k + 1]].reshape(a.shape)
    mix = g_own[2]
    return (
        gathered[:, 0],
        gathered[:, 1],
        jnp.stack([mix[:, c * q4 : (c + 1) * q4] for c in range(3)]),
        mix[:, 3 * q4 :].T,
        g_own[0],
        g_own[1].T,
        part(0, b_qv),
        part(1, b_up),
        part(2, out_bias),
        part(3, norm_gain),
        part(4, norm_bias),
    )

def solution(mesh):
    placed = (
        P(None, "dp", None),
        P(None, "dp", None),
        P(None, "dp", "mp"),
        P("mp", "dp"),
        P("dp", "mp"),
        P("mp", "dp"),
        P(None, "mp", "dp"),
        P("mp", "dp"),
        P(None, "dp"),
        P(None, "dp"),
        P(None, "dp"),
        P(None, "dp"),
        P(None, "dp"),
    )
    body = body_split if mesh.shape["mp"] == 2 else body_generic
    return jax.shard_map(
        body,
        mesh=mesh,
        in_specs=placed,
        out_specs=(
            P(None, "dp", None),
            P(None, "dp", None),
            P(None, "dp", "mp"),
            P("mp", "dp"),
            P("dp", "mp"),
            P("mp", "dp"),
            P(None, "mp", "dp"),
            P("mp", "dp"),
            P(None, "dp"),
            P(None, "dp"),
            P(None, "dp"),
        ),
        check_vma=False,
    )
```

```python
import functools
import math

import jax
import jax.numpy as jnp
from jax import lax
from jax.experimental import pallas as pl
from jax.experimental.pallas import tpu as pltpu
from jax.sharding import PartitionSpec as P

epsilon = 1e-05
masked_value = -1e30
TILE = 256
FULL = pl.BlockSpec(memory_space=pltpu.VMEM)

GAIN1, SHIFT1, GAIN2, SHIFT2, BQ, BV, BO1, BO2 = range(8)


def dot(left, right):
    return jnp.dot(left, right, preferred_element_type=jnp.float32)


def dot_last(left, right):
    return lax.dot_general(left, right, (((1,), (1,)), ((), ())), preferred_element_type=jnp.float32)


def dot_first(left, right):
    return lax.dot_general(left, right, (((0,), (0,)), ((), ())), preferred_element_type=jnp.float32)


def tile_rows(index):
    return pl.ds(pl.multiple_of(index * TILE, TILE), TILE)


def statistics(values):
    centred = values - jnp.mean(values, axis=-1, keepdims=True)
    inverse = lax.rsqrt(jnp.mean(centred * centred, axis=-1, keepdims=True) + epsilon)
    return centred * inverse, inverse


def norm_back(grad, scaled, inverse, gain):
    inner = grad * gain
    return inverse * (
        inner - jnp.mean(inner, axis=-1, keepdims=True) - scaled * jnp.mean(inner * scaled, axis=-1, keepdims=True)
    )


def add_row(ref, row, values):
    ref[row : row + 1, :] += jnp.sum(values, axis=0, keepdims=True)


def qkv_phase(x, w_mix, vecs, h1t, query, key, value):
    halves, quarter = query.shape[0], query.shape[2]
    scale = 1.0 / math.sqrt(64)

    def step(tile, _):
        rows = tile_rows(tile)
        scaled, _ = statistics(x[rows, :].astype(jnp.float32))
        hidden = (scaled * vecs[GAIN1 : GAIN1 + 1, :] + vecs[SHIFT1 : SHIFT1 + 1, :]).astype(jnp.bfloat16)
        h1t[:, rows] = hidden.T
        for half in range(halves):
            cols = slice(half * quarter, (half + 1) * quarter)
            part = lambda c: dot(hidden, w_mix[half, :, c * quarter : (c + 1) * quarter])
            query[half, rows, :] = ((part(0) + vecs[BQ : BQ + 1, cols]).astype(jnp.bfloat16) * scale).astype(jnp.bfloat16)
            key[half, rows, :] = part(1).astype(jnp.bfloat16)
            value[half, rows, :] = (part(2) + vecs[BV : BV + 1, cols]).astype(jnp.bfloat16)
        return 0

    lax.fori_loop(0, x.shape[0] // TILE, step, 0)


def attend_phase(query, key, value, marks_row, marks_col, bias, mixed, logs):
    halves, slots, quarter = query.shape

    def tile_step(tile, _):
        rows = tile_rows(tile)
        same = marks_col[rows, 0:1] == marks_row[1:2, :]
        here = lax.broadcasted_iota(jnp.int32, (TILE, slots), 0) + tile * TILE
        there = lax.broadcasted_iota(jnp.int32, (TILE, slots), 1)
        bias[...] = jnp.where(same | (here == there), 0.0, masked_value)

        def half_step(half, _):
            lane = lax.broadcasted_iota(jnp.int32, (TILE, 128), 1)
            stats = jnp.zeros((TILE, 128), jnp.float32)
            for pair in range(quarter // 128):
                cols = slice(pair * 128, (pair + 1) * 128)
                both = query[half, rows, cols]
                keys = key[half, :, cols]
                values = value[half, :, cols]
                sums = []
                for side in range(2):
                    mine = (lane < 64) if side == 0 else (lane >= 64)
                    scores = dot_last(jnp.where(mine, both, jnp.zeros_like(both)), keys) + bias[...]
                    top = jnp.max(scores, axis=1, keepdims=True)
                    expo = jnp.exp(scores - top)
                    total = jnp.sum(expo, axis=1, keepdims=True)
                    sums.append(dot(expo.astype(jnp.bfloat16), values) * (1.0 / total))
                    stats = jnp.where(lane == pair * 2 + side, top + jnp.log(total), stats)
                mixed[half, rows, cols] = jnp.where(lane < 64, sums[0], sums[1]).astype(jnp.bfloat16)
            logs[half, :, rows] = stats.T[0:4, :]
            return 0

        lax.fori_loop(0, halves, half_step, 0)
        return 0

    lax.fori_loop(0, slots // TILE, tile_step, 0)


def middle_phase(x, cot, live_col, w_up, w_down, w_mix, vecs, b_up, mixed, h2t, glowt, glow2t, act, gpre, gmix, dots, out, gres, sums, sums_up):
    halves, quarter, hidden_half = mixed.shape[0], mixed.shape[2], w_up.shape[2]

    def step(tile, _):
        rows = tile_rows(tile)
        attn = sum(dot_last(mixed[half, rows, :], w_mix[half, :, 3 * quarter : 4 * quarter]) for half in range(halves))
        resid = x[rows, :].astype(jnp.float32) + attn + vecs[BO1 : BO1 + 1, :]
        scaled, inverse = statistics(resid)
        hidden = (scaled * vecs[GAIN2 : GAIN2 + 1, :] + vecs[SHIFT2 : SHIFT2 + 1, :]).astype(jnp.bfloat16)
        h2t[:, rows] = hidden.T
        grad_out = cot[rows, :].astype(jnp.float32) * live_col[rows, 2:3]
        grad_low = grad_out.astype(jnp.bfloat16)
        glowt[:, rows] = grad_low.T
        ffn = jnp.zeros(resid.shape, jnp.float32)
        grad_two = jnp.zeros(resid.shape, jnp.float32)
        for half in range(halves):
            pre = dot(hidden, w_up[half]) + b_up[half : half + 1, :]
            cdf = 0.5 * (1.0 + lax.erf(pre * 0.7071067811865476))
            slope = cdf + pre * (jnp.exp(-0.5 * pre * pre) * 0.3989422804014327)
            active = (pre * cdf).astype(jnp.bfloat16)
            act[half, rows, :] = active
            ffn += dot_last(active, w_down[half])
            grad_pre = (dot(grad_low, w_down[half]) * slope).astype(jnp.bfloat16)
            gpre[half, rows, :] = grad_pre
            grad_two += dot_last(grad_pre, w_up[half])
            add_row(sums_up, half, grad_pre.astype(jnp.float32))
        out[rows, :] = (resid + ffn + vecs[BO2 : BO2 + 1, :]).astype(out.dtype)
        add_row(sums, GAIN2, grad_two * scaled)
        add_row(sums, SHIFT2, grad_two)
        grad_resid = grad_out + norm_back(grad_two, scaled, inverse, vecs[GAIN2 : GAIN2 + 1, :])
        add_row(sums, BO1, grad_resid)
        add_row(sums, BO2, grad_out)
        gres[rows, :] = grad_resid
        low = grad_resid.astype(jnp.bfloat16)
        glow2t[:, rows] = low.T
        for half in range(halves):
            grad_mixed = dot(low, w_mix[half, :, 3 * quarter : 4 * quarter]).astype(jnp.bfloat16)
            gmix[half, rows, :] = grad_mixed
            both = grad_mixed.astype(jnp.float32) * mixed[half, rows, :].astype(jnp.float32)
            dots[half, :, rows] = jnp.sum(both.T.reshape(quarter // 64, 64, TILE), axis=1)
        return 0

    sums[...] = jnp.zeros_like(sums)
    sums_up[...] = jnp.zeros_like(sums_up)
    lax.fori_loop(0, x.shape[0] // TILE, step, 0)


def weight_phase(left_t, right, grads, where):
    halves, _, columns = right.shape
    chunk = min(columns, 512)

    def step(half, _):
        for start in range(0, columns, chunk):
            cols = slice(start, start + chunk)
            grads[where, half, :, cols] = dot(left_t[...], right[half, :, cols]).astype(jnp.bfloat16)
        return 0

    lax.fori_loop(0, halves, step, 0)


def output_weight_phase(glow2t, mixed, grads):
    halves, _, quarter = mixed.shape

    def step(half, _):
        grads[2, half, :, 3 * quarter : 4 * quarter] = dot(glow2t[...], mixed[half]).astype(jnp.bfloat16)
        return 0

    lax.fori_loop(0, halves, step, 0)


def attend_back_phase(query, key, value, gmix, marks_row, marks_col, bias, logs, dots, grad_query, grad_key, grad_value):
    halves, slots, quarter = query.shape
    grad_query[...] = jnp.zeros_like(grad_query)

    def tile_step(tile, _):
        rows = tile_rows(tile)
        same = marks_col[rows, 1:2] == marks_row[0:1, :]
        here = lax.broadcasted_iota(jnp.int32, (TILE, slots), 0) + tile * TILE
        there = lax.broadcasted_iota(jnp.int32, (TILE, slots), 1)
        bias[...] = jnp.where(same | (here == there), 0.0, masked_value)

        def half_step(half, _):
            for pair in range(quarter // 128):
                cols = slice(pair * 128, (pair + 1) * 128)
                queries, grads = query[half, :, cols], gmix[half, :, cols]
                keys, values = key[half, rows, cols], value[half, rows, cols]
                lane = lax.broadcasted_iota(jnp.int32, (TILE, 128), 1)
                wide = lax.broadcasted_iota(jnp.int32, (slots, 128), 1)
                parts = []
                for side in range(2):
                    head = pair * 2 + side
                    mine = (lane < 64) if side == 0 else (lane >= 64)
                    zero = jnp.zeros_like(keys)
                    scores = dot_last(jnp.where(mine, keys, zero), queries) + bias[...]
                    probs = jnp.exp(scores - logs[half, head : head + 1, :])
                    grad_probs = dot_last(jnp.where(mine, values, zero), grads)
                    grad_scores = (probs * (grad_probs - dots[half, head : head + 1, :])).astype(jnp.bfloat16)
                    parts.append(
                        (dot(probs.astype(jnp.bfloat16), grads), dot(grad_scores, queries), dot_first(grad_scores, keys))
                    )
                grad_value[half, rows, cols] = jnp.where(lane < 64, parts[0][0], parts[1][0]).astype(jnp.bfloat16)
                grad_key[half, rows, cols] = jnp.where(lane < 64, parts[0][1], parts[1][1]).astype(jnp.bfloat16)
                grad_query[half, :, cols] += jnp.where(wide < 64, parts[0][2], parts[1][2])
            return 0

        lax.fori_loop(0, halves, half_step, 0)
        return 0

    lax.fori_loop(0, slots // TILE, tile_step, 0)


def input_phase(x, w_mix, vecs, grad_query, grad_low, grad_key, grad_value, gres, sums, grad_x):
    halves, slots, quarter = grad_key.shape
    scale = 1.0 / math.sqrt(64)

    def step(tile, _):
        rows = tile_rows(tile)
        scaled, inverse = statistics(x[rows, :].astype(jnp.float32))
        grad_one = jnp.zeros((TILE, x.shape[1]), jnp.float32)
        for half in range(halves):
            cols = slice(half * quarter, (half + 1) * quarter)
            low = (grad_query[half, rows, :] * scale).astype(jnp.bfloat16)
            grad_low[half, rows, :] = low
            three = (low, grad_key[half, rows, :], grad_value[half, rows, :])
            for c in range(3):
                grad_one += dot_last(three[c], w_mix[half, :, c * quarter : (c + 1) * quarter])
            sums[BQ : BQ + 1, cols] += jnp.sum(three[0].astype(jnp.float32), axis=0, keepdims=True)
            sums[BV : BV + 1, cols] += jnp.sum(three[2].astype(jnp.float32), axis=0, keepdims=True)
        add_row(sums, GAIN1, grad_one * scaled)
        add_row(sums, SHIFT1, grad_one)
        grad_x[rows, :] = (gres[rows, :] + norm_back(grad_one, scaled, inverse, vecs[GAIN1 : GAIN1 + 1, :])).astype(grad_x.dtype)
        return 0

    lax.fori_loop(0, slots // TILE, step, 0)


def qkv_weight_phase(h1t, grad_query, grad_key, grad_value, grads):
    halves, _, quarter = grad_key.shape

    def step(half, _):
        for c, ref in enumerate((grad_query, grad_key, grad_value)):
            grads[2, half, :, c * quarter : (c + 1) * quarter] = dot(h1t[...], ref[half]).astype(jnp.bfloat16)
        return 0

    lax.fori_loop(0, halves, step, 0)


def compute_kernel(x, cot, weights, vecs, b_up, marks_row, out, grad_x, grads, sums, sums_up,
                   h1t, query, key, value, bias, mixed, logs, h2t, glowt, glow2t, act, gpre, gmix, dots, gres,
                   gq_wide, gq, gk, gv, marks_col):
    marks_col[...] = marks_row[...].T
    w_up, w_down, w_mix = weights.at[0], weights.at[1], weights.at[2]
    qkv_phase(x, w_mix, vecs, h1t, query, key, value)
    attend_phase(query, key, value, marks_row, marks_col, bias, mixed, logs)
    middle_phase(x, cot, marks_col, w_up, w_down, w_mix, vecs, b_up, mixed, h2t, glowt, glow2t, act, gpre, gmix, dots, out, gres, sums, sums_up)
    weight_phase(h2t, gpre, grads, 0)
    weight_phase(glowt, act, grads, 1)
    output_weight_phase(glow2t, mixed, grads)
    attend_back_phase(query, key, value, gmix, marks_row, marks_col, bias, logs, dots, gq_wide, gk, gv)
    input_phase(x, w_mix, vecs, gq_wide, gq, gk, gv, gres, sums, grad_x)
    qkv_weight_phase(h1t, gq, gk, gv, grads)


def compute_scratch(slots, width, hidden):
    half = (2, slots, width // 2)
    bf, f32 = jnp.bfloat16, jnp.float32
    V = pltpu.VMEM
    return [
        V((width, slots), bf), V(half, bf), V(half, bf), V(half, bf), V((TILE, slots), f32), V(half, bf),
        V((2, 4, slots), f32), V((width, slots), bf), V((width, slots), bf), V((width, slots), bf),
        V((2, slots, hidden // 2), bf), V((2, slots, hidden // 2), bf), V(half, bf), V((2, 4, slots), f32),
        V((slots, width), f32), V(half, f32), V(half, bf), V(half, bf), V(half, bf), V((slots, 8), f32),
    ]


def compute(x, cot, weights, vecs, b_up, marks_row):
    slots, width = x.shape
    hidden = b_up.shape[0] * b_up.shape[1]
    bf, f32 = jnp.bfloat16, jnp.float32
    return pl.pallas_call(
        compute_kernel,
        out_shape=(
            jax.ShapeDtypeStruct((slots, width), bf),
            jax.ShapeDtypeStruct((slots, width), bf),
            jax.ShapeDtypeStruct(weights.shape, bf),
            jax.ShapeDtypeStruct((8, width), f32),
            jax.ShapeDtypeStruct(b_up.shape, f32),
        ),
        in_specs=[FULL] * 6,
        out_specs=(FULL,) * 5,
        scratch_shapes=compute_scratch(slots, width, hidden),
        compiler_params=pltpu.CompilerParams(vmem_limit_bytes=67043328),
    )(x, cot, weights, vecs, b_up, marks_row)


def marks_of(chain, keep):
    label = chain.astype(jnp.float32)
    live = (chain >= 0).astype(jnp.float32)
    as_key = jnp.where(keep == 1, label, -2.0)
    return jnp.stack([label, as_key, live, live, live, live, live, live])


def product(left, right):
    return jnp.dot(left, right, preferred_element_type=jnp.float32)


def normalize(values, scale_row, shift_row):
    row_mean = jnp.mean(values, axis=-1, keepdims=True)
    centred = values - row_mean
    inverse = lax.rsqrt(jnp.mean(centred * centred, axis=-1, keepdims=True) + epsilon)
    scaled = centred * inverse
    return (scaled * scale_row + shift_row, scaled, inverse)


def normalize_back(grad_rows, scaled, inverse, scale_row):
    inner = grad_rows * scale_row
    return inverse * (
        inner
        - jnp.mean(inner, axis=-1, keepdims=True)
        - scaled * jnp.mean(inner * scaled, axis=-1, keepdims=True)
    )


def gelu_slope(values):
    normal_cdf = 0.5 * (1.0 + lax.erf(values * 0.7071067811865476))
    density = jnp.exp(-0.5 * values * values) * 0.3989422804014327
    return normal_cdf + values * density


def permitted(chain_rows, keep_rows):
    slot_count = chain_rows.shape[0]
    same_chain = chain_rows[:, None] == chain_rows[None, :]
    diagonal = lax.broadcasted_iota(jnp.int32, (slot_count, slot_count), 0) == lax.broadcasted_iota(
        jnp.int32, (slot_count, slot_count), 1
    )
    return same_chain & ((keep_rows[None, :] == 1) | diagonal)


def head_scores(query, key_rows, allowed, head_count, head_width):
    query_heads = query.reshape(-1, head_count, head_width)
    key_heads = key_rows.reshape(-1, head_count, head_width)
    scores = jnp.einsum(
        "qhd,khd->hqk", query_heads, key_heads, preferred_element_type=jnp.float32
    ) * (1.0 / math.sqrt(head_width))
    return jnp.where(allowed[None], scores, masked_value)


def forward(rows_in, chain_rows, keep_rows, weights, join=lambda a: a):
    qkv_full, out_full, up_full, down_full, bias_qv, bias_up, bias_out, gain_full, shift_full = (
        weights
    )
    head_count = bias_qv.shape[1]
    head_width = bias_qv.shape[2]
    row_count = rows_in.shape[0]
    bias_qv = bias_qv.astype(jnp.float32)
    bias_out = bias_out.astype(jnp.float32)
    gain_full = gain_full.astype(jnp.float32)
    shift_full = shift_full.astype(jnp.float32)
    allowed = permitted(chain_rows, keep_rows)
    normed_one, scaled_one, inverse_one = normalize(rows_in, gain_full[0], shift_full[0])
    hidden_one = normed_one.astype(jnp.bfloat16)
    query = (product(hidden_one, qkv_full[0]) + bias_qv[0].reshape(-1)).astype(jnp.bfloat16)
    key_rows = product(hidden_one, qkv_full[1]).astype(jnp.bfloat16)
    value_rows = (product(hidden_one, qkv_full[2]) + bias_qv[1].reshape(-1)).astype(jnp.bfloat16)
    scores = head_scores(query, key_rows, allowed, head_count, head_width)
    row_top = jnp.max(scores, axis=-1, keepdims=True)
    log_total = jnp.log(jnp.sum(jnp.exp(scores - row_top), axis=-1, keepdims=True)) + row_top
    probs_low = jnp.exp(scores - log_total).astype(jnp.bfloat16)
    mixed = jnp.einsum(
        "hqk,khd->qhd",
        probs_low,
        value_rows.reshape(row_count, head_count, head_width),
        preferred_element_type=jnp.float32,
    )
    mixed = mixed.reshape(row_count, -1).astype(jnp.bfloat16)
    partial_attn = product(mixed, out_full)
    resid = rows_in + join(partial_attn) + bias_out[0]
    normed_two, scaled_two, inverse_two = normalize(resid, gain_full[1], shift_full[1])
    hidden_two = normed_two.astype(jnp.bfloat16)
    pre = product(hidden_two, up_full) + bias_up.astype(jnp.float32).reshape(-1)
    act = jax.nn.gelu(pre, approximate=False).astype(jnp.bfloat16)
    partial_ffn = product(act, down_full)
    result = (
        resid + join(partial_ffn.astype(jnp.bfloat16)).astype(jnp.float32) + bias_out[1]
    )
    kept = (
        allowed,
        scaled_one,
        inverse_one,
        hidden_one,
        query,
        key_rows,
        value_rows,
        log_total,
        mixed,
        scaled_two,
        inverse_two,
        hidden_two,
        pre,
        act,
    )
    return (result, kept)


def backward(grad_out, result, kept, weights, join=lambda a: a):
    qkv_full, out_full, up_full, down_full, bias_qv, bias_up, bias_out, gain_full, shift_full = (
        weights
    )
    (
        allowed,
        scaled_one,
        inverse_one,
        hidden_one,
        query,
        key_rows,
        value_rows,
        log_total,
        mixed,
        scaled_two,
        inverse_two,
        hidden_two,
        pre,
        act,
    ) = kept
    head_count = bias_qv.shape[1]
    head_width = bias_qv.shape[2]
    row_count = grad_out.shape[0]
    gain_full = gain_full.astype(jnp.float32)
    grad_low = grad_out.astype(jnp.bfloat16)
    grad_down = product(act.T, grad_low)
    grad_pre = (product(grad_low, down_full.T) * gelu_slope(pre)).astype(jnp.bfloat16)
    grad_bup = jnp.sum(grad_pre, axis=0, dtype=jnp.float32).reshape(bias_up.shape)
    grad_up = product(hidden_two.T, grad_pre)
    partial_two = product(grad_pre, up_full.T)
    grad_two = join(partial_two.astype(jnp.bfloat16)).astype(jnp.float32)
    gain_two = jnp.sum(grad_two * scaled_two, axis=0)
    shift_two = jnp.sum(grad_two, axis=0)
    grad_resid = grad_out + normalize_back(grad_two, scaled_two, inverse_two, gain_full[1])
    resid_low = grad_resid.astype(jnp.bfloat16)
    grad_out_proj = product(mixed.T, resid_low)
    grad_mixed = (
        product(resid_low, out_full.T)
        .astype(jnp.bfloat16)
        .reshape(row_count, head_count, head_width)
    )
    scores = head_scores(query, key_rows, allowed, head_count, head_width)
    probs = jnp.exp(scores - log_total)
    probs_low = probs.astype(jnp.bfloat16)
    value_heads = value_rows.reshape(row_count, head_count, head_width)
    grad_value = jnp.einsum(
        "hqk,qhd->khd", probs_low, grad_mixed, preferred_element_type=jnp.float32
    ).astype(jnp.bfloat16)
    grad_probs = jnp.einsum(
        "qhd,khd->hqk", grad_mixed, value_heads, preferred_element_type=jnp.float32
    )
    grad_scores = (
        probs * (grad_probs - jnp.sum(grad_probs * probs, axis=-1, keepdims=True))
    ).astype(jnp.bfloat16)
    score_scale = 1.0 / math.sqrt(head_width)
    key_heads = key_rows.reshape(row_count, head_count, head_width)
    query_heads = query.reshape(row_count, head_count, head_width)
    grad_query = (
        jnp.einsum("hqk,khd->qhd", grad_scores, key_heads, preferred_element_type=jnp.float32)
        * score_scale
    ).astype(jnp.bfloat16)
    grad_key = (
        jnp.einsum("hqk,qhd->khd", grad_scores, query_heads, preferred_element_type=jnp.float32)
        * score_scale
    ).astype(jnp.bfloat16)
    stacked = jnp.stack(
        [
            grad_query.reshape(row_count, -1),
            grad_key.reshape(row_count, -1),
            grad_value.reshape(row_count, -1),
        ]
    )
    grad_qkv = jnp.einsum("rd,crk->cdk", hidden_one, stacked, preferred_element_type=jnp.float32)
    partial_one = jnp.einsum("crk,cdk->rd", stacked, qkv_full, preferred_element_type=jnp.float32)
    grad_one = join(partial_one.astype(jnp.bfloat16)).astype(jnp.float32)
    grad_bqv = jnp.stack(
        [
            jnp.sum(stacked[0], axis=0, dtype=jnp.float32),
            jnp.sum(stacked[2], axis=0, dtype=jnp.float32),
        ]
    ).reshape(2, head_count, head_width)
    gain_one = jnp.sum(grad_one * scaled_one, axis=0)
    shift_one = jnp.sum(grad_one, axis=0)
    grad_in = grad_resid + normalize_back(grad_one, scaled_one, inverse_one, gain_full[0])
    small_sums = jnp.stack(
        [
            jnp.sum(grad_resid, axis=0),
            jnp.sum(grad_out, axis=0),
            gain_one,
            gain_two,
            shift_one,
            shift_two,
        ]
    )
    local_grads = (
        grad_qkv,
        grad_out_proj,
        grad_up,
        grad_down,
        grad_bqv,
        grad_bup,
        small_sums[0:2],
        small_sums[2:4],
        small_sums[4:6],
    )
    return (result, grad_in, local_grads)


def body_generic(
    activations,
    cotangent,
    w_qkv,
    w_o,
    w_up,
    w_down,
    b_qv,
    b_up,
    out_bias,
    norm_gain,
    norm_bias,
    chain_ids,
    key_keep,
):
    batch_count = activations.shape[0]
    outputs = []
    input_grads = []
    running = None
    for batch_index in range(batch_count):
        weights = (
            lax.all_gather(w_qkv, "dp", axis=1, tiled=True),
            lax.all_gather(w_o, "dp", axis=1, tiled=True),
            lax.all_gather(w_up, "dp", axis=0, tiled=True),
            lax.all_gather(w_down, "dp", axis=1, tiled=True),
            lax.all_gather(b_qv, "dp", axis=2, tiled=True),
            lax.all_gather(b_up, "dp", axis=1, tiled=True),
            lax.all_gather(out_bias, "dp", axis=1, tiled=True),
            lax.all_gather(norm_gain, "dp", axis=1, tiled=True),
            lax.all_gather(norm_bias, "dp", axis=1, tiled=True),
        )
        result, kept = forward(
            activations[batch_index].astype(jnp.float32),
            chain_ids[batch_index],
            key_keep[batch_index],
            weights,
            lambda a: lax.psum(a, "mp"),
        )
        live_rows = (chain_ids[batch_index] >= 0).astype(jnp.float32)[:, None]
        output_rows, grad_in, local_grads = backward(
            cotangent[batch_index].astype(jnp.float32) * live_rows, result, kept, weights, lambda a: lax.psum(a, "mp")
        )
        outputs.append(output_rows)
        input_grads.append(grad_in)
        shares = (
            lax.psum_scatter(
                local_grads[0].astype(jnp.bfloat16), "dp", scatter_dimension=1, tiled=True
            ).astype(jnp.float32),
            lax.psum_scatter(
                local_grads[1].astype(jnp.bfloat16), "dp", scatter_dimension=1, tiled=True
            ).astype(jnp.float32),
            lax.psum_scatter(
                local_grads[2].astype(jnp.bfloat16), "dp", scatter_dimension=0, tiled=True
            ).astype(jnp.float32),
            lax.psum_scatter(
                local_grads[3].astype(jnp.bfloat16), "dp", scatter_dimension=1, tiled=True
            ).astype(jnp.float32),
            lax.psum_scatter(
                local_grads[4].astype(jnp.bfloat16), "dp", scatter_dimension=2, tiled=True
            ).astype(jnp.float32),
            lax.psum_scatter(
                local_grads[5].astype(jnp.bfloat16), "dp", scatter_dimension=1, tiled=True
            ).astype(jnp.float32),
            lax.psum_scatter(
                local_grads[6].astype(jnp.bfloat16), "dp", scatter_dimension=1, tiled=True
            ).astype(jnp.float32),
            lax.psum_scatter(
                local_grads[7].astype(jnp.bfloat16), "dp", scatter_dimension=1, tiled=True
            ).astype(jnp.float32),
            lax.psum_scatter(
                local_grads[8].astype(jnp.bfloat16), "dp", scatter_dimension=1, tiled=True
            ).astype(jnp.float32),
        )
        if running is None:
            running = tuple(shares)
        else:
            running = tuple(jax.tree.map(jnp.add, tuple(running), tuple(shares)))
    return (
        jnp.stack(outputs),
        jnp.stack(input_grads),
        running[0],
        running[1],
        running[2],
        running[3],
        running[4],
        running[5],
        running[6],
        running[7],
        running[8],
    )


def fits(mesh):
    return mesh.shape["mp"] == 2


def cat_weights(w_qkv, w_o, w_up, w_down):
    mixed_part = jnp.concatenate([w_qkv[0], w_qkv[1], w_qkv[2], w_o.T], axis=1)
    return jnp.stack([w_up, w_down.T, mixed_part])


def cat_small(b_qv, b_up, out_bias, norm_gain, norm_bias):
    parts = [b_qv, b_up, norm_gain, norm_bias, out_bias]
    return jnp.concatenate([part.reshape(-1) for part in parts])


def spread_small(smalls, b_qv, b_up):
    mp, dp = smalls.shape[:2]
    n0, n1 = b_qv.size, b_qv.size + b_up.size
    qv = smalls[:, :, :n0].reshape(mp, dp, 2, b_qv.shape[1], b_qv.shape[2])
    qv = qv.transpose(2, 0, 3, 1, 4).reshape(2, -1)
    up = smalls[:, :, n0:n1].reshape(mp, dp, b_up.shape[0], b_up.shape[1]).transpose(0, 2, 1, 3).reshape(mp, -1)
    rest = smalls[0, :, n1:].reshape(dp, 3, 2, -1).transpose(1, 2, 0, 3).reshape(6, -1)
    gain, shift, bias = rest[0:2], rest[2:4], rest[4:6]
    vecs = jnp.stack([gain[0], shift[0], gain[1], shift[1], qv[0], qv[1], bias[0], bias[1]])
    return vecs, up


def body_split(
    activations,
    cotangent,
    w_qkv,
    w_o,
    w_up,
    w_down,
    b_qv,
    b_up,
    out_bias,
    norm_gain,
    norm_bias,
    chain_ids,
    key_keep,
):
    own = lax.axis_index("mp")
    mp = lax.axis_size("mp")
    dp = lax.axis_size("dp")
    packed = cat_weights(w_qkv, w_o, w_up, w_down)
    small = cat_small(b_qv, b_up, out_bias, norm_gain, norm_bias)
    depth = packed.shape[1]
    full = lax.all_gather(packed, ("mp", "dp"), axis=0, tiled=False)
    full = full.reshape(mp, dp, 3, depth, -1).transpose(2, 0, 1, 3, 4).reshape(3, mp, dp * depth, -1)
    smalls = lax.all_gather(small, ("mp", "dp"), axis=0, tiled=False).reshape(mp, dp, -1)
    vecs, up_bias = spread_small(smalls.astype(jnp.float32), b_qv, b_up)
    take = lambda a: lax.dynamic_index_in_dim(a, own, 0, keepdims=False)
    marks = marks_of(take(chain_ids), take(key_keep))
    out, grad_x, grads, sums, sums_up = compute(
        take(activations), take(cotangent), full, vecs, up_bias, marks
    )
    gathered = lax.all_gather(jnp.stack([out, grad_x]), "mp", axis=0, tiled=False).astype(jnp.float32)
    g_all = grads.reshape(3, mp, dp, depth, -1).transpose(1, 2, 0, 3, 4).reshape(mp * dp, 3, depth, -1)
    g_own = lax.psum_scatter(g_all, ("mp", "dp"), scatter_dimension=0, tiled=False).astype(jnp.float32)
    total = lax.psum(jnp.concatenate([sums.reshape(-1), sums_up.reshape(-1)]), ("mp", "dp"))
    s_vec, s_up = total[: sums.size].reshape(sums.shape), total[sums.size :].reshape(sums_up.shape)
    at = lax.axis_index("dp")
    pick = lambda a, axis: lax.dynamic_index_in_dim(a, at, axis, keepdims=False)
    pairs = lambda r0, r1: pick(jnp.stack([s_vec[r0], s_vec[r1]]).reshape(2, dp, -1), 1)
    s_qv = pick(take(s_vec[BQ : BV + 1].reshape(2, mp, -1).transpose(1, 0, 2)).reshape(2, b_qv.shape[1], dp, -1), 2)
    s_bup = pick(take(s_up).reshape(b_up.shape[0], dp, -1), 1)
    mix, quarter = g_own[2], packed.shape[2] // 4
    return (
        gathered[:, 0],
        gathered[:, 1],
        jnp.stack([mix[:, c * quarter : (c + 1) * quarter] for c in range(3)]),
        mix[:, 3 * quarter :].T,
        g_own[0],
        g_own[1].T,
        s_qv,
        s_bup,
        pairs(BO1, BO2),
        pairs(GAIN1, GAIN2),
        pairs(SHIFT1, SHIFT2),
    )


def solution(mesh):
    placed = (
        P(None, "dp", None),
        P(None, "dp", None),
        P(None, "dp", "mp"),
        P("mp", "dp"),
        P("dp", "mp"),
        P("mp", "dp"),
        P(None, "mp", "dp"),
        P("mp", "dp"),
        P(None, "dp"),
        P(None, "dp"),
        P(None, "dp"),
        P(None, "dp"),
        P(None, "dp"),
    )
    body = body_split if fits(mesh) else body_generic
    return jax.shard_map(
        body,
        mesh=mesh,
        in_specs=placed,
        out_specs=(
            P(None, "dp", None),
            P(None, "dp", None),
            P(None, "dp", "mp"),
            P("mp", "dp"),
            P("dp", "mp"),
            P("mp", "dp"),
            P(None, "mp", "dp"),
            P("mp", "dp"),
            P(None, "dp"),
            P(None, "dp"),
            P(None, "dp"),
        ),
        check_vma=False,
    )
```

```python
import functools
import math

import jax
import jax.numpy as jnp
from jax import lax
from jax.experimental import pallas as pl
from jax.experimental.pallas import tpu as pltpu
from jax.sharding import PartitionSpec as P

epsilon = 1e-05
masked_value = -1e30
TILE = 256
FULL = pl.BlockSpec(memory_space=pltpu.VMEM)

GAIN1, SHIFT1, GAIN2, SHIFT2, BQ, BV, BO1, BO2 = range(8)


def dot(left, right):
    return jnp.dot(left, right, preferred_element_type=jnp.float32)


def dot_last(left, right):
    return lax.dot_general(left, right, (((1,), (1,)), ((), ())), preferred_element_type=jnp.float32)


def dot_first(left, right):
    return lax.dot_general(left, right, (((0,), (0,)), ((), ())), preferred_element_type=jnp.float32)


def tile_rows(index):
    return pl.ds(pl.multiple_of(index * TILE, TILE), TILE)


def statistics(values):
    centred = values - jnp.mean(values, axis=-1, keepdims=True)
    inverse = lax.rsqrt(jnp.mean(centred * centred, axis=-1, keepdims=True) + epsilon)
    return centred * inverse, inverse


def norm_back(grad, scaled, inverse, gain):
    inner = grad * gain
    return inverse * (
        inner - jnp.mean(inner, axis=-1, keepdims=True) - scaled * jnp.mean(inner * scaled, axis=-1, keepdims=True)
    )


def add_row(ref, row, values):
    ref[row : row + 1, :] += jnp.sum(values, axis=0, keepdims=True)


def qkv_phase(x, w_mix, vecs, h1t, query, key, value):
    halves, quarter = query.shape[0], query.shape[2]
    scale = 1.0 / math.sqrt(64)

    def step(tile, _):
        rows = tile_rows(tile)
        scaled, _ = statistics(x[rows, :].astype(jnp.float32))
        hidden = (scaled * vecs[GAIN1 : GAIN1 + 1, :] + vecs[SHIFT1 : SHIFT1 + 1, :]).astype(jnp.bfloat16)
        h1t[:, rows] = hidden.T
        for half in range(halves):
            cols = slice(half * quarter, (half + 1) * quarter)
            part = lambda c: dot(hidden, w_mix[half, :, c * quarter : (c + 1) * quarter])
            query[half, rows, :] = ((part(0) + vecs[BQ : BQ + 1, cols]).astype(jnp.bfloat16) * scale).astype(jnp.bfloat16)
            key[half, rows, :] = part(1).astype(jnp.bfloat16)
            value[half, rows, :] = (part(2) + vecs[BV : BV + 1, cols]).astype(jnp.bfloat16)
        return 0

    lax.fori_loop(0, x.shape[0] // TILE, step, 0)


def attend_phase(query, key, value, marks_row, marks_col, bias, mixed, logs, beside):
    halves, slots, quarter = query.shape

    def tile_step(tile, _):
        rows = tile_rows(tile)
        for when, action in beside:
            pl.when(tile == when)(action)
        same = marks_col[rows, 0:1] == marks_row[1:2, :]
        here = lax.broadcasted_iota(jnp.int32, (TILE, slots), 0) + tile * TILE
        there = lax.broadcasted_iota(jnp.int32, (TILE, slots), 1)
        bias[...] = jnp.where(same | (here == there), 0.0, masked_value)

        def half_step(half, _):
            lane = lax.broadcasted_iota(jnp.int32, (TILE, 128), 1)
            stats = jnp.zeros((TILE, 128), jnp.float32)
            for pair in range(quarter // 128):
                cols = slice(pair * 128, (pair + 1) * 128)
                both = query[half, rows, cols]
                keys = key[half, :, cols]
                values = value[half, :, cols]
                sums = []
                for side in range(2):
                    mine = (lane < 64) if side == 0 else (lane >= 64)
                    scores = dot_last(jnp.where(mine, both, jnp.zeros_like(both)), keys) + bias[...]
                    top = jnp.max(scores, axis=1, keepdims=True)
                    expo = jnp.exp(scores - top)
                    total = jnp.sum(expo, axis=1, keepdims=True)
                    sums.append(dot(expo.astype(jnp.bfloat16), values) * (1.0 / total))
                    stats = jnp.where(lane == pair * 2 + side, top + jnp.log(total), stats)
                mixed[half, rows, cols] = jnp.where(lane < 64, sums[0], sums[1]).astype(jnp.bfloat16)
            logs[half, :, rows] = stats.T[0:4, :]
            return 0

        lax.fori_loop(0, halves, half_step, 0)
        return 0

    lax.fori_loop(0, slots // TILE, tile_step, 0)


def middle_phase(x, cot, live_col, w_up, w_down, w_mix, vecs, b_up, mixed, h2t, glowt, glow2t, act, gpre, gmix, dots, out, gres, sums, sums_up, send):
    halves, quarter, hidden_half = mixed.shape[0], mixed.shape[2], w_up.shape[2]

    def step(tile, _):
        rows = tile_rows(tile)
        attn = sum(dot_last(mixed[half, rows, :], w_mix[half, :, 3 * quarter : 4 * quarter]) for half in range(halves))
        resid = x[rows, :].astype(jnp.float32) + attn + vecs[BO1 : BO1 + 1, :]
        scaled, inverse = statistics(resid)
        hidden = (scaled * vecs[GAIN2 : GAIN2 + 1, :] + vecs[SHIFT2 : SHIFT2 + 1, :]).astype(jnp.bfloat16)
        h2t[:, rows] = hidden.T
        grad_out = cot[rows, :].astype(jnp.float32) * live_col[rows, 2:3]
        grad_low = grad_out.astype(jnp.bfloat16)
        glowt[:, rows] = grad_low.T
        ffn = jnp.zeros(resid.shape, jnp.float32)
        grad_two = jnp.zeros(resid.shape, jnp.float32)
        for half in range(halves):
            pre = dot(hidden, w_up[half]) + b_up[half : half + 1, :]
            cdf = 0.5 * (1.0 + lax.erf(pre * 0.7071067811865476))
            slope = cdf + pre * (jnp.exp(-0.5 * pre * pre) * 0.3989422804014327)
            active = (pre * cdf).astype(jnp.bfloat16)
            act[half, rows, :] = active
            ffn += dot_last(active, w_down[half])
            grad_pre = (dot(grad_low, w_down[half]) * slope).astype(jnp.bfloat16)
            gpre[half, rows, :] = grad_pre
            grad_two += dot_last(grad_pre, w_up[half])
            add_row(sums_up, half, grad_pre.astype(jnp.float32))
        out[rows, :] = (resid + ffn + vecs[BO2 : BO2 + 1, :]).astype(out.dtype)
        add_row(sums, GAIN2, grad_two * scaled)
        add_row(sums, SHIFT2, grad_two)
        grad_resid = grad_out + norm_back(grad_two, scaled, inverse, vecs[GAIN2 : GAIN2 + 1, :])
        add_row(sums, BO1, grad_resid)
        add_row(sums, BO2, grad_out)
        gres[rows, :] = grad_resid
        low = grad_resid.astype(jnp.bfloat16)
        glow2t[:, rows] = low.T
        for half in range(halves):
            grad_mixed = dot(low, w_mix[half, :, 3 * quarter : 4 * quarter]).astype(jnp.bfloat16)
            gmix[half, rows, :] = grad_mixed
            both = grad_mixed.astype(jnp.float32) * mixed[half, rows, :].astype(jnp.float32)
            dots[half, :, rows] = jnp.sum(both.T.reshape(quarter // 64, 64, TILE), axis=1)
        send(tile)
        return 0

    sums[...] = jnp.zeros_like(sums)
    sums_up[...] = jnp.zeros_like(sums_up)
    lax.fori_loop(0, x.shape[0] // TILE, step, 0)


def weight_phase(left_t, right, grads, where):
    halves, _, columns = right.shape
    chunk = min(columns, 512)

    def step(half, _):
        for start in range(0, columns, chunk):
            cols = slice(start, start + chunk)
            grads[where, half, :, cols] = dot(left_t[...], right[half, :, cols]).astype(jnp.bfloat16)
        return 0

    lax.fori_loop(0, halves, step, 0)


def output_weight_phase(glow2t, mixed, grads):
    halves, _, quarter = mixed.shape

    def step(half, _):
        grads[2, half, :, 3 * quarter : 4 * quarter] = dot(glow2t[...], mixed[half]).astype(jnp.bfloat16)
        return 0

    lax.fori_loop(0, halves, step, 0)


def attend_back_phase(query, key, value, gmix, marks_row, marks_col, bias, logs, dots, grad_query, grad_key, grad_value, beside):
    halves, slots, quarter = query.shape
    grad_query[...] = jnp.zeros_like(grad_query)

    def tile_step(tile, _):
        rows = tile_rows(tile)
        for when, action in beside:
            pl.when(tile == when)(action)
        same = marks_col[rows, 1:2] == marks_row[0:1, :]
        here = lax.broadcasted_iota(jnp.int32, (TILE, slots), 0) + tile * TILE
        there = lax.broadcasted_iota(jnp.int32, (TILE, slots), 1)
        bias[...] = jnp.where(same | (here == there), 0.0, masked_value)

        def half_step(half, _):
            for pair in range(quarter // 128):
                cols = slice(pair * 128, (pair + 1) * 128)
                queries, grads = query[half, :, cols], gmix[half, :, cols]
                keys, values = key[half, rows, cols], value[half, rows, cols]
                lane = lax.broadcasted_iota(jnp.int32, (TILE, 128), 1)
                wide = lax.broadcasted_iota(jnp.int32, (slots, 128), 1)
                parts = []
                for side in range(2):
                    head = pair * 2 + side
                    mine = (lane < 64) if side == 0 else (lane >= 64)
                    zero = jnp.zeros_like(keys)
                    scores = dot_last(jnp.where(mine, keys, zero), queries) + bias[...]
                    probs = jnp.exp(scores - logs[half, head : head + 1, :])
                    grad_probs = dot_last(jnp.where(mine, values, zero), grads)
                    grad_scores = (probs * (grad_probs - dots[half, head : head + 1, :])).astype(jnp.bfloat16)
                    parts.append(
                        (dot(probs.astype(jnp.bfloat16), grads), dot(grad_scores, queries), dot_first(grad_scores, keys))
                    )
                grad_value[half, rows, cols] = jnp.where(lane < 64, parts[0][0], parts[1][0]).astype(jnp.bfloat16)
                grad_key[half, rows, cols] = jnp.where(lane < 64, parts[0][1], parts[1][1]).astype(jnp.bfloat16)
                grad_query[half, :, cols] += jnp.where(wide < 64, parts[0][2], parts[1][2])
            return 0

        lax.fori_loop(0, halves, half_step, 0)
        return 0

    lax.fori_loop(0, slots // TILE, tile_step, 0)


def round_phase(wide, low):
    scale = 1.0 / math.sqrt(64)

    def step(half, _):
        low[half] = (wide[half] * scale).astype(jnp.bfloat16)
        return 0

    lax.fori_loop(0, low.shape[0], step, 0)


def qkv_weight_phase(h1t, grad_query, grad_key, grad_value, grads):
    halves, _, quarter = grad_key.shape

    def step(half, _):
        for c, ref in enumerate((grad_query, grad_key, grad_value)):
            grads[2, half, :, c * quarter : (c + 1) * quarter] = dot(h1t[...], ref[half]).astype(jnp.bfloat16)
        return 0

    lax.fori_loop(0, halves, step, 0)


def input_phase(x, w_mix, vecs, grad_query, grad_key, grad_value, gres, sums, grad_x, send):
    halves, slots, quarter = grad_key.shape

    def step(tile, _):
        rows = tile_rows(tile)
        scaled, inverse = statistics(x[rows, :].astype(jnp.float32))
        grad_one = jnp.zeros((TILE, x.shape[1]), jnp.float32)
        for half in range(halves):
            cols = slice(half * quarter, (half + 1) * quarter)
            three = (grad_query[half, rows, :], grad_key[half, rows, :], grad_value[half, rows, :])
            for c in range(3):
                grad_one += dot_last(three[c], w_mix[half, :, c * quarter : (c + 1) * quarter])
            sums[BQ : BQ + 1, cols] += jnp.sum(three[0].astype(jnp.float32), axis=0, keepdims=True)
            sums[BV : BV + 1, cols] += jnp.sum(three[2].astype(jnp.float32), axis=0, keepdims=True)
        add_row(sums, GAIN1, grad_one * scaled)
        add_row(sums, SHIFT1, grad_one)
        grad_x[rows, :] = (gres[rows, :] + norm_back(grad_one, scaled, inverse, vecs[GAIN1 : GAIN1 + 1, :])).astype(grad_x.dtype)
        send(tile)
        return 0

    lax.fori_loop(0, slots // TILE, step, 0)


class Place:
    def __init__(self, depth_z):
        at = lax.axis_index("dp")
        self.x, self.z, self.y, self.c = lax.axis_index("mp"), at // 4, (at // 2) % 2, at % 2
        self.count = depth_z

    def other(self, axis):
        x, z, y, c = self.x, self.z, self.y, self.c
        x, y, c = (1 - x if axis == "x" else x), (1 - y if axis == "y" else y), (1 - c if axis == "c" else c)
        return {"dp": z * 4 + y * 2 + c, "mp": x}

    def along(self, hop):
        z = lax.rem(self.z + hop, self.count)
        return {"dp": z * 4 + self.y * 2 + self.c, "mp": self.x}, z


class Wire:
    def __init__(self, send, recv):
        self.send_sems, self.recv_sems = send, recv

    def copy(self, src, dst, number, device):
        return pltpu.make_async_remote_copy(
            src_ref=src,
            dst_ref=dst,
            send_sem=self.send_sems.at[number],
            recv_sem=self.recv_sems.at[number],
            device_id=device,
            device_id_type=pl.DeviceIdType.MESH,
        )


GATHER_SEMS = 15
REDUCE_SEMS = 9
SMALL_SEMS = 7


class Gather:
    def __init__(self, ref, base, wire, place):
        self.ref, self.base, self.wire, self.place = ref, base, wire, place
        self.top = pl.ds(0, ref.shape[4] // 2)
        self.low = pl.ds(ref.shape[4] // 2, ref.shape[4] // 2)

    def own(self, axis, src, number):
        return self.wire.copy(src, src, self.base + number, self.place.other(axis))

    def z_copies(self):
        p, ref = self.place, self.ref
        mine = ref.at[p.x, p.z, p.y, p.c]
        for hop in range(1, p.count):
            device, _ = p.along(hop)
            yield self.wire.copy(mine, mine, self.base + hop - 1, device)

    def second(self):
        p, ref = self.place, self.ref
        return (
            self.own("y", ref.at[p.x, :, p.y, p.c, self.top], 3),
            self.own("x", ref.at[p.x, :, p.y, p.c, self.low], 4),
        )

    def third(self):
        p, ref = self.place, self.ref
        return (
            self.own("x", ref.at[p.x, :, :, p.c, self.top], 5),
            self.own("y", ref.at[:, :, p.y, p.c, self.low], 6),
        )

    def core(self, step):
        p, ref = self.place, self.ref
        if step == 1:
            return (self.own("c", ref.at[p.x, :, p.y, p.c], 7),)
        if step == 2:
            return (
                self.own("c", ref.at[p.x, :, 1 - p.y, p.c, self.top], 8),
                self.own("c", ref.at[1 - p.x, :, p.y, p.c, self.low], 9),
            )
        return (
            self.own("c", ref.at[1 - p.x, :, :, p.c, self.top], 10),
            self.own("c", ref.at[:, :, 1 - p.y, p.c, self.low], 11),
        )

    def start(self):
        for copy in self.z_copies():
            copy.start()

    def after_start(self):
        for copy in self.z_copies():
            copy.wait_recv()
        for copy in self.second() + self.core(1):
            copy.start()

    def after_second(self):
        for copy in self.second():
            copy.wait_recv()
        for copy in self.third() + self.core(2):
            copy.start()

    def after_third(self):
        for copy in self.third():
            copy.wait_recv()
        for copy in self.core(3):
            copy.start()

    def finish(self):
        for step in (1, 2, 3):
            for copy in self.core(step):
                copy.wait_recv()

    def drain(self):
        for copy in self.z_copies():
            copy.wait_send()
        for copy in self.second() + self.third() + self.core(1) + self.core(2) + self.core(3):
            copy.wait_send()


class SmallGather:
    def __init__(self, ref, base, wire, place):
        self.ref, self.base, self.wire, self.place = ref, base, wire, place

    def z_copies(self):
        p = self.place
        mine = self.ref.at[p.x, p.z, p.y, p.c]
        return [self.wire.copy(mine, mine, self.base + hop - 1, p.along(hop)[0]) for hop in range(1, p.count)]

    def step(self, axis):
        p, ref = self.place, self.ref
        src = {"y": ref.at[p.x, :, p.y, p.c], "x": ref.at[p.x, :, :, p.c], "c": ref.at[:, :, :, p.c]}[axis]
        return self.wire.copy(src, src, self.base + {"y": 3, "x": 4, "c": 5}[axis], p.other(axis))


class Reduce:
    def __init__(self, grads, from_core, from_a, from_b, from_c, from_d, from_z, base, wire, place):
        self.grads, self.base, self.wire, self.place = grads, base, wire, place
        self.from_core, self.from_a, self.from_b = from_core, from_a, from_b
        self.from_c, self.from_d, self.from_z = from_c, from_d, from_z
        rows = grads.shape[4]
        self.top, self.low = pl.ds(0, rows // 2), pl.ds(rows // 2, rows // 2)

    def copies(self, step):
        p, g, w, base = self.place, self.grads, self.wire, self.base
        if step == 0:
            return [w.copy(g.at[:, :, :, 1 - p.c], self.from_core, base, p.other("c"))]
        if step == 1:
            return [
                w.copy(g.at[1 - p.x, :, :, p.c, self.top], self.from_a, base + 1, p.other("x")),
                w.copy(g.at[:, :, 1 - p.y, p.c, self.low], self.from_b, base + 2, p.other("y")),
            ]
        if step == 2:
            return [
                w.copy(g.at[p.x, :, 1 - p.y, p.c, self.top], self.from_c, base + 3, p.other("y")),
                w.copy(g.at[1 - p.x, :, p.y, p.c, self.low], self.from_d, base + 4, p.other("x")),
            ]
        out = []
        for hop in range(1, p.count):
            device, z = p.along(hop)
            out.append(w.copy(g.at[p.x, z, p.y, p.c], self.from_z.at[hop - 1], base + 4 + hop, device))
        return out

    def send(self, step):
        for copy in self.copies(step):
            copy.start()

    def take(self, step):
        p, g = self.place, self.grads
        for copy in self.copies(step):
            copy.wait_recv()
        if step == 0:

            def add(index, _):
                x, z = index // p.count, lax.rem(index, p.count)
                for y in range(2):
                    g[x, z, y, p.c] += self.from_core[x, z, y]
                return 0

            lax.fori_loop(0, 2 * p.count, add, 0)
        elif step == 1:

            def add(z, _):
                for k in range(2):
                    g[p.x, z, k, p.c, self.top] += self.from_a[z, k]
                    g[k, z, p.y, p.c, self.low] += self.from_b[k, z]
                return 0

            lax.fori_loop(0, p.count, add, 0)
        elif step == 2:

            def add(z, _):
                g[p.x, z, p.y, p.c, self.top] += self.from_c[z]
                g[p.x, z, p.y, p.c, self.low] += self.from_d[z]
                return 0

            lax.fori_loop(0, p.count, add, 0)

    def result(self):
        p = self.place
        total = self.grads[p.x, p.z, p.y, p.c].astype(jnp.float32)
        for hop in range(1, p.count):
            total += self.from_z[hop - 1].astype(jnp.float32)
        return total

    def drain(self):
        for step in range(4):
            for copy in self.copies(step):
                copy.wait_send()


def whole_kernel(
    acts, cots, chain_ids, key_keep, w_up, w_down_t, w_mix, small,
    outs, grads_x, g_up, g_down, g_mix, small_sum,
    weights, smalls, x, cot, vecs, b_up, marks, marks_col, sums, sums_up,
    h1t, query, key, value, bias, mixed, logs, h2t, glowt, glow2t, act, gpre, gmix, dots, gres,
    gq_wide, gq, gk, gv, grads, from_core, from_a, from_b, from_c, from_d, from_z, small_from, small_tot,
    local, send, recv,
):
    count = weights.shape[2]
    place = Place(count)
    wire = Wire(send, recv)
    me = (place.x, place.z, place.y, place.c)
    loads = [pltpu.make_async_copy(acts.at[place.x], x, local.at[0]), pltpu.make_async_copy(cots.at[place.x], cot, local.at[1])]
    for part, ref in enumerate((w_up, w_down_t, w_mix)):
        loads.append(pltpu.make_async_copy(ref, weights.at[(part, *me)], local.at[2 + part]))
    loads.append(pltpu.make_async_copy(small, smalls.at[me], local.at[5]))
    for load in loads:
        load.start()

    barrier = pltpu.get_barrier_semaphore()
    partners = [place.other(axis) for axis in "xyc"] + [place.along(hop)[0] for hop in range(1, count)]
    for device in partners:
        pl.semaphore_signal(barrier, inc=1, device_id=device, device_id_type=pl.DeviceIdType.MESH)
    pl.semaphore_wait(barrier, len(partners))

    gathers = [Gather(weights.at[part], part * GATHER_SEMS, wire, place) for part in range(3)]
    tiny = SmallGather(smalls, 3 * GATHER_SEMS, wire, place)
    base = 3 * GATHER_SEMS + SMALL_SEMS
    reduces = [
        Reduce(
            grads.at[part], from_core.at[part], from_a.at[part], from_b.at[part], from_c.at[part], from_d.at[part],
            from_z.at[part], base + part * REDUCE_SEMS, wire, place,
        )
        for part in range(3)
    ]
    base += 3 * REDUCE_SEMS
    forward_rows = lambda ref, first, tile: wire.copy(
        ref.at[place.x, tile_rows(tile)], ref.at[place.x, tile_rows(tile)], first + tile, place.other("x")
    )
    out_base, gx_base, small_base = base, base + 8, base + 16
    tiles = x.shape[0] // TILE

    loads[5].wait()
    for copy in tiny.z_copies():
        copy.start()
    loads[4].wait()
    gathers[2].start()
    loads[0].wait()
    loads[1].wait()
    loads[2].wait()
    loads[3].wait()
    for copy in tiny.z_copies():
        copy.wait_recv()
    tiny.step("y").start()
    gathers[2].after_start()
    gathers[0].start()
    gathers[1].start()
    tiny.step("y").wait_recv()
    tiny.step("x").start()
    gathers[2].after_second()
    tiny.step("x").wait_recv()
    tiny.step("c").start()
    gathers[2].after_third()
    gathers[0].after_start()
    gathers[1].after_start()

    x_label = chain_ids[pl.ds(place.x, 1), :]
    label = x_label.astype(jnp.float32)
    marks[0:1, :] = label
    marks[1:2, :] = jnp.where(key_keep[pl.ds(place.x, 1), :] == 1, label, -2.0)
    marks[2:8, :] = jnp.broadcast_to((x_label >= 0).astype(jnp.float32), (6, label.shape[1]))
    marks_col[...] = marks[...].T

    tiny.step("c").wait_recv()
    total = jnp.zeros(smalls.shape[4:], jnp.float32)
    for px in range(2):
        for pz in range(count):
            for py in range(2):
                for pc in range(2):
                    total += smalls[px, pz, py, pc].astype(jnp.float32)
    vecs[...] = total[0:8, :]
    wide = vecs.shape[1]
    for half in range(2):
        for k in range(2):
            row = 8 + half * 2 + k
            b_up[half : half + 1, k * wide : (k + 1) * wide] = total[row : row + 1, :]
    gathers[2].finish()

    flat = weights.reshape(3, 2, vecs.shape[1], weights.shape[6])
    g_flat = grads.reshape(3, 2, vecs.shape[1], weights.shape[6])
    w0, w1, w2 = flat.at[0], flat.at[1], flat.at[2]
    qkv_phase(x, w2, vecs, h1t, query, key, value)

    def second_step():
        gathers[0].after_second()
        gathers[1].after_second()

    def third_step():
        gathers[0].after_third()
        gathers[1].after_third()

    attend_phase(query, key, value, marks, marks_col, bias, mixed, logs, ((0, second_step), (3, third_step)))
    gathers[0].finish()
    gathers[1].finish()
    send_out = lambda tile: forward_rows(outs, out_base, tile).start()
    middle_phase(x, cot, marks_col, w0, w1, w2, vecs, b_up, mixed, h2t, glowt, glow2t, act, gpre, gmix, dots,
                 outs.at[place.x], gres, sums, sums_up, send_out)
    weight_phase(h2t, gpre, g_flat, 0)
    reduces[0].send(0)
    weight_phase(glowt, act, g_flat, 1)
    reduces[1].send(0)
    output_weight_phase(glow2t, mixed, g_flat)

    def back_first():
        for part in range(2):
            reduces[part].take(0)
            reduces[part].send(1)

    def back_second():
        for part in range(2):
            reduces[part].take(1)
            reduces[part].send(2)

    attend_back_phase(query, key, value, gmix, marks, marks_col, bias, logs, dots, gq_wide, gk, gv,
                      ((1, back_first), (3, back_second)))
    for part in range(2):
        reduces[part].take(2)
        reduces[part].send(3)
    round_phase(gq_wide, gq)
    qkv_weight_phase(h1t, gq, gk, gv, g_flat)
    reduces[2].send(0)
    send_gx = lambda tile: forward_rows(grads_x, gx_base, tile).start()
    input_phase(x, w2, vecs, gq, gk, gv, gres, sums, grads_x.at[place.x], send_gx)
    small_tot[0:8, :] = sums[...]
    for half in range(2):
        for k in range(2):
            row = 8 + half * 2 + k
            small_tot[row : row + 1, :] = sums_up[half : half + 1, k * wide : (k + 1) * wide]
    small_tot[12:16, :] = jnp.zeros((4, wide), jnp.float32)

    def small_copy(number, axis):
        return wire.copy(small_tot, small_from.at[number], small_base + number, place.other(axis))

    for number, axis in enumerate("cyx"):
        small_copy(number, axis).start()
        reduces[2].take(number)
        reduces[2].send(number + 1)
        small_copy(number, axis).wait()
        small_tot[...] += small_from[number]
    last = []
    for hop in range(1, count):
        device, z = place.along(hop)
        copy = wire.copy(small_tot, small_from.at[2 + hop], small_base + 2 + hop, device)
        copy.start()
        last.append(copy)
    for part in range(2):
        reduces[part].take(3)
    g_up[...] = reduces[0].result()
    g_down[...] = reduces[1].result()
    for copy in last:
        copy.wait_recv()
    ordered = jnp.zeros(small_tot.shape, jnp.float32)
    for z in range(count):
        term = small_tot[...]
        for hop in range(1, count):
            term = jnp.where(lax.rem(place.z + count - hop, count) == z, small_from[2 + hop], term)
        ordered += term
    small_sum[...] = ordered
    reduces[2].take(3)
    g_mix[...] = reduces[2].result()

    def land(tile, _):
        forward_rows(outs, out_base, tile).wait()
        forward_rows(grads_x, gx_base, tile).wait()
        return 0

    lax.fori_loop(0, tiles, land, 0)
    for gather in gathers:
        gather.drain()
    for copy in tiny.z_copies():
        copy.wait_send()
    for axis in "yxc":
        tiny.step(axis).wait_send()
    for reduce in reduces:
        reduce.drain()
    for copy in last:
        copy.wait_send()


def whole(acts, cots, chain_ids, key_keep, w_up, w_down_t, w_mix, small, count):
    slots, width = acts.shape[1], acts.shape[2]
    rows, columns = w_up.shape
    bf, f32 = jnp.bfloat16, jnp.float32
    V = pltpu.VMEM
    half = (2, slots, width // 2)
    any_space = pl.BlockSpec(memory_space=pl.ANY)
    sems = 3 * GATHER_SEMS + SMALL_SEMS + 3 * REDUCE_SEMS + 16 + 8
    out_shape = (
        jax.ShapeDtypeStruct((2, slots, width), bf),
        jax.ShapeDtypeStruct((2, slots, width), bf),
        jax.ShapeDtypeStruct((rows, columns), f32),
        jax.ShapeDtypeStruct((rows, columns), f32),
        jax.ShapeDtypeStruct((rows, columns), f32),
        jax.ShapeDtypeStruct(small.shape, f32),
    )
    scratch = [
        V((3, 2, count, 2, 2, rows, columns), bf), V((2, count, 2, 2, *small.shape), bf),
        V((slots, width), bf), V((slots, width), bf), V((8, width), f32), V((2, columns), f32),
        V((8, slots), f32), V((slots, 8), f32), V((8, width), f32), V((2, columns), f32),
        V((width, slots), bf), V(half, bf), V(half, bf), V(half, bf), V((TILE, slots), f32), V(half, bf),
        V((2, 4, slots), f32), V((width, slots), bf), V((width, slots), bf), V((width, slots), bf),
        V((2, slots, columns), bf), V((2, slots, columns), bf), V(half, bf), V((2, 4, slots), f32),
        V((slots, width), f32), V(half, f32), V(half, bf), V(half, bf), V(half, bf),
        V((3, 2, count, 2, 2, rows, columns), bf),
        V((3, 2, count, 2, rows, columns), bf),
        V((3, count, 2, rows // 2, columns), bf), V((3, 2, count, rows // 2, columns), bf),
        V((3, count, rows // 2, columns), bf), V((3, count, rows // 2, columns), bf),
        V((3, count - 1, rows, columns), bf),
        V((count + 2, *small.shape), f32), V(small.shape, f32),
        pltpu.SemaphoreType.DMA((6,)), pltpu.SemaphoreType.DMA((sems,)), pltpu.SemaphoreType.DMA((sems,)),
    ]
    return pl.pallas_call(
        whole_kernel,
        out_shape=out_shape,
        in_specs=[any_space, any_space, FULL, FULL, any_space, any_space, any_space, any_space],
        out_specs=(FULL,) * 6,
        scratch_shapes=scratch,
        compiler_params=pltpu.CompilerParams(
            vmem_limit_bytes=67043328, collective_id=0, has_side_effects=True
        ),
    )(acts, cots, chain_ids, key_keep, w_up, w_down_t, w_mix, small)


def product(left, right):
    return jnp.dot(left, right, preferred_element_type=jnp.float32)


def normalize(values, scale_row, shift_row):
    row_mean = jnp.mean(values, axis=-1, keepdims=True)
    centred = values - row_mean
    inverse = lax.rsqrt(jnp.mean(centred * centred, axis=-1, keepdims=True) + epsilon)
    scaled = centred * inverse
    return (scaled * scale_row + shift_row, scaled, inverse)


def normalize_back(grad_rows, scaled, inverse, scale_row):
    inner = grad_rows * scale_row
    return inverse * (
        inner
        - jnp.mean(inner, axis=-1, keepdims=True)
        - scaled * jnp.mean(inner * scaled, axis=-1, keepdims=True)
    )


def gelu_slope(values):
    normal_cdf = 0.5 * (1.0 + lax.erf(values * 0.7071067811865476))
    density = jnp.exp(-0.5 * values * values) * 0.3989422804014327
    return normal_cdf + values * density


def permitted(chain_rows, keep_rows):
    slot_count = chain_rows.shape[0]
    same_chain = chain_rows[:, None] == chain_rows[None, :]
    diagonal = lax.broadcasted_iota(jnp.int32, (slot_count, slot_count), 0) == lax.broadcasted_iota(
        jnp.int32, (slot_count, slot_count), 1
    )
    return same_chain & ((keep_rows[None, :] == 1) | diagonal)


def head_scores(query, key_rows, allowed, head_count, head_width):
    query_heads = query.reshape(-1, head_count, head_width)
    key_heads = key_rows.reshape(-1, head_count, head_width)
    scores = jnp.einsum(
        "qhd,khd->hqk", query_heads, key_heads, preferred_element_type=jnp.float32
    ) * (1.0 / math.sqrt(head_width))
    return jnp.where(allowed[None], scores, masked_value)


def forward(rows_in, chain_rows, keep_rows, weights, join=lambda a: a):
    qkv_full, out_full, up_full, down_full, bias_qv, bias_up, bias_out, gain_full, shift_full = (
        weights
    )
    head_count = bias_qv.shape[1]
    head_width = bias_qv.shape[2]
    row_count = rows_in.shape[0]
    bias_qv = bias_qv.astype(jnp.float32)
    bias_out = bias_out.astype(jnp.float32)
    gain_full = gain_full.astype(jnp.float32)
    shift_full = shift_full.astype(jnp.float32)
    allowed = permitted(chain_rows, keep_rows)
    normed_one, scaled_one, inverse_one = normalize(rows_in, gain_full[0], shift_full[0])
    hidden_one = normed_one.astype(jnp.bfloat16)
    query = (product(hidden_one, qkv_full[0]) + bias_qv[0].reshape(-1)).astype(jnp.bfloat16)
    key_rows = product(hidden_one, qkv_full[1]).astype(jnp.bfloat16)
    value_rows = (product(hidden_one, qkv_full[2]) + bias_qv[1].reshape(-1)).astype(jnp.bfloat16)
    scores = head_scores(query, key_rows, allowed, head_count, head_width)
    row_top = jnp.max(scores, axis=-1, keepdims=True)
    log_total = jnp.log(jnp.sum(jnp.exp(scores - row_top), axis=-1, keepdims=True)) + row_top
    probs_low = jnp.exp(scores - log_total).astype(jnp.bfloat16)
    mixed = jnp.einsum(
        "hqk,khd->qhd",
        probs_low,
        value_rows.reshape(row_count, head_count, head_width),
        preferred_element_type=jnp.float32,
    )
    mixed = mixed.reshape(row_count, -1).astype(jnp.bfloat16)
    partial_attn = product(mixed, out_full)
    resid = rows_in + join(partial_attn) + bias_out[0]
    normed_two, scaled_two, inverse_two = normalize(resid, gain_full[1], shift_full[1])
    hidden_two = normed_two.astype(jnp.bfloat16)
    pre = product(hidden_two, up_full) + bias_up.astype(jnp.float32).reshape(-1)
    act = jax.nn.gelu(pre, approximate=False).astype(jnp.bfloat16)
    partial_ffn = product(act, down_full)
    result = (
        resid + join(partial_ffn.astype(jnp.bfloat16)).astype(jnp.float32) + bias_out[1]
    )
    kept = (
        allowed,
        scaled_one,
        inverse_one,
        hidden_one,
        query,
        key_rows,
        value_rows,
        log_total,
        mixed,
        scaled_two,
        inverse_two,
        hidden_two,
        pre,
        act,
    )
    return (result, kept)


def backward(grad_out, result, kept, weights, join=lambda a: a):
    qkv_full, out_full, up_full, down_full, bias_qv, bias_up, bias_out, gain_full, shift_full = (
        weights
    )
    (
        allowed,
        scaled_one,
        inverse_one,
        hidden_one,
        query,
        key_rows,
        value_rows,
        log_total,
        mixed,
        scaled_two,
        inverse_two,
        hidden_two,
        pre,
        act,
    ) = kept
    head_count = bias_qv.shape[1]
    head_width = bias_qv.shape[2]
    row_count = grad_out.shape[0]
    gain_full = gain_full.astype(jnp.float32)
    grad_low = grad_out.astype(jnp.bfloat16)
    grad_down = product(act.T, grad_low)
    grad_pre = (product(grad_low, down_full.T) * gelu_slope(pre)).astype(jnp.bfloat16)
    grad_bup = jnp.sum(grad_pre, axis=0, dtype=jnp.float32).reshape(bias_up.shape)
    grad_up = product(hidden_two.T, grad_pre)
    partial_two = product(grad_pre, up_full.T)
    grad_two = join(partial_two.astype(jnp.bfloat16)).astype(jnp.float32)
    gain_two = jnp.sum(grad_two * scaled_two, axis=0)
    shift_two = jnp.sum(grad_two, axis=0)
    grad_resid = grad_out + normalize_back(grad_two, scaled_two, inverse_two, gain_full[1])
    resid_low = grad_resid.astype(jnp.bfloat16)
    grad_out_proj = product(mixed.T, resid_low)
    grad_mixed = (
        product(resid_low, out_full.T)
        .astype(jnp.bfloat16)
        .reshape(row_count, head_count, head_width)
    )
    scores = head_scores(query, key_rows, allowed, head_count, head_width)
    probs = jnp.exp(scores - log_total)
    probs_low = probs.astype(jnp.bfloat16)
    value_heads = value_rows.reshape(row_count, head_count, head_width)
    grad_value = jnp.einsum(
        "hqk,qhd->khd", probs_low, grad_mixed, preferred_element_type=jnp.float32
    ).astype(jnp.bfloat16)
    grad_probs = jnp.einsum(
        "qhd,khd->hqk", grad_mixed, value_heads, preferred_element_type=jnp.float32
    )
    grad_scores = (
        probs * (grad_probs - jnp.sum(grad_probs * probs, axis=-1, keepdims=True))
    ).astype(jnp.bfloat16)
    score_scale = 1.0 / math.sqrt(head_width)
    key_heads = key_rows.reshape(row_count, head_count, head_width)
    query_heads = query.reshape(row_count, head_count, head_width)
    grad_query = (
        jnp.einsum("hqk,khd->qhd", grad_scores, key_heads, preferred_element_type=jnp.float32)
        * score_scale
    ).astype(jnp.bfloat16)
    grad_key = (
        jnp.einsum("hqk,qhd->khd", grad_scores, query_heads, preferred_element_type=jnp.float32)
        * score_scale
    ).astype(jnp.bfloat16)
    stacked = jnp.stack(
        [
            grad_query.reshape(row_count, -1),
            grad_key.reshape(row_count, -1),
            grad_value.reshape(row_count, -1),
        ]
    )
    grad_qkv = jnp.einsum("rd,crk->cdk", hidden_one, stacked, preferred_element_type=jnp.float32)
    partial_one = jnp.einsum("crk,cdk->rd", stacked, qkv_full, preferred_element_type=jnp.float32)
    grad_one = join(partial_one.astype(jnp.bfloat16)).astype(jnp.float32)
    grad_bqv = jnp.stack(
        [
            jnp.sum(stacked[0], axis=0, dtype=jnp.float32),
            jnp.sum(stacked[2], axis=0, dtype=jnp.float32),
        ]
    ).reshape(2, head_count, head_width)
    gain_one = jnp.sum(grad_one * scaled_one, axis=0)
    shift_one = jnp.sum(grad_one, axis=0)
    grad_in = grad_resid + normalize_back(grad_one, scaled_one, inverse_one, gain_full[0])
    small_sums = jnp.stack(
        [
            jnp.sum(grad_resid, axis=0),
            jnp.sum(grad_out, axis=0),
            gain_one,
            gain_two,
            shift_one,
            shift_two,
        ]
    )
    local_grads = (
        grad_qkv,
        grad_out_proj,
        grad_up,
        grad_down,
        grad_bqv,
        grad_bup,
        small_sums[0:2],
        small_sums[2:4],
        small_sums[4:6],
    )
    return (result, grad_in, local_grads)


def body_generic(
    activations,
    cotangent,
    w_qkv,
    w_o,
    w_up,
    w_down,
    b_qv,
    b_up,
    out_bias,
    norm_gain,
    norm_bias,
    chain_ids,
    key_keep,
):
    batch_count = activations.shape[0]
    outputs = []
    input_grads = []
    running = None
    for batch_index in range(batch_count):
        weights = (
            lax.all_gather(w_qkv, "dp", axis=1, tiled=True),
            lax.all_gather(w_o, "dp", axis=1, tiled=True),
            lax.all_gather(w_up, "dp", axis=0, tiled=True),
            lax.all_gather(w_down, "dp", axis=1, tiled=True),
            lax.all_gather(b_qv, "dp", axis=2, tiled=True),
            lax.all_gather(b_up, "dp", axis=1, tiled=True),
            lax.all_gather(out_bias, "dp", axis=1, tiled=True),
            lax.all_gather(norm_gain, "dp", axis=1, tiled=True),
            lax.all_gather(norm_bias, "dp", axis=1, tiled=True),
        )
        result, kept = forward(
            activations[batch_index].astype(jnp.float32),
            chain_ids[batch_index],
            key_keep[batch_index],
            weights,
            lambda a: lax.psum(a, "mp"),
        )
        live_rows = (chain_ids[batch_index] >= 0).astype(jnp.float32)[:, None]
        output_rows, grad_in, local_grads = backward(
            cotangent[batch_index].astype(jnp.float32) * live_rows, result, kept, weights, lambda a: lax.psum(a, "mp")
        )
        outputs.append(output_rows)
        input_grads.append(grad_in)
        shares = (
            lax.psum_scatter(
                local_grads[0].astype(jnp.bfloat16), "dp", scatter_dimension=1, tiled=True
            ).astype(jnp.float32),
            lax.psum_scatter(
                local_grads[1].astype(jnp.bfloat16), "dp", scatter_dimension=1, tiled=True
            ).astype(jnp.float32),
            lax.psum_scatter(
                local_grads[2].astype(jnp.bfloat16), "dp", scatter_dimension=0, tiled=True
            ).astype(jnp.float32),
            lax.psum_scatter(
                local_grads[3].astype(jnp.bfloat16), "dp", scatter_dimension=1, tiled=True
            ).astype(jnp.float32),
            lax.psum_scatter(
                local_grads[4].astype(jnp.bfloat16), "dp", scatter_dimension=2, tiled=True
            ).astype(jnp.float32),
            lax.psum_scatter(
                local_grads[5].astype(jnp.bfloat16), "dp", scatter_dimension=1, tiled=True
            ).astype(jnp.float32),
            lax.psum_scatter(
                local_grads[6].astype(jnp.bfloat16), "dp", scatter_dimension=1, tiled=True
            ).astype(jnp.float32),
            lax.psum_scatter(
                local_grads[7].astype(jnp.bfloat16), "dp", scatter_dimension=1, tiled=True
            ).astype(jnp.float32),
            lax.psum_scatter(
                local_grads[8].astype(jnp.bfloat16), "dp", scatter_dimension=1, tiled=True
            ).astype(jnp.float32),
        )
        if running is None:
            running = tuple(shares)
        else:
            running = tuple(jax.tree.map(jnp.add, tuple(running), tuple(shares)))
    return (
        jnp.stack(outputs),
        jnp.stack(input_grads),
        running[0],
        running[1],
        running[2],
        running[3],
        running[4],
        running[5],
        running[6],
        running[7],
        running[8],
    )


def fits(mesh):
    return mesh.shape["mp"] == 2 and mesh.shape["dp"] == 16


def place_small(b_qv, b_up, out_bias, norm_gain, norm_bias):
    own, at, mp, dp = lax.axis_index("mp"), lax.axis_index("dp"), lax.axis_size("mp"), lax.axis_size("dp")
    here = jnp.arange(dp) == at
    mine = jnp.arange(mp) == own
    zero = jnp.zeros((), b_qv.dtype)
    spread = lambda a: jnp.where((here & (own == 0))[None, :, None], a[:, None, :], zero).reshape(2, -1)
    gain, shift, bias = spread(norm_gain), spread(norm_bias), spread(out_bias)
    qv = jnp.where(mine[None, :, None, None, None] & here[None, None, None, :, None], b_qv[:, None, :, None, :], zero)
    up = jnp.where(mine[:, None, None, None] & here[None, None, :, None], b_up[None, :, None, :], zero)
    width = gain.shape[1]
    rows = [gain[0:1], shift[0:1], gain[1:2], shift[1:2], qv.reshape(2, width), bias, up.reshape(-1, width)]
    table = jnp.concatenate(rows)
    return jnp.pad(table, ((0, 16 - table.shape[0]), (0, 0)))


def body_split(
    activations,
    cotangent,
    w_qkv,
    w_o,
    w_up,
    w_down,
    b_qv,
    b_up,
    out_bias,
    norm_gain,
    norm_bias,
    chain_ids,
    key_keep,
):
    own, at = lax.axis_index("mp"), lax.axis_index("dp")
    mp, dp = lax.axis_size("mp"), lax.axis_size("dp")
    w_mix = jnp.concatenate([w_qkv[0], w_qkv[1], w_qkv[2], w_o.T], axis=1)
    small = place_small(b_qv, b_up, out_bias, norm_gain, norm_bias)
    out, grad_x, g_up, g_down, g_mix, total = whole(
        activations, cotangent, chain_ids, key_keep, w_up, w_down.T, w_mix, small, dp // 4
    )
    pick = lambda a, axis: lax.dynamic_index_in_dim(a, at, axis, keepdims=False)
    take = lambda a: lax.dynamic_index_in_dim(a, own, 0, keepdims=False)
    pairs = lambda r0, r1: pick(jnp.stack([total[r0], total[r1]]).reshape(2, dp, -1), 1)
    s_qv = pick(take(total[BQ : BV + 1].reshape(2, mp, -1).transpose(1, 0, 2)).reshape(2, b_qv.shape[1], dp, -1), 2)
    s_bup = pick(take(total[8:12].reshape(mp, -1)).reshape(b_up.shape[0], dp, -1), 1)
    quarter = w_qkv.shape[2]
    return (
        out.astype(jnp.float32),
        grad_x.astype(jnp.float32),
        jnp.stack([g_mix[:, c * quarter : (c + 1) * quarter] for c in range(3)]),
        g_mix[:, 3 * quarter :].T,
        g_up,
        g_down.T,
        s_qv,
        s_bup,
        pairs(BO1, BO2),
        pairs(GAIN1, GAIN2),
        pairs(SHIFT1, SHIFT2),
    )


def solution(mesh):
    placed = (
        P(None, "dp", None),
        P(None, "dp", None),
        P(None, "dp", "mp"),
        P("mp", "dp"),
        P("dp", "mp"),
        P("mp", "dp"),
        P(None, "mp", "dp"),
        P("mp", "dp"),
        P(None, "dp"),
        P(None, "dp"),
        P(None, "dp"),
        P(None, "dp"),
        P(None, "dp"),
    )
    body = body_split if fits(mesh) else body_generic
    return jax.shard_map(
        body,
        mesh=mesh,
        in_specs=placed,
        out_specs=(
            P(None, "dp", None),
            P(None, "dp", None),
            P(None, "dp", "mp"),
            P("mp", "dp"),
            P("dp", "mp"),
            P("mp", "dp"),
            P(None, "mp", "dp"),
            P("mp", "dp"),
            P(None, "dp"),
            P(None, "dp"),
            P(None, "dp"),
        ),
        check_vma=False,
    )
```

```python
import functools
import math

import jax
import jax.numpy as jnp
from jax import lax
from jax.experimental import pallas as pl
from jax.experimental.pallas import tpu as pltpu
from jax.sharding import PartitionSpec as P

epsilon = 1e-05
masked_value = -1e30
TILE = 256
FULL = pl.BlockSpec(memory_space=pltpu.VMEM)

GAIN1, SHIFT1, GAIN2, SHIFT2, BQ, BV, BO1, BO2 = range(8)


def dot(left, right):
    return jnp.dot(left, right, preferred_element_type=jnp.float32)


def dot_last(left, right):
    return lax.dot_general(left, right, (((1,), (1,)), ((), ())), preferred_element_type=jnp.float32)


def dot_first(left, right):
    return lax.dot_general(left, right, (((0,), (0,)), ((), ())), preferred_element_type=jnp.float32)


def tile_rows(index):
    return pl.ds(pl.multiple_of(index * TILE, TILE), TILE)


def statistics(values):
    centred = values - jnp.mean(values, axis=-1, keepdims=True)
    inverse = lax.rsqrt(jnp.mean(centred * centred, axis=-1, keepdims=True) + epsilon)
    return centred * inverse, inverse


def norm_back(grad, scaled, inverse, gain):
    inner = grad * gain
    return inverse * (
        inner - jnp.mean(inner, axis=-1, keepdims=True) - scaled * jnp.mean(inner * scaled, axis=-1, keepdims=True)
    )


def add_row(ref, row, values):
    ref[row : row + 1, :] += jnp.sum(values, axis=0, keepdims=True)


def qkv_phase(x, w_mix, vecs, h1t, query, key, value):
    halves, quarter = query.shape[0], query.shape[2]
    scale = 1.0 / math.sqrt(64)

    def step(tile, _):
        rows = tile_rows(tile)
        scaled, _ = statistics(x[rows, :].astype(jnp.float32))
        hidden = (scaled * vecs[GAIN1 : GAIN1 + 1, :] + vecs[SHIFT1 : SHIFT1 + 1, :]).astype(jnp.bfloat16)
        h1t[:, rows] = hidden.T
        for half in range(halves):
            cols = slice(half * quarter, (half + 1) * quarter)
            part = lambda c: dot(hidden, w_mix[half, :, c * quarter : (c + 1) * quarter])
            query[half, rows, :] = ((part(0) + vecs[BQ : BQ + 1, cols]).astype(jnp.bfloat16) * scale).astype(jnp.bfloat16)
            key[half, rows, :] = part(1).astype(jnp.bfloat16)
            value[half, rows, :] = (part(2) + vecs[BV : BV + 1, cols]).astype(jnp.bfloat16)
        return 0

    lax.fori_loop(0, x.shape[0] // TILE, step, 0)


def attend_phase(query, key, value, marks_row, marks_col, bias, mixed, logs, beside):
    halves, slots, quarter = query.shape

    def tile_step(tile, _):
        rows = tile_rows(tile)
        same = marks_col[rows, 0:1] == marks_row[1:2, :]
        here = lax.broadcasted_iota(jnp.int32, (TILE, slots), 0) + tile * TILE
        there = lax.broadcasted_iota(jnp.int32, (TILE, slots), 1)
        bias[...] = jnp.where(same | (here == there), 0.0, masked_value)

        def half_step(half, _):
            for when, action in beside:
                pl.when(tile * halves + half == when)(action)
            lane = lax.broadcasted_iota(jnp.int32, (TILE, 128), 1)
            stats = jnp.zeros((TILE, 128), jnp.float32)
            for pair in range(quarter // 128):
                cols = slice(pair * 128, (pair + 1) * 128)
                both = query[half, rows, cols]
                keys = key[half, :, cols]
                values = value[half, :, cols]
                sums = []
                for side in range(2):
                    mine = (lane < 64) if side == 0 else (lane >= 64)
                    scores = dot_last(jnp.where(mine, both, jnp.zeros_like(both)), keys) + bias[...]
                    top = jnp.max(scores, axis=1, keepdims=True)
                    expo = jnp.exp(scores - top)
                    total = jnp.sum(expo, axis=1, keepdims=True)
                    sums.append(dot(expo.astype(jnp.bfloat16), values) * (1.0 / total))
                    stats = jnp.where(lane == pair * 2 + side, top + jnp.log(total), stats)
                mixed[half, rows, cols] = jnp.where(lane < 64, sums[0], sums[1]).astype(jnp.bfloat16)
            logs[half, :, rows] = stats.T[0:4, :]
            return 0

        lax.fori_loop(0, halves, half_step, 0)
        return 0

    lax.fori_loop(0, slots // TILE, tile_step, 0)


def middle_phase(x, cot, live_col, w_up, w_down, w_o, vecs, b_up, mixed, h2t, glowt, glow2t, act, gpre, gmix, dots, out, gres, sums, sums_up, send):
    halves, quarter, hidden_half = mixed.shape[0], mixed.shape[2], w_up.shape[2]

    def step(tile, _):
        rows = tile_rows(tile)
        attn = sum(dot_last(mixed[half, rows, :], w_o[half]) for half in range(halves))
        resid = x[rows, :].astype(jnp.float32) + attn + vecs[BO1 : BO1 + 1, :]
        scaled, inverse = statistics(resid)
        hidden = (scaled * vecs[GAIN2 : GAIN2 + 1, :] + vecs[SHIFT2 : SHIFT2 + 1, :]).astype(jnp.bfloat16)
        h2t[:, rows] = hidden.T
        grad_out = cot[rows, :].astype(jnp.float32) * live_col[rows, 2:3]
        grad_low = grad_out.astype(jnp.bfloat16)
        glowt[:, rows] = grad_low.T
        ffn = jnp.zeros(resid.shape, jnp.float32)
        grad_two = jnp.zeros(resid.shape, jnp.float32)
        for half in range(halves):
            pre = dot(hidden, w_up[half]) + b_up[half : half + 1, :]
            cdf = 0.5 * (1.0 + lax.erf(pre * 0.7071067811865476))
            slope = cdf + pre * (jnp.exp(-0.5 * pre * pre) * 0.3989422804014327)
            active = (pre * cdf).astype(jnp.bfloat16)
            act[half, rows, :] = active
            ffn += dot_last(active, w_down[half])
            grad_pre = (dot(grad_low, w_down[half]) * slope).astype(jnp.bfloat16)
            gpre[half, rows, :] = grad_pre
            grad_two += dot_last(grad_pre, w_up[half])
            add_row(sums_up, half, grad_pre.astype(jnp.float32))
        out[rows, :] = (resid + ffn + vecs[BO2 : BO2 + 1, :]).astype(out.dtype)
        add_row(sums, GAIN2, grad_two * scaled)
        add_row(sums, SHIFT2, grad_two)
        grad_resid = grad_out + norm_back(grad_two, scaled, inverse, vecs[GAIN2 : GAIN2 + 1, :])
        add_row(sums, BO1, grad_resid)
        add_row(sums, BO2, grad_out)
        gres[rows, :] = grad_resid
        low = grad_resid.astype(jnp.bfloat16)
        glow2t[:, rows] = low.T
        for half in range(halves):
            grad_mixed = dot(low, w_o[half]).astype(jnp.bfloat16)
            gmix[half, rows, :] = grad_mixed
            both = grad_mixed.astype(jnp.float32) * mixed[half, rows, :].astype(jnp.float32)
            dots[half, :, rows] = jnp.sum(both.T.reshape(quarter // 64, 64, TILE), axis=1)
        send(tile)
        return 0

    sums[...] = jnp.zeros_like(sums)
    sums_up[...] = jnp.zeros_like(sums_up)
    lax.fori_loop(0, x.shape[0] // TILE, step, 0)


def weight_phase(left_t, right, grads):
    halves, _, columns = right.shape
    chunk = min(columns, 512)

    def step(half, _):
        for start in range(0, columns, chunk):
            cols = slice(start, start + chunk)
            grads[half, :, cols] = dot(left_t[...], right[half, :, cols]).astype(jnp.bfloat16)
        return 0

    lax.fori_loop(0, halves, step, 0)


def attend_back_phase(query, key, value, gmix, marks_row, marks_col, bias, logs, dots, grad_query, grad_key, grad_value, beside):
    halves, slots, quarter = query.shape
    grad_query[...] = jnp.zeros_like(grad_query)

    def tile_step(tile, _):
        rows = tile_rows(tile)
        same = marks_col[rows, 1:2] == marks_row[0:1, :]
        here = lax.broadcasted_iota(jnp.int32, (TILE, slots), 0) + tile * TILE
        there = lax.broadcasted_iota(jnp.int32, (TILE, slots), 1)
        bias[...] = jnp.where(same | (here == there), 0.0, masked_value)

        def half_step(half, _):
            for when, action in beside:
                pl.when(tile * halves + half == when)(action)
            for pair in range(quarter // 128):
                cols = slice(pair * 128, (pair + 1) * 128)
                queries, grads = query[half, :, cols], gmix[half, :, cols]
                keys, values = key[half, rows, cols], value[half, rows, cols]
                lane = lax.broadcasted_iota(jnp.int32, (TILE, 128), 1)
                wide = lax.broadcasted_iota(jnp.int32, (slots, 128), 1)
                parts = []
                for side in range(2):
                    head = pair * 2 + side
                    mine = (lane < 64) if side == 0 else (lane >= 64)
                    zero = jnp.zeros_like(keys)
                    scores = dot_last(jnp.where(mine, keys, zero), queries) + bias[...]
                    probs = jnp.exp(scores - logs[half, head : head + 1, :])
                    grad_probs = dot_last(jnp.where(mine, values, zero), grads)
                    grad_scores = (probs * (grad_probs - dots[half, head : head + 1, :])).astype(jnp.bfloat16)
                    parts.append(
                        (dot(probs.astype(jnp.bfloat16), grads), dot(grad_scores, queries), dot_first(grad_scores, keys))
                    )
                grad_value[half, rows, cols] = jnp.where(lane < 64, parts[0][0], parts[1][0]).astype(jnp.bfloat16)
                grad_key[half, rows, cols] = jnp.where(lane < 64, parts[0][1], parts[1][1]).astype(jnp.bfloat16)
                grad_query[half, :, cols] += jnp.where(wide < 64, parts[0][2], parts[1][2])
            return 0

        lax.fori_loop(0, halves, half_step, 0)
        return 0

    lax.fori_loop(0, slots // TILE, tile_step, 0)


def round_phase(wide, low):
    scale = 1.0 / math.sqrt(64)

    def step(half, _):
        low[half] = (wide[half] * scale).astype(jnp.bfloat16)
        return 0

    lax.fori_loop(0, low.shape[0], step, 0)


def qkv_weight_phase(h1t, grad_query, grad_key, grad_value, grads, then):
    halves, _, quarter = grad_key.shape

    def step(half, _):
        for c, ref in enumerate((grad_query, grad_key, grad_value)):
            grads[half, :, c * quarter : (c + 1) * quarter] = dot(h1t[...], ref[half]).astype(jnp.bfloat16)
        then(half)
        return 0

    lax.fori_loop(0, halves, step, 0)


def input_phase(x, w_mix, vecs, grad_query, grad_key, grad_value, gres, sums, grad_x, send):
    halves, slots, quarter = grad_key.shape

    def step(tile, _):
        rows = tile_rows(tile)
        scaled, inverse = statistics(x[rows, :].astype(jnp.float32))
        grad_one = jnp.zeros((TILE, x.shape[1]), jnp.float32)
        for half in range(halves):
            cols = slice(half * quarter, (half + 1) * quarter)
            three = (grad_query[half, rows, :], grad_key[half, rows, :], grad_value[half, rows, :])
            for c in range(3):
                grad_one += dot_last(three[c], w_mix[half, :, c * quarter : (c + 1) * quarter])
            sums[BQ : BQ + 1, cols] += jnp.sum(three[0].astype(jnp.float32), axis=0, keepdims=True)
            sums[BV : BV + 1, cols] += jnp.sum(three[2].astype(jnp.float32), axis=0, keepdims=True)
        add_row(sums, GAIN1, grad_one * scaled)
        add_row(sums, SHIFT1, grad_one)
        grad_x[rows, :] = (gres[rows, :] + norm_back(grad_one, scaled, inverse, vecs[GAIN1 : GAIN1 + 1, :])).astype(grad_x.dtype)
        send(tile)
        return 0

    lax.fori_loop(0, slots // TILE, step, 0)


class Place:
    def __init__(self, depth_z):
        at = lax.axis_index("dp")
        self.x, self.z, self.y, self.c = lax.axis_index("mp"), at // 4, (at // 2) % 2, at % 2
        self.count = depth_z

    def other(self, axis):
        x, z, y, c = self.x, self.z, self.y, self.c
        x, y, c = (1 - x if axis == "x" else x), (1 - y if axis == "y" else y), (1 - c if axis == "c" else c)
        return {"dp": z * 4 + y * 2 + c, "mp": x}

    def along(self, hop):
        z = lax.rem(self.z + hop, self.count)
        return {"dp": z * 4 + self.y * 2 + self.c, "mp": self.x}, z


class Wire:
    def __init__(self, send, recv):
        self.send_sems, self.recv_sems = send, recv

    def copy(self, src, dst, number, device):
        return pltpu.make_async_remote_copy(
            src_ref=src,
            dst_ref=dst,
            send_sem=self.send_sems.at[number],
            recv_sem=self.recv_sems.at[number],
            device_id=device,
            device_id_type=pl.DeviceIdType.MESH,
        )


GATHER_SEMS = 15
REDUCE_SEMS = 9
SMALL_SEMS = 7


class Gather:
    def __init__(self, ref, base, wire, place):
        self.ref, self.base, self.wire, self.place = ref, base, wire, place
        self.top = pl.ds(0, ref.shape[4] // 2)
        self.low = pl.ds(ref.shape[4] // 2, ref.shape[4] // 2)

    def own(self, axis, src, number):
        return self.wire.copy(src, src, self.base + number, self.place.other(axis))

    def z_copies(self):
        p, ref = self.place, self.ref
        mine = ref.at[p.x, p.z, p.y, p.c]
        for hop in range(1, p.count):
            device, _ = p.along(hop)
            yield self.wire.copy(mine, mine, self.base + hop - 1, device)

    def second(self):
        p, ref = self.place, self.ref
        return (
            self.own("y", ref.at[p.x, :, p.y, p.c, self.top], 3),
            self.own("x", ref.at[p.x, :, p.y, p.c, self.low], 4),
        )

    def third(self):
        p, ref = self.place, self.ref
        return (
            self.own("x", ref.at[p.x, :, :, p.c, self.top], 5),
            self.own("y", ref.at[:, :, p.y, p.c, self.low], 6),
        )

    def core(self, step):
        p, ref = self.place, self.ref
        if step == 1:
            return (self.own("c", ref.at[p.x, :, p.y, p.c], 7),)
        if step == 2:
            return (
                self.own("c", ref.at[p.x, :, 1 - p.y, p.c, self.top], 8),
                self.own("c", ref.at[1 - p.x, :, p.y, p.c, self.low], 9),
            )
        return (
            self.own("c", ref.at[1 - p.x, :, :, p.c, self.top], 10),
            self.own("c", ref.at[:, :, 1 - p.y, p.c, self.low], 11),
        )

    def start(self):
        for copy in self.z_copies():
            copy.start()

    def after_start(self):
        for copy in self.z_copies():
            copy.wait_recv()
        for copy in self.second() + self.core(1):
            copy.start()

    def after_second(self):
        for copy in self.second():
            copy.wait_recv()
        for copy in self.third() + self.core(2):
            copy.start()

    def after_third(self):
        for copy in self.third():
            copy.wait_recv()
        for copy in self.core(3):
            copy.start()

    def finish(self):
        for step in (1, 2, 3):
            for copy in self.core(step):
                copy.wait_recv()

    def drain(self):
        for copy in self.z_copies():
            copy.wait_send()
        for copy in self.second() + self.third() + self.core(1) + self.core(2) + self.core(3):
            copy.wait_send()


class SmallGather:
    def __init__(self, ref, base, wire, place):
        self.ref, self.base, self.wire, self.place = ref, base, wire, place

    def z_copies(self):
        p = self.place
        mine = self.ref.at[p.x, p.z, p.y, p.c]
        return [self.wire.copy(mine, mine, self.base + hop - 1, p.along(hop)[0]) for hop in range(1, p.count)]

    def step(self, axis):
        p, ref = self.place, self.ref
        src = {"y": ref.at[p.x, :, p.y, p.c], "x": ref.at[p.x, :, :, p.c], "c": ref.at[:, :, :, p.c]}[axis]
        return self.wire.copy(src, src, self.base + {"y": 3, "x": 4, "c": 5}[axis], p.other(axis))


class Reduce:
    def __init__(self, grads, from_core, from_a, from_b, from_c, from_d, from_z, base, wire, place):
        self.grads, self.base, self.wire, self.place = grads, base, wire, place
        self.from_core, self.from_a, self.from_b = from_core, from_a, from_b
        self.from_c, self.from_d, self.from_z = from_c, from_d, from_z
        rows = grads.shape[4]
        self.top, self.low = pl.ds(0, rows // 2), pl.ds(rows // 2, rows // 2)

    def copies(self, step):
        p, g, w, base = self.place, self.grads, self.wire, self.base
        if step == 0:
            return [w.copy(g.at[:, :, :, 1 - p.c], self.from_core, base, p.other("c"))]
        if step == 1:
            return [
                w.copy(g.at[1 - p.x, :, :, p.c, self.top], self.from_a, base + 1, p.other("x")),
                w.copy(g.at[:, :, 1 - p.y, p.c, self.low], self.from_b, base + 2, p.other("y")),
            ]
        if step == 2:
            return [
                w.copy(g.at[p.x, :, 1 - p.y, p.c, self.top], self.from_c, base + 3, p.other("y")),
                w.copy(g.at[1 - p.x, :, p.y, p.c, self.low], self.from_d, base + 4, p.other("x")),
            ]
        out = []
        for hop in range(1, p.count):
            device, z = p.along(hop)
            out.append(w.copy(g.at[p.x, z, p.y, p.c], self.from_z.at[hop - 1], base + 4 + hop, device))
        return out

    def send(self, step):
        for copy in self.copies(step):
            copy.start()

    def take(self, step):
        p, g = self.place, self.grads
        for copy in self.copies(step):
            copy.wait_recv()
        if step == 0:

            def add(index, _):
                x, z = index // p.count, lax.rem(index, p.count)
                for y in range(2):
                    g[x, z, y, p.c] += self.from_core[x, z, y]
                return 0

            lax.fori_loop(0, 2 * p.count, add, 0)
        elif step == 1:

            def add(z, _):
                for k in range(2):
                    g[p.x, z, k, p.c, self.top] += self.from_a[z, k]
                    g[k, z, p.y, p.c, self.low] += self.from_b[k, z]
                return 0

            lax.fori_loop(0, p.count, add, 0)
        elif step == 2:

            def add(z, _):
                g[p.x, z, p.y, p.c, self.top] += self.from_c[z]
                g[p.x, z, p.y, p.c, self.low] += self.from_d[z]
                return 0

            lax.fori_loop(0, p.count, add, 0)

    def result(self):
        p = self.place
        total = self.grads[p.x, p.z, p.y, p.c].astype(jnp.float32)
        for hop in range(1, p.count):
            total += self.from_z[hop - 1].astype(jnp.float32)
        return total

    def drain(self):
        for step in range(4):
            for copy in self.copies(step):
                copy.wait_send()


class ReduceLast:
    def __init__(self, grads, from_core, from_y, from_z, from_x, base, wire, place):
        self.grads, self.base, self.wire, self.place = grads, base, wire, place
        self.from_core, self.from_y, self.from_z, self.from_x = from_core, from_y, from_z, from_x

    def copies(self, step, chunk):
        p, g, w, base = self.place, self.grads, self.wire, self.base + 5 * chunk
        if step == 0:
            return [w.copy(g.at[chunk, :, :, 1 - p.c], self.from_core.at[chunk], base, p.other("c"))]
        if step == 1:
            return [w.copy(g.at[chunk, :, 1 - p.y, p.c], self.from_y.at[chunk], base + 1, p.other("y"))]
        out = []
        for hop in range(1, p.count):
            device, z = p.along(hop)
            out.append(w.copy(g.at[chunk, z, p.y, p.c], self.from_z.at[chunk, hop - 1], base + 1 + hop, device))
        return out

    def send(self, step, chunk):
        for copy in self.copies(step, chunk):
            copy.start()

    def take(self, step, chunk):
        p, g = self.place, self.grads
        for copy in self.copies(step, chunk):
            copy.wait_recv()

        def add(z, _):
            if step == 0:
                for y in range(2):
                    g[chunk, z, y, p.c] += self.from_core[chunk, z, y]
            else:
                g[chunk, z, p.y, p.c] += self.from_y[chunk, z]
            return 0

        if step < 2:
            lax.fori_loop(0, p.count, add, 0)

    def total(self, chunk):
        p = self.place
        total = self.grads[chunk, p.z, p.y, p.c].astype(jnp.float32)
        for hop in range(1, p.count):
            total += self.from_z[chunk, hop - 1].astype(jnp.float32)
        return total

    def last(self):
        p = self.place
        mine = self.grads.at[1 - p.x, p.z, p.y, p.c]
        return self.wire.copy(mine, self.from_x, self.base + 10, p.other("x"))

    def send_last(self):
        p = self.place
        self.grads[1 - p.x, p.z, p.y, p.c] = self.total(1 - p.x).astype(jnp.bfloat16)
        self.last().start()

    def result(self):
        total = self.total(self.place.x)
        self.last().wait()
        return total + self.from_x[...].astype(jnp.float32)

    def drain(self):
        for chunk in range(2):
            for step in range(3):
                for copy in self.copies(step, chunk):
                    copy.wait_send()


LAST_SEMS = 11


def lane_is(rows, lanes, test):
    row = lax.broadcasted_iota(jnp.int32, (rows, lanes), 0)
    lane = lax.broadcasted_iota(jnp.int32, (rows, lanes), 1)
    return jnp.where(test(row, lane), 1.0, 0.0)


def place_small(b_qv, b_up_t, out_bias, norm_gain, norm_bias, width, own, at):
    heads, hd = b_qv.shape[1], b_qv.shape[2]
    span = out_bias.shape[1]
    groups = width // 64
    first = jnp.where(own == 0, 1.0, 0.0)
    wide = lane_is(span, width, lambda row, lane: lane == at * span + row).astype(jnp.bfloat16)
    narrow = lane_is(hd, width, lambda row, lane: lane % 64 == at * hd + row).astype(jnp.bfloat16)
    gain, shift, bias = [dot(ref[...], wide) * first for ref in (norm_gain, norm_bias, out_bias)]
    spot = lane_is(heads, width, lambda row, lane: lane // 64 == own * heads + row)
    qv = [jnp.sum(dot(b_qv[k], narrow) * spot, axis=0, keepdims=True) for k in range(2)]
    ups = dot_first(b_up_t[...], narrow) * lane_is(b_up_t.shape[1], width, lambda row, lane: lane // 64 == row % groups)
    ups = [jnp.sum(ups[k * groups : (k + 1) * groups], axis=0, keepdims=True) for k in range(2)]
    ups = [row * scale for scale in (first, 1.0 - first) for row in ups]
    rows = [gain[0:1], shift[0:1], gain[1:2], shift[1:2], *qv, bias[0:1], bias[1:2], *ups]
    return rows


def exact(left, right):
    return lax.dot_general(
        left, right, (((1,), (1,)), ((), ())), precision=lax.Precision.HIGHEST, preferred_element_type=jnp.float32
    )


def pick_small(total, own, at, s_qv, s_up, s_bias, s_gain, s_shift):
    width = total.shape[1]
    heads, hd = s_qv.shape[1], s_qv.shape[2]
    span, groups = s_bias.shape[1], width // 64
    wide = lane_is(span, width, lambda row, lane: lane == at * span + row)
    narrow = lane_is(hd, width, lambda row, lane: lane % 64 == at * hd + row)
    vectors = exact(total[0:8, :], wide)
    for ref, (one, two) in ((s_gain, (GAIN1, GAIN2)), (s_shift, (SHIFT1, SHIFT2)), (s_bias, (BO1, BO2))):
        ref[0:1, :] = vectors[one : one + 1, :]
        ref[1:2, :] = vectors[two : two + 1, :]
    spot = lane_is(heads, width, lambda row, lane: lane // 64 == own * heads + row)
    for k in range(2):
        s_qv[k] = exact(total[BQ + k : BQ + k + 1, :] * spot, narrow)
    mine = jnp.where(own == 0, total[8:10, :], total[10:12, :])
    rows = [jnp.broadcast_to(mine[k : k + 1, :], (groups, width)) for k in range(2)]
    spot = lane_is(2 * groups, width, lambda row, lane: lane // 64 == row % groups)
    s_up[...] = exact(narrow, jnp.concatenate(rows) * spot)


def whole_kernel(
    acts, cots, chain_ids, key_keep, w_up, w_down_t, w_o_t, w_qkv, b_qv, b_up_t, out_bias, norm_gain, norm_bias,
    outs, grads_x, g_up, g_down, g_out, g_qkv, small_sum,
    w_0, w_1, w_2, w_3, smalls, x, cot, vecs, b_up, marks, marks_col, sums, sums_up,
    h1t, query, key, value, bias, mixed, logs, h2t, glowt, glow2t, act, gpre, gmix, dots, gres,
    gq_wide, gq, gk, gv, *rest,
):
    weights = (w_0, w_1, w_2, w_3)
    g_parts, rest = rest[:4], rest[4:]
    froms, rest = rest[:22], rest[22:]
    small_from, small_tot, local, send, recv = rest
    count, wide = w_0.shape[1], vecs.shape[1]
    place = Place(count)
    wire = Wire(send, recv)
    me = (place.x, place.z, place.y, place.c)
    quarter = w_qkv.shape[2]
    loads = [
        pltpu.make_async_copy(w_qkv.at[c], w_3.at[(*me, slice(None), pl.ds(c * quarter, quarter))], local.at[c])
        for c in range(3)
    ]
    for k, (ref, full) in enumerate(((w_up, w_0), (w_down_t, w_1), (w_o_t, w_2))):
        loads.append(pltpu.make_async_copy(ref, full.at[me], local.at[3 + k]))
    loads.append(pltpu.make_async_copy(acts.at[place.x], x, local.at[6]))
    loads.append(pltpu.make_async_copy(cots.at[place.x], cot, local.at[7]))
    for load in loads:
        load.start()

    barrier = pltpu.get_barrier_semaphore()
    partners = [place.other(axis) for axis in "xyc"] + [place.along(hop)[0] for hop in range(1, count)]
    for device in partners:
        pl.semaphore_signal(barrier, inc=1, device_id=device, device_id_type=pl.DeviceIdType.MESH)

    rows = place_small(b_qv, b_up_t, out_bias, norm_gain, norm_bias, wide, place.x, lax.axis_index("dp"))
    rows = jnp.concatenate([*rows, jnp.zeros((16 - len(rows), wide), jnp.float32)])
    smalls[me] = rows.astype(jnp.bfloat16)
    pl.semaphore_wait(barrier, len(partners))

    gathers = [Gather(weights[part], part * GATHER_SEMS, wire, place) for part in range(4)]
    tiny = SmallGather(smalls, 4 * GATHER_SEMS, wire, place)
    base = 4 * GATHER_SEMS + SMALL_SEMS
    reduces = [
        Reduce(g_parts[part], *froms[6 * part : 6 * part + 6], base + part * REDUCE_SEMS, wire, place) for part in range(3)
    ]
    base += 3 * REDUCE_SEMS
    final = ReduceLast(g_parts[3], *froms[18:22], base, wire, place)
    base += LAST_SEMS
    out_base, gx_base, small_base = base, base + 8, base + 16
    tiles = x.shape[0] // TILE

    def forward_rows(ref, first, tile):
        part = ref.at[place.x, tile_rows(tile)]
        return wire.copy(part, part, first + tile, place.other("x"))

    for load in loads[:3]:
        load.wait()
    gathers[3].start()
    for copy in tiny.z_copies():
        copy.start()
    for load in loads[3:]:
        load.wait()
    for copy in tiny.z_copies():
        copy.wait_recv()
    tiny.step("y").start()
    gathers[3].after_start()
    for part in range(3):
        gathers[part].start()
    tiny.step("y").wait_recv()
    tiny.step("x").start()
    gathers[3].after_second()
    x_label = chain_ids[pl.ds(place.x, 1), :]
    label = x_label.astype(jnp.float32)
    marks[0:1, :] = label
    marks[1:2, :] = jnp.where(key_keep[pl.ds(place.x, 1), :] == 1, label, -2.0)
    marks[2:8, :] = jnp.broadcast_to((x_label >= 0).astype(jnp.float32), (6, label.shape[1]))
    marks_col[...] = marks[...].T
    tiny.step("x").wait_recv()
    tiny.step("c").start()
    gathers[3].after_third()
    gathers[0].after_start()

    tiny.step("c").wait_recv()
    total = jnp.zeros(smalls.shape[4:], jnp.float32)
    for px in range(2):
        for pz in range(count):
            for py in range(2):
                for pc in range(2):
                    total += smalls[px, pz, py, pc].astype(jnp.float32)
    vecs[...] = total[0:8, :]
    for half in range(2):
        for k in range(2):
            row = 8 + half * 2 + k
            b_up[half : half + 1, k * wide : (k + 1) * wide] = total[row : row + 1, :]
    gathers[3].finish()

    flat = [ref.reshape(2, wide, ref.shape[5]) for ref in weights]
    g_flat = [ref.reshape(2, wide, ref.shape[5]) for ref in g_parts]
    qkv_phase(x, flat[3], vecs, h1t, query, key, value)
    gathers[1].after_start()
    gathers[2].after_start()

    def up_second():
        gathers[0].after_second()

    def down_second():
        gathers[1].after_second()
        gathers[2].after_second()

    def up_third():
        gathers[0].after_third()

    attend_phase(query, key, value, marks, marks_col, bias, mixed, logs, ((0, up_second), (2, down_second), (5, up_third)))
    gathers[1].after_third()
    gathers[2].after_third()
    for part in range(3):
        gathers[part].finish()
    send_out = lambda tile: forward_rows(outs, out_base, tile).start()
    middle_phase(x, cot, marks_col, flat[0], flat[1], flat[2], vecs, b_up, mixed, h2t, glowt, glow2t, act, gpre, gmix,
                 dots, outs.at[place.x], gres, sums, sums_up, send_out)
    for part, (left, right) in enumerate(((h2t, gpre), (glowt, act), (glow2t, mixed))):
        weight_phase(left, right, g_flat[part])
        reduces[part].send(0)

    def back_step(step):
        def act_now():
            for reduce in reduces:
                reduce.take(step)
                reduce.send(step + 1)

        return act_now

    attend_back_phase(query, key, value, gmix, marks, marks_col, bias, logs, dots, gq_wide, gk, gv,
                      ((1, back_step(0)), (5, back_step(1)), (7, back_step(2))))
    round_phase(gq_wide, gq)
    send_gx = lambda tile: forward_rows(grads_x, gx_base, tile).start()
    input_phase(x, flat[3], vecs, gq, gk, gv, gres, sums, grads_x.at[place.x], send_gx)
    qkv_weight_phase(h1t, gq, gk, gv, g_flat[3], lambda half: final.send(0, half))
    small_tot[0:8, :] = sums[...]
    for half in range(2):
        for k in range(2):
            row = 8 + half * 2 + k
            small_tot[row : row + 1, :] = sums_up[half : half + 1, k * wide : (k + 1) * wide]
    small_tot[12:16, :] = jnp.zeros((4, wide), jnp.float32)

    def small_copy(number, axis):
        return wire.copy(small_tot, small_from.at[number], small_base + number, place.other(axis))

    def small_add(number, axis):
        small_copy(number, axis).wait()
        small_tot[...] += small_from[number]

    small_copy(0, "c").start()
    for chunk in range(2):
        final.take(0, chunk)
        final.send(1, chunk)
    small_add(0, "c")
    small_copy(1, "y").start()
    for part, ref in enumerate((g_up, g_down, g_out)):
        reduces[part].take(3)
        ref[...] = reduces[part].result()
    final.take(1, 0)
    final.send(2, 0)
    small_add(1, "y")
    small_copy(2, "x").start()
    final.take(1, 1)
    final.send(2, 1)
    small_add(2, "x")
    last = [wire.copy(small_tot, small_from.at[2 + hop], small_base + 2 + hop, place.along(hop)[0]) for hop in range(1, count)]
    for copy in last:
        copy.start()
    for chunk in range(2):
        final.take(2, chunk)
    final.send_last()
    for copy in last:
        copy.wait_recv()
    ordered = jnp.zeros(small_tot.shape, jnp.float32)
    for z in range(count):
        term = small_tot[...]
        for hop in range(1, count):
            term = jnp.where(lax.rem(place.z + count - hop, count) == z, small_from[2 + hop], term)
        ordered += term
    small_sum[...] = ordered
    mine = final.result()
    for c in range(3):
        g_qkv[c] = mine[:, c * quarter : (c + 1) * quarter]

    def land(tile, _):
        forward_rows(outs, out_base, tile).wait()
        forward_rows(grads_x, gx_base, tile).wait()
        return 0

    for gather in gathers:
        gather.drain()
    for copy in tiny.z_copies():
        copy.wait_send()
    for axis in "yxc":
        tiny.step(axis).wait_send()
    for reduce in (*reduces, final):
        reduce.drain()
    for copy in last:
        copy.wait_send()
    lax.fori_loop(0, tiles, land, 0)


def whole(operands, count):
    acts, w_up, w_qkv = operands[0], operands[4], operands[7]
    slots, width = acts.shape[1], acts.shape[2]
    rows, columns = w_up.shape
    quarter = w_qkv.shape[2]
    bf, f32 = jnp.bfloat16, jnp.float32
    V = pltpu.VMEM
    half = (2, slots, width // 2)
    any_space = pl.BlockSpec(memory_space=pl.ANY)
    sems = 4 * GATHER_SEMS + SMALL_SEMS + 3 * REDUCE_SEMS + LAST_SEMS + 16 + 8
    out_shape = [
        jax.ShapeDtypeStruct((2, slots, width), bf),
        jax.ShapeDtypeStruct((2, slots, width), bf),
        jax.ShapeDtypeStruct((rows, columns), f32),
        jax.ShapeDtypeStruct((rows, columns), f32),
        jax.ShapeDtypeStruct((rows, quarter), f32),
        jax.ShapeDtypeStruct((3, rows, quarter), f32),
        jax.ShapeDtypeStruct((16, width), f32),
    ]
    sizes = (columns, columns, quarter, 3 * quarter)
    fulls = [V((2, count, 2, 2, rows, size), bf) for size in sizes]
    scratch = [
        *fulls, V((2, count, 2, 2, 16, width), bf),
        V((slots, width), bf), V((slots, width), bf), V((8, width), f32), V((2, columns), f32),
        V((8, slots), f32), V((slots, 8), f32), V((8, width), f32), V((2, columns), f32),
        V((width, slots), bf), V(half, bf), V(half, bf), V(half, bf), V((TILE, slots), f32), V(half, bf),
        V((2, 4, slots), f32), V((width, slots), bf), V((width, slots), bf), V((width, slots), bf),
        V((2, slots, columns), bf), V((2, slots, columns), bf), V(half, bf), V((2, 4, slots), f32),
        V((slots, width), f32), V(half, f32), V(half, bf), V(half, bf), V(half, bf), *fulls,
    ]
    for size in sizes[:3]:
        scratch += [
            V((2, count, 2, rows, size), bf),
            V((count, 2, rows // 2, size), bf), V((2, count, rows // 2, size), bf),
            V((count, rows // 2, size), bf), V((count, rows // 2, size), bf),
            V((count - 1, rows, size), bf),
        ]
    scratch += [
        V((2, count, 2, rows, 3 * quarter), bf), V((2, count, rows, 3 * quarter), bf),
        V((2, count - 1, rows, 3 * quarter), bf), V((rows, 3 * quarter), bf),
        V((count + 2, 16, width), f32), V((16, width), f32),
        pltpu.SemaphoreType.DMA((8,)), pltpu.SemaphoreType.DMA((sems,)), pltpu.SemaphoreType.DMA((sems,)),
    ]
    return pl.pallas_call(
        whole_kernel,
        out_shape=out_shape,
        in_specs=[any_space] * 2 + [FULL] * 2 + [any_space] * 4 + [FULL] * 5,
        out_specs=[FULL] * 7,
        scratch_shapes=scratch,
        compiler_params=pltpu.CompilerParams(
            vmem_limit_bytes=67043328, collective_id=0, has_side_effects=True
        ),
    )(*operands)


def finish_kernel(out, grad_x, up, down, o_t, qkv, total, r_out, r_gx, r_qkv, r_o, r_up, r_down, r_qv, r_bup, r_bias, r_gain, r_shift):
    r_out[...] = out[...].astype(jnp.float32)
    r_gx[...] = grad_x[...].astype(jnp.float32)

    @pl.when(pl.program_id(0) == 0)
    def _():
        r_qkv[...] = qkv[...]
        r_o[...] = o_t[...]
        r_up[...] = up[...]
        r_down[...] = down[...]
        pick_small(total, lax.axis_index("mp"), lax.axis_index("dp"), r_qv, r_bup, r_bias, r_gain, r_shift)


def finish(parts, qv_shape, up_shape, pair_shape):
    out, grad_x = parts[0], parts[1]
    block = pl.BlockSpec((1, 512, out.shape[2]), lambda step: (step // 2, step % 2, 0))
    fixed = lambda shape: pl.BlockSpec(shape, lambda step: (0,) * len(shape))
    f32 = jnp.float32
    order = (5, 4, 2, 3)
    shapes = [parts[k].shape for k in order] + [qv_shape, up_shape, pair_shape, pair_shape, pair_shape]
    return pl.pallas_call(
        finish_kernel,
        grid=(2 * out.shape[1] // 512,),
        out_shape=[jax.ShapeDtypeStruct(out.shape, f32)] * 2 + [jax.ShapeDtypeStruct(shape, f32) for shape in shapes],
        in_specs=[block, block] + [fixed(part.shape) for part in parts[2:]],
        out_specs=[block, block] + [fixed(shape) for shape in shapes],
    )(*parts)


def product(left, right):
    return jnp.dot(left, right, preferred_element_type=jnp.float32)


def normalize(values, scale_row, shift_row):
    row_mean = jnp.mean(values, axis=-1, keepdims=True)
    centred = values - row_mean
    inverse = lax.rsqrt(jnp.mean(centred * centred, axis=-1, keepdims=True) + epsilon)
    scaled = centred * inverse
    return (scaled * scale_row + shift_row, scaled, inverse)


def normalize_back(grad_rows, scaled, inverse, scale_row):
    inner = grad_rows * scale_row
    return inverse * (
        inner
        - jnp.mean(inner, axis=-1, keepdims=True)
        - scaled * jnp.mean(inner * scaled, axis=-1, keepdims=True)
    )


def gelu_slope(values):
    normal_cdf = 0.5 * (1.0 + lax.erf(values * 0.7071067811865476))
    density = jnp.exp(-0.5 * values * values) * 0.3989422804014327
    return normal_cdf + values * density


def permitted(chain_rows, keep_rows):
    slot_count = chain_rows.shape[0]
    same_chain = chain_rows[:, None] == chain_rows[None, :]
    diagonal = lax.broadcasted_iota(jnp.int32, (slot_count, slot_count), 0) == lax.broadcasted_iota(
        jnp.int32, (slot_count, slot_count), 1
    )
    return same_chain & ((keep_rows[None, :] == 1) | diagonal)


def head_scores(query, key_rows, allowed, head_count, head_width):
    query_heads = query.reshape(-1, head_count, head_width)
    key_heads = key_rows.reshape(-1, head_count, head_width)
    scores = jnp.einsum(
        "qhd,khd->hqk", query_heads, key_heads, preferred_element_type=jnp.float32
    ) * (1.0 / math.sqrt(head_width))
    return jnp.where(allowed[None], scores, masked_value)


def forward(rows_in, chain_rows, keep_rows, weights, join=lambda a: a):
    qkv_full, out_full, up_full, down_full, bias_qv, bias_up, bias_out, gain_full, shift_full = (
        weights
    )
    head_count = bias_qv.shape[1]
    head_width = bias_qv.shape[2]
    row_count = rows_in.shape[0]
    bias_qv = bias_qv.astype(jnp.float32)
    bias_out = bias_out.astype(jnp.float32)
    gain_full = gain_full.astype(jnp.float32)
    shift_full = shift_full.astype(jnp.float32)
    allowed = permitted(chain_rows, keep_rows)
    normed_one, scaled_one, inverse_one = normalize(rows_in, gain_full[0], shift_full[0])
    hidden_one = normed_one.astype(jnp.bfloat16)
    query = (product(hidden_one, qkv_full[0]) + bias_qv[0].reshape(-1)).astype(jnp.bfloat16)
    key_rows = product(hidden_one, qkv_full[1]).astype(jnp.bfloat16)
    value_rows = (product(hidden_one, qkv_full[2]) + bias_qv[1].reshape(-1)).astype(jnp.bfloat16)
    scores = head_scores(query, key_rows, allowed, head_count, head_width)
    row_top = jnp.max(scores, axis=-1, keepdims=True)
    log_total = jnp.log(jnp.sum(jnp.exp(scores - row_top), axis=-1, keepdims=True)) + row_top
    probs_low = jnp.exp(scores - log_total).astype(jnp.bfloat16)
    mixed = jnp.einsum(
        "hqk,khd->qhd",
        probs_low,
        value_rows.reshape(row_count, head_count, head_width),
        preferred_element_type=jnp.float32,
    )
    mixed = mixed.reshape(row_count, -1).astype(jnp.bfloat16)
    partial_attn = product(mixed, out_full)
    resid = rows_in + join(partial_attn) + bias_out[0]
    normed_two, scaled_two, inverse_two = normalize(resid, gain_full[1], shift_full[1])
    hidden_two = normed_two.astype(jnp.bfloat16)
    pre = product(hidden_two, up_full) + bias_up.astype(jnp.float32).reshape(-1)
    act = jax.nn.gelu(pre, approximate=False).astype(jnp.bfloat16)
    partial_ffn = product(act, down_full)
    result = (
        resid + join(partial_ffn.astype(jnp.bfloat16)).astype(jnp.float32) + bias_out[1]
    )
    kept = (
        allowed,
        scaled_one,
        inverse_one,
        hidden_one,
        query,
        key_rows,
        value_rows,
        log_total,
        mixed,
        scaled_two,
        inverse_two,
        hidden_two,
        pre,
        act,
    )
    return (result, kept)


def backward(grad_out, result, kept, weights, join=lambda a: a):
    qkv_full, out_full, up_full, down_full, bias_qv, bias_up, bias_out, gain_full, shift_full = (
        weights
    )
    (
        allowed,
        scaled_one,
        inverse_one,
        hidden_one,
        query,
        key_rows,
        value_rows,
        log_total,
        mixed,
        scaled_two,
        inverse_two,
        hidden_two,
        pre,
        act,
    ) = kept
    head_count = bias_qv.shape[1]
    head_width = bias_qv.shape[2]
    row_count = grad_out.shape[0]
    gain_full = gain_full.astype(jnp.float32)
    grad_low = grad_out.astype(jnp.bfloat16)
    grad_down = product(act.T, grad_low)
    grad_pre = (product(grad_low, down_full.T) * gelu_slope(pre)).astype(jnp.bfloat16)
    grad_bup = jnp.sum(grad_pre, axis=0, dtype=jnp.float32).reshape(bias_up.shape)
    grad_up = product(hidden_two.T, grad_pre)
    partial_two = product(grad_pre, up_full.T)
    grad_two = join(partial_two.astype(jnp.bfloat16)).astype(jnp.float32)
    gain_two = jnp.sum(grad_two * scaled_two, axis=0)
    shift_two = jnp.sum(grad_two, axis=0)
    grad_resid = grad_out + normalize_back(grad_two, scaled_two, inverse_two, gain_full[1])
    resid_low = grad_resid.astype(jnp.bfloat16)
    grad_out_proj = product(mixed.T, resid_low)
    grad_mixed = (
        product(resid_low, out_full.T)
        .astype(jnp.bfloat16)
        .reshape(row_count, head_count, head_width)
    )
    scores = head_scores(query, key_rows, allowed, head_count, head_width)
    probs = jnp.exp(scores - log_total)
    probs_low = probs.astype(jnp.bfloat16)
    value_heads = value_rows.reshape(row_count, head_count, head_width)
    grad_value = jnp.einsum(
        "hqk,qhd->khd", probs_low, grad_mixed, preferred_element_type=jnp.float32
    ).astype(jnp.bfloat16)
    grad_probs = jnp.einsum(
        "qhd,khd->hqk", grad_mixed, value_heads, preferred_element_type=jnp.float32
    )
    grad_scores = (
        probs * (grad_probs - jnp.sum(grad_probs * probs, axis=-1, keepdims=True))
    ).astype(jnp.bfloat16)
    score_scale = 1.0 / math.sqrt(head_width)
    key_heads = key_rows.reshape(row_count, head_count, head_width)
    query_heads = query.reshape(row_count, head_count, head_width)
    grad_query = (
        jnp.einsum("hqk,khd->qhd", grad_scores, key_heads, preferred_element_type=jnp.float32)
        * score_scale
    ).astype(jnp.bfloat16)
    grad_key = (
        jnp.einsum("hqk,qhd->khd", grad_scores, query_heads, preferred_element_type=jnp.float32)
        * score_scale
    ).astype(jnp.bfloat16)
    stacked = jnp.stack(
        [
            grad_query.reshape(row_count, -1),
            grad_key.reshape(row_count, -1),
            grad_value.reshape(row_count, -1),
        ]
    )
    grad_qkv = jnp.einsum("rd,crk->cdk", hidden_one, stacked, preferred_element_type=jnp.float32)
    partial_one = jnp.einsum("crk,cdk->rd", stacked, qkv_full, preferred_element_type=jnp.float32)
    grad_one = join(partial_one.astype(jnp.bfloat16)).astype(jnp.float32)
    grad_bqv = jnp.stack(
        [
            jnp.sum(stacked[0], axis=0, dtype=jnp.float32),
            jnp.sum(stacked[2], axis=0, dtype=jnp.float32),
        ]
    ).reshape(2, head_count, head_width)
    gain_one = jnp.sum(grad_one * scaled_one, axis=0)
    shift_one = jnp.sum(grad_one, axis=0)
    grad_in = grad_resid + normalize_back(grad_one, scaled_one, inverse_one, gain_full[0])
    small_sums = jnp.stack(
        [
            jnp.sum(grad_resid, axis=0),
            jnp.sum(grad_out, axis=0),
            gain_one,
            gain_two,
            shift_one,
            shift_two,
        ]
    )
    local_grads = (
        grad_qkv,
        grad_out_proj,
        grad_up,
        grad_down,
        grad_bqv,
        grad_bup,
        small_sums[0:2],
        small_sums[2:4],
        small_sums[4:6],
    )
    return (result, grad_in, local_grads)


def body_generic(
    activations,
    cotangent,
    w_qkv,
    w_o,
    w_up,
    w_down,
    b_qv,
    b_up,
    out_bias,
    norm_gain,
    norm_bias,
    chain_ids,
    key_keep,
):
    batch_count = activations.shape[0]
    outputs = []
    input_grads = []
    running = None
    for batch_index in range(batch_count):
        weights = (
            lax.all_gather(w_qkv, "dp", axis=1, tiled=True),
            lax.all_gather(w_o, "dp", axis=1, tiled=True),
            lax.all_gather(w_up, "dp", axis=0, tiled=True),
            lax.all_gather(w_down, "dp", axis=1, tiled=True),
            lax.all_gather(b_qv, "dp", axis=2, tiled=True),
            lax.all_gather(b_up, "dp", axis=1, tiled=True),
            lax.all_gather(out_bias, "dp", axis=1, tiled=True),
            lax.all_gather(norm_gain, "dp", axis=1, tiled=True),
            lax.all_gather(norm_bias, "dp", axis=1, tiled=True),
        )
        result, kept = forward(
            activations[batch_index].astype(jnp.float32),
            chain_ids[batch_index],
            key_keep[batch_index],
            weights,
            lambda a: lax.psum(a, "mp"),
        )
        live_rows = (chain_ids[batch_index] >= 0).astype(jnp.float32)[:, None]
        output_rows, grad_in, local_grads = backward(
            cotangent[batch_index].astype(jnp.float32) * live_rows, result, kept, weights, lambda a: lax.psum(a, "mp")
        )
        outputs.append(output_rows)
        input_grads.append(grad_in)
        shares = (
            lax.psum_scatter(
                local_grads[0].astype(jnp.bfloat16), "dp", scatter_dimension=1, tiled=True
            ).astype(jnp.float32),
            lax.psum_scatter(
                local_grads[1].astype(jnp.bfloat16), "dp", scatter_dimension=1, tiled=True
            ).astype(jnp.float32),
            lax.psum_scatter(
                local_grads[2].astype(jnp.bfloat16), "dp", scatter_dimension=0, tiled=True
            ).astype(jnp.float32),
            lax.psum_scatter(
                local_grads[3].astype(jnp.bfloat16), "dp", scatter_dimension=1, tiled=True
            ).astype(jnp.float32),
            lax.psum_scatter(
                local_grads[4].astype(jnp.bfloat16), "dp", scatter_dimension=2, tiled=True
            ).astype(jnp.float32),
            lax.psum_scatter(
                local_grads[5].astype(jnp.bfloat16), "dp", scatter_dimension=1, tiled=True
            ).astype(jnp.float32),
            lax.psum_scatter(
                local_grads[6].astype(jnp.bfloat16), "dp", scatter_dimension=1, tiled=True
            ).astype(jnp.float32),
            lax.psum_scatter(
                local_grads[7].astype(jnp.bfloat16), "dp", scatter_dimension=1, tiled=True
            ).astype(jnp.float32),
            lax.psum_scatter(
                local_grads[8].astype(jnp.bfloat16), "dp", scatter_dimension=1, tiled=True
            ).astype(jnp.float32),
        )
        if running is None:
            running = tuple(shares)
        else:
            running = tuple(jax.tree.map(jnp.add, tuple(running), tuple(shares)))
    return (
        jnp.stack(outputs),
        jnp.stack(input_grads),
        running[0],
        running[1],
        running[2],
        running[3],
        running[4],
        running[5],
        running[6],
        running[7],
        running[8],
    )


def fits(mesh):
    return mesh.shape["mp"] == 2 and mesh.shape["dp"] == 16


def body_split(
    activations,
    cotangent,
    w_qkv,
    w_o,
    w_up,
    w_down,
    b_qv,
    b_up,
    out_bias,
    norm_gain,
    norm_bias,
    chain_ids,
    key_keep,
):
    parts = whole(
        (activations, cotangent, chain_ids, key_keep, w_up, w_down.T, w_o.T, w_qkv, b_qv, b_up.T, out_bias, norm_gain, norm_bias),
        lax.axis_size("dp") // 4,
    )
    out, grad_x, qkv, o_t, up, down_t, qv, bup_t, bias, gain, shift = finish(parts, b_qv.shape, b_up.shape[::-1], out_bias.shape)
    return (out, grad_x, qkv, o_t.T, up, down_t.T, qv, bup_t.T, bias, gain, shift)


def solution(mesh):
    placed = (
        P(None, "dp", None),
        P(None, "dp", None),
        P(None, "dp", "mp"),
        P("mp", "dp"),
        P("dp", "mp"),
        P("mp", "dp"),
        P(None, "mp", "dp"),
        P("mp", "dp"),
        P(None, "dp"),
        P(None, "dp"),
        P(None, "dp"),
        P(None, "dp"),
        P(None, "dp"),
    )
    body = body_split if fits(mesh) else body_generic
    return jax.shard_map(
        body,
        mesh=mesh,
        in_specs=placed,
        out_specs=(
            P(None, "dp", None),
            P(None, "dp", None),
            P(None, "dp", "mp"),
            P("mp", "dp"),
            P("dp", "mp"),
            P("mp", "dp"),
            P(None, "mp", "dp"),
            P("mp", "dp"),
            P(None, "dp"),
            P(None, "dp"),
            P(None, "dp"),
        ),
        check_vma=False,
    )
```

```python
import functools
import math

import jax
import jax.numpy as jnp
from jax import lax
from jax.experimental import pallas as pl
from jax.experimental.pallas import tpu as pltpu
from jax.sharding import PartitionSpec as P

epsilon = 1e-05
masked_value = -1e30
LOG2E = math.log2(math.e)
TILE = 256
AHEAD = 3
FULL = pl.BlockSpec(memory_space=pltpu.VMEM)

GAIN1, SHIFT1, GAIN2, SHIFT2, BQ, BV, BO1, BO2 = range(8)


def dot(left, right):
    return jnp.dot(left, right, preferred_element_type=jnp.float32)


def dot_last(left, right):
    return lax.dot_general(left, right, (((1,), (1,)), ((), ())), preferred_element_type=jnp.float32)


def dot_first(left, right):
    return lax.dot_general(left, right, (((0,), (0,)), ((), ())), preferred_element_type=jnp.float32)


def tile_rows(index):
    return pl.ds(pl.multiple_of(index * TILE, TILE), TILE)


def statistics(values):
    centred = values - jnp.mean(values, axis=-1, keepdims=True)
    inverse = lax.rsqrt(jnp.mean(centred * centred, axis=-1, keepdims=True) + epsilon)
    return centred * inverse, inverse


def norm_back(grad, scaled, inverse, gain):
    inner = grad * gain
    return inverse * (
        inner - jnp.mean(inner, axis=-1, keepdims=True) - scaled * jnp.mean(inner * scaled, axis=-1, keepdims=True)
    )


def add_row(ref, row, values):
    ref[row : row + 1, :] += jnp.sum(values, axis=0, keepdims=True)


def qkv_phase(x, w_mix, vecs, h1t, query_t, key, key_t, value, value_t):
    halves, quarter = key.shape[0], key.shape[2]
    heads = quarter // 64
    scale = 1.0 / math.sqrt(64)
    value_t[:, 64:, :] = jnp.ones((value_t.shape[0], value_t.shape[1] - 64, value_t.shape[2]), value_t.dtype)

    def step(tile, _):
        rows = tile_rows(tile)
        scaled, _ = statistics(x[rows, :].astype(jnp.float32))
        hidden = (scaled * vecs[GAIN1 : GAIN1 + 1, :] + vecs[SHIFT1 : SHIFT1 + 1, :]).astype(jnp.bfloat16)
        h1t[:, rows] = hidden.T
        for half in range(halves):
            cols = slice(half * quarter, (half + 1) * quarter)
            part = lambda c: dot(hidden, w_mix[half, :, c * quarter : (c + 1) * quarter])
            query = ((part(0) + vecs[BQ : BQ + 1, cols]).astype(jnp.bfloat16) * scale).astype(jnp.bfloat16)
            query_t[cols, rows] = query.T
            keys = part(1).astype(jnp.bfloat16)
            key[half, rows, :] = keys
            key_t[cols, rows] = keys.T
            values = (part(2) + vecs[BV : BV + 1, cols]).astype(jnp.bfloat16)
            value[half, rows, :] = values
            turned = values.T
            for head in range(heads):
                value_t[half * heads + head, 0:64, rows] = turned[head * 64 : (head + 1) * 64, :]
        return 0

    lax.fori_loop(0, x.shape[0] // TILE, step, 0)


def attend_phase(query_t, key, value_t, marks_row, marks_col, bias, mixed_t, inverse, expos, store, beside):
    halves, slots, quarter = key.shape
    heads = quarter // 64

    def tile_step(tile, _):
        lanes = tile_rows(tile)
        same = marks_col[:, 1:2] == marks_row[0:1, lanes]
        here = lax.broadcasted_iota(jnp.int32, (slots, TILE), 0)
        there = lax.broadcasted_iota(jnp.int32, (slots, TILE), 1) + tile * TILE
        bias[...] = jnp.where(same | (here == there), 0.0, masked_value)

        def half_step(half, _):
            for when, action in beside:
                pl.when(tile * halves + half == when)(action)

            @pl.when(tile > 0)
            def _():
                store(tile - 1, half).wait()

            lane = lax.broadcasted_iota(jnp.int32, (TILE, 128), 1)

            def scores_of(head, chunk):
                part = slice(chunk * TILE, (chunk + 1) * TILE)
                pair = head // 2
                keys = key[half, part, pair * 128 : (pair + 1) * 128]
                first = pl.multiple_of(half * quarter + pair * 128, 128)
                mine = (lane < 64) if head % 2 == 0 else (lane >= 64)
                return dot(jnp.where(mine, keys, jnp.zeros_like(keys)), query_t[pl.ds(first, 128), lanes]) + bias[part, :]

            chunks = slots // TILE
            scores = [scores_of(0, chunk) for chunk in range(chunks)]
            for head in range(heads):
                top = functools.reduce(jnp.maximum, [jnp.max(part, axis=0, keepdims=True) for part in scores])
                summed, following = 0.0, []
                for chunk in range(chunks):
                    part = slice(chunk * TILE, (chunk + 1) * TILE)
                    expo = jnp.exp2(((scores[chunk] - top) * LOG2E).astype(jnp.bfloat16))
                    expos[half, head, part, :] = expo
                    if head + 1 < heads:
                        following.append(scores_of(head + 1, chunk))
                    summed = summed + dot(value_t[half * heads + head, :, part], expo)
                share = 1.0 / summed[64:65, :]
                inverse[half * heads + head, 0:1, lanes] = share
                at = pl.multiple_of(half * quarter + head * 64, 64)
                mixed_t[pl.ds(at, 64), lanes] = (summed[0:64, :] * share).astype(jnp.bfloat16)
                scores = following
            store(tile, half).start()
            return 0

        lax.fori_loop(0, halves, half_step, 0)
        return 0

    lax.fori_loop(0, slots // TILE, tile_step, 0)
    for half in range(halves):
        store(slots // TILE - 1, half).wait()


def middle_phase(x, cot, live_col, w_up, w_down, w_o, vecs, b_up, mixed_t, inverse_sum, h2t, glowt, glow2t, act, gpre, gmix_t, dots, out, gres, sums, sums_up, send):
    halves, quarter, hidden_half = w_up.shape[0], w_o.shape[2], w_up.shape[2]
    heads = quarter // 64

    def step(tile, _):
        rows = tile_rows(tile)
        attn = sum(dot_last(mixed_t[half * quarter : (half + 1) * quarter, rows].T, w_o[half]) for half in range(halves))
        resid = x[rows, :].astype(jnp.float32) + attn + vecs[BO1 : BO1 + 1, :]
        scaled, inverse = statistics(resid)
        hidden = (scaled * vecs[GAIN2 : GAIN2 + 1, :] + vecs[SHIFT2 : SHIFT2 + 1, :]).astype(jnp.bfloat16)
        h2t[:, rows] = hidden.T
        grad_out = cot[rows, :].astype(jnp.float32) * live_col[rows, 2:3]
        grad_low = grad_out.astype(jnp.bfloat16)
        glowt[:, rows] = grad_low.T
        ffn = jnp.zeros(resid.shape, jnp.float32)
        grad_two = jnp.zeros(resid.shape, jnp.float32)
        for half in range(halves):
            pre = dot(hidden, w_up[half]) + b_up[half : half + 1, :]
            cdf = 0.5 * (1.0 + lax.erf(pre * 0.7071067811865476))
            slope = cdf + pre * (jnp.exp(-0.5 * pre * pre) * 0.3989422804014327)
            active = (pre * cdf).astype(jnp.bfloat16)
            act[half, rows, :] = active
            ffn += dot_last(active, w_down[half])
            grad_pre = (dot(grad_low, w_down[half]) * slope).astype(jnp.bfloat16)
            gpre[half, rows, :] = grad_pre
            grad_two += dot_last(grad_pre, w_up[half])
            add_row(sums_up, half, grad_pre.astype(jnp.float32))
        out[rows, :] = (resid + ffn + vecs[BO2 : BO2 + 1, :]).astype(out.dtype)
        add_row(sums, GAIN2, grad_two * scaled)
        add_row(sums, SHIFT2, grad_two)
        grad_resid = grad_out + norm_back(grad_two, scaled, inverse, vecs[GAIN2 : GAIN2 + 1, :])
        add_row(sums, BO1, grad_resid)
        add_row(sums, BO2, grad_out)
        gres[rows, :] = grad_resid
        low = grad_resid.astype(jnp.bfloat16)
        glow2t[:, rows] = low.T
        for half in range(halves):
            grads = dot(low, w_o[half]).T
            for head in range(heads):
                at = half * quarter + head * 64
                share = inverse_sum[half * heads + head, 0:1, rows]
                scaled_grads = grads[head * 64 : (head + 1) * 64, :] * share
                gmix_t[at : at + 64, rows] = scaled_grads.astype(jnp.bfloat16)
                both = scaled_grads * mixed_t[at : at + 64, rows].astype(jnp.float32)
                dots[half * heads + head, 0:1, rows] = jnp.sum(both, axis=0, keepdims=True)
        send(tile)
        return 0

    sums[...] = jnp.zeros_like(sums)
    sums_up[...] = jnp.zeros_like(sums_up)
    lax.fori_loop(0, x.shape[0] // TILE, step, 0)


def weight_phase(left_t, right, grads, then):
    halves, _, columns = right.shape
    chunk = min(columns, 512)

    def step(half, _):
        for start in range(0, columns, chunk):
            cols = slice(start, start + chunk)
            grads[half, :, cols] = dot(left_t[...], right[half, :, cols]).astype(jnp.bfloat16)
        then(half)
        return 0

    lax.fori_loop(0, halves, step, 0)


def turned_weight_phase(left_t, right_t, grads, then):
    halves, _, quarter = grads.shape

    def step(half, _):
        grads[half] = dot_last(left_t[...], right_t[tile_rows(half), :]).astype(jnp.bfloat16)
        then(half)
        return 0

    lax.fori_loop(0, halves, step, 0)


def attend_back_phase(query_t, key_t, value, gmix_t, dots, expos, load, grad_query, wide_key, wide_value, beside):
    halves, slots, quarter = value.shape
    heads = quarter // 64
    wide_key[...] = jnp.zeros_like(wide_key)
    wide_value[...] = jnp.zeros_like(wide_value)
    scale = 1.0 / math.sqrt(64)

    def tile_step(tile, _):
        lanes = tile_rows(tile)

        def half_step(half, _):
            for when, action in beside:
                pl.when(tile * halves + half == when)(action)
            load(tile, half).wait()
            lane = lax.broadcasted_iota(jnp.int32, (TILE, 128), 1)
            chunks = slots // TILE

            def grad_probs_of(step):
                head, chunk = step // chunks, step % chunks
                pair = head // 2
                values = value[half, chunk * TILE : (chunk + 1) * TILE, pair * 128 : (pair + 1) * 128]
                first = pl.multiple_of(half * quarter + pair * 128, 128)
                mine = (lane < 64) if head % 2 == 0 else (lane >= 64)
                return dot(jnp.where(mine, values, jnp.zeros_like(values)), gmix_t[pl.ds(first, 128), lanes])

            ahead = [grad_probs_of(step) for step in range(AHEAD)]
            for step in range(heads * chunks):
                head, chunk = step // chunks, step % chunks
                part = slice(chunk * TILE, (chunk + 1) * TILE)
                at = pl.ds(pl.multiple_of(half * quarter + head * 64, 64), 64)
                if step + AHEAD < heads * chunks:
                    ahead.append(grad_probs_of(step + AHEAD))
                expo = expos[half, head, part, :]
                grad_scores = expo * (ahead[step] - dots[half * heads + head, 0:1, lanes]).astype(jnp.bfloat16)
                wide_value[at, part] += dot_last(gmix_t[at, lanes], expo)
                wide_key[at, part] += dot_last(query_t[at, lanes], grad_scores)
                term = dot(key_t[at, part], grad_scores)
                total = term if chunk == 0 else total + term
                if chunk == chunks - 1:
                    grad_query[at, lanes] = (total * scale).astype(jnp.bfloat16)

            @pl.when(tile + 1 < slots // TILE)
            def _():
                load(tile + 1, half).start()

            return 0

        lax.fori_loop(0, halves, half_step, 0)
        return 0

    lax.fori_loop(0, slots // TILE, tile_step, 0)


def round_phase(wide, low):
    def step(tile, _):
        rows = tile_rows(tile)
        low[rows, :] = wide[rows, :].astype(jnp.bfloat16)
        return 0

    lax.fori_loop(0, low.shape[0] // TILE, step, 0)


def qkv_weight_phase(h1t, grad_query, grad_key, grad_value, grads, then):
    halves, quarter = grads.shape[0], grads.shape[2] // 3

    def step(half, _):
        for c, ref in enumerate((grad_query, grad_key, grad_value)):
            grads[half, :, c * quarter : (c + 1) * quarter] = dot_last(h1t[...], ref[tile_rows(half), :]).astype(jnp.bfloat16)
        then(half)
        return 0

    lax.fori_loop(0, halves, step, 0)


def input_phase(x, w_mix, vecs, grad_query, grad_key, grad_value, gres, sums, grad_x, free, send):
    slots, halves, quarter = x.shape[0], w_mix.shape[0], w_mix.shape[2] // 3
    ones = jnp.ones((8, slots), jnp.bfloat16)
    for row, ref in ((BQ, grad_query), (BV, grad_value)):
        sums[row : row + 1, :] = dot_last(ones, ref[...])[0:1, :]

    def step(tile, _):
        rows = tile_rows(tile)
        scaled, inverse = statistics(x[rows, :].astype(jnp.float32))
        turned = jnp.zeros((x.shape[1], TILE), jnp.float32)
        for half in range(halves):
            for c, ref in enumerate((grad_query, grad_key, grad_value)):
                part = ref[half * quarter : (half + 1) * quarter, rows]
                turned += dot(w_mix[half, :, c * quarter : (c + 1) * quarter], part)
        grad_one = turned.T
        add_row(sums, GAIN1, grad_one * scaled)
        add_row(sums, SHIFT1, grad_one)
        free(tile)
        grad_x[rows, :] = (gres[rows, :] + norm_back(grad_one, scaled, inverse, vecs[GAIN1 : GAIN1 + 1, :])).astype(grad_x.dtype)
        send(tile)
        return 0

    lax.fori_loop(0, slots // TILE, step, 0)


class Place:
    def __init__(self, depth_z):
        at = lax.axis_index("dp")
        self.x, self.z, self.y, self.c = lax.axis_index("mp"), at // 4, (at // 2) % 2, at % 2
        self.count = depth_z

    def other(self, axis):
        x, z, y, c = self.x, self.z, self.y, self.c
        x, y, c = (1 - x if axis == "x" else x), (1 - y if axis == "y" else y), (1 - c if axis == "c" else c)
        return {"dp": z * 4 + y * 2 + c, "mp": x}

    def along(self, hop):
        z = lax.rem(self.z + hop, self.count)
        return {"dp": z * 4 + self.y * 2 + self.c, "mp": self.x}, z


class Wire:
    def __init__(self, send, recv):
        self.send_sems, self.recv_sems = send, recv

    def copy(self, src, dst, number, device):
        return pltpu.make_async_remote_copy(
            src_ref=src,
            dst_ref=dst,
            send_sem=self.send_sems.at[number],
            recv_sem=self.recv_sems.at[number],
            device_id=device,
            device_id_type=pl.DeviceIdType.MESH,
        )


GATHER_SEMS = 15
REDUCE_SEMS = 11
SMALL_SEMS = 7


class Gather:
    def __init__(self, ref, base, wire, place):
        self.ref, self.base, self.wire, self.place = ref, base, wire, place
        self.top = pl.ds(0, ref.shape[4] // 2)
        self.low = pl.ds(ref.shape[4] // 2, ref.shape[4] // 2)

    def own(self, axis, src, number):
        return self.wire.copy(src, src, self.base + number, self.place.other(axis))

    def z_copies(self):
        p, ref = self.place, self.ref
        mine = ref.at[p.x, p.z, p.y, p.c]
        for hop in range(1, p.count):
            device, _ = p.along(hop)
            yield self.wire.copy(mine, mine, self.base + hop - 1, device)

    def second(self):
        p, ref = self.place, self.ref
        return (
            self.own("y", ref.at[p.x, :, p.y, p.c, self.top], 3),
            self.own("x", ref.at[p.x, :, p.y, p.c, self.low], 4),
        )

    def third(self):
        p, ref = self.place, self.ref
        return (
            self.own("x", ref.at[p.x, :, :, p.c, self.top], 5),
            self.own("y", ref.at[:, :, p.y, p.c, self.low], 6),
        )

    def core(self, step):
        p, ref = self.place, self.ref
        if step == 1:
            return (self.own("c", ref.at[p.x, :, p.y, p.c], 7),)
        if step == 2:
            return (
                self.own("c", ref.at[p.x, :, 1 - p.y, p.c, self.top], 8),
                self.own("c", ref.at[1 - p.x, :, p.y, p.c, self.low], 9),
            )
        return (
            self.own("c", ref.at[1 - p.x, :, :, p.c, self.top], 10),
            self.own("c", ref.at[:, :, 1 - p.y, p.c, self.low], 11),
        )

    def start(self):
        for copy in self.z_copies():
            copy.start()

    def after_start(self):
        for copy in self.z_copies():
            copy.wait_recv()
        for copy in self.second() + self.core(1):
            copy.start()

    def after_second(self):
        for copy in self.second():
            copy.wait_recv()
        for copy in self.third() + self.core(2):
            copy.start()

    def after_third(self):
        for copy in self.third():
            copy.wait_recv()
        for copy in self.core(3):
            copy.start()

    def finish(self):
        for step in (1, 2, 3):
            for copy in self.core(step):
                copy.wait_recv()

    def drain(self):
        for copy in self.z_copies():
            copy.wait_send()
        for copy in self.second() + self.third() + self.core(1) + self.core(2) + self.core(3):
            copy.wait_send()


class SmallSum:
    def __init__(self, held, arrived, base, wire, place):
        self.held, self.arrived, self.base, self.wire, self.place = held, arrived, base, wire, place

    def z_copies(self):
        p = self.place
        return [
            self.wire.copy(self.held.at[0], self.arrived.at[hop - 1], self.base + hop - 1, p.along(hop)[0])
            for hop in range(1, p.count)
        ]

    def step(self, axis):
        p, k = self.place, {"y": 1, "x": 2, "c": 3}[axis]
        number = p.count - 2 + k
        return self.wire.copy(self.held.at[k], self.arrived.at[number], self.base + number, p.other(axis))

    def add_z(self):
        total = self.held[0]
        for hop in range(1, self.place.count):
            total += self.arrived[hop - 1]
        self.held[1] = total

    def add(self, axis):
        k = {"y": 1, "x": 2, "c": 3}[axis]
        self.held[k + 1] = self.held[k] + self.arrived[self.place.count - 2 + k]


class Reduce:
    def __init__(self, grads, from_core, from_y, from_z, from_x, base, wire, place):
        self.grads, self.base, self.wire, self.place = grads, base, wire, place
        self.from_core, self.from_y, self.from_z, self.from_x = from_core, from_y, from_z, from_x

    def copies(self, step, chunk):
        p, g, w, base = self.place, self.grads, self.wire, self.base + 5 * chunk
        if step == 0:
            return [w.copy(g.at[chunk, :, :, 1 - p.c], self.from_core.at[chunk], base, p.other("c"))]
        if step == 1:
            return [w.copy(g.at[chunk, :, 1 - p.y, p.c], self.from_y.at[chunk], base + 1, p.other("y"))]
        out = []
        for hop in range(1, p.count):
            device, z = p.along(hop)
            out.append(w.copy(g.at[chunk, z, p.y, p.c], self.from_z.at[chunk, hop - 1], base + 1 + hop, device))
        return out

    def send(self, step, chunk):
        for copy in self.copies(step, chunk):
            copy.start()

    def take(self, step, chunk):
        p, g = self.place, self.grads
        for copy in self.copies(step, chunk):
            copy.wait_recv()

        def add(z, _):
            if step == 0:
                for y in range(2):
                    g[chunk, z, y, p.c] += self.from_core[chunk, z, y]
            else:
                g[chunk, z, p.y, p.c] += self.from_y[chunk, z]
            return 0

        if step < 2:
            lax.fori_loop(0, p.count, add, 0)

    def total(self, chunk):
        p = self.place
        total = self.grads[chunk, p.z, p.y, p.c].astype(jnp.float32)
        for hop in range(1, p.count):
            total += self.from_z[chunk, hop - 1].astype(jnp.float32)
        return total

    def last(self):
        p = self.place
        mine = self.grads.at[1 - p.x, p.z, p.y, p.c]
        return self.wire.copy(mine, self.from_x, self.base + 10, p.other("x"))

    def send_last(self):
        p = self.place
        self.grads[1 - p.x, p.z, p.y, p.c] = self.total(1 - p.x).astype(jnp.bfloat16)
        self.last().start()

    def result(self):
        total = self.total(self.place.x)
        self.last().wait()
        return total + self.from_x[...].astype(jnp.float32)

    def drain(self):
        for chunk in range(2):
            for step in range(3):
                for copy in self.copies(step, chunk):
                    copy.wait_send()


def lane_is(rows, lanes, test):
    row = lax.broadcasted_iota(jnp.int32, (rows, lanes), 0)
    lane = lax.broadcasted_iota(jnp.int32, (rows, lanes), 1)
    return jnp.where(test(row, lane), 1.0, 0.0)


def place_small(b_qv, b_up_t, out_bias, norm_gain, norm_bias, width, own, at):
    heads, hd = b_qv.shape[1], b_qv.shape[2]
    span = out_bias.shape[1]
    groups = width // 64
    first = jnp.where(own == 0, 1.0, 0.0)
    wide = lane_is(span, width, lambda row, lane: lane == at * span + row).astype(jnp.bfloat16)
    narrow = lane_is(hd, width, lambda row, lane: lane % 64 == at * hd + row).astype(jnp.bfloat16)
    gain, shift, bias = [dot(ref[...], wide) * first for ref in (norm_gain, norm_bias, out_bias)]
    spot = lane_is(heads, width, lambda row, lane: lane // 64 == own * heads + row)
    qv = [jnp.sum(dot(b_qv[k], narrow) * spot, axis=0, keepdims=True) for k in range(2)]
    ups = dot_first(b_up_t[...], narrow) * lane_is(b_up_t.shape[1], width, lambda row, lane: lane // 64 == row % groups)
    ups = [jnp.sum(ups[k * groups : (k + 1) * groups], axis=0, keepdims=True) for k in range(2)]
    ups = [row * scale for scale in (first, 1.0 - first) for row in ups]
    rows = [gain[0:1], shift[0:1], gain[1:2], shift[1:2], *qv, bias[0:1], bias[1:2], *ups]
    return rows


def exact(left, right):
    return lax.dot_general(
        left, right, (((1,), (1,)), ((), ())), precision=lax.Precision.HIGHEST, preferred_element_type=jnp.float32
    )


def pick_small(total, own, at, s_qv, s_up, s_bias, s_gain, s_shift):
    width = total.shape[1]
    heads, hd = s_qv.shape[1], s_qv.shape[2]
    span, groups = s_bias.shape[1], width // 64
    wide = lane_is(span, width, lambda row, lane: lane == at * span + row)
    narrow = lane_is(hd, width, lambda row, lane: lane % 64 == at * hd + row)
    vectors = exact(total[0:8, :], wide)
    for ref, (one, two) in ((s_gain, (GAIN1, GAIN2)), (s_shift, (SHIFT1, SHIFT2)), (s_bias, (BO1, BO2))):
        ref[0:1, :] = vectors[one : one + 1, :]
        ref[1:2, :] = vectors[two : two + 1, :]
    spot = lane_is(heads, width, lambda row, lane: lane // 64 == own * heads + row)
    for k in range(2):
        s_qv[k] = exact(total[BQ + k : BQ + k + 1, :] * spot, narrow)
    mine = jnp.where(own == 0, total[8:10, :], total[10:12, :])
    rows = [jnp.broadcast_to(mine[k : k + 1, :], (groups, width)) for k in range(2)]
    spot = lane_is(2 * groups, width, lambda row, lane: lane // 64 == row % groups)
    s_up[...] = exact(narrow, jnp.concatenate(rows) * spot)


def whole_kernel(
    acts, cots, chain_ids, key_keep, w_up, w_down_t, w_o_t, w_qkv, b_qv, b_up_t, out_bias, norm_gain, norm_bias,
    outs, grads_x, g_up, g_down, g_out, g_qkv, small_sum, kept,
    w_0, w_1, w_2, w_3, smalls, smalls_from, x, cot, vecs, b_up, marks, marks_col, sums, sums_up,
    h1t, query_t, key, key_t, value, value_t, bias, mixed_t, inverse_sum, expos, h2t, glowt, glow2t, act, gpre,
    gmix_t, dots, gres, wide_key, wide_value, stage, *rest,
):
    weights = (w_0, w_1, w_2, w_3)
    gq, gk, gv = [act.at[k // 2, pl.ds(k % 2 * vecs.shape[1], vecs.shape[1])] for k in range(3)]
    g_parts, rest = rest[:4], rest[4:]
    froms, rest = rest[:16], rest[16:]
    small_from, small_tot, local, send, recv = rest
    count, wide = w_0.shape[1], vecs.shape[1]
    place = Place(count)
    wire = Wire(send, recv)
    me = (place.x, place.z, place.y, place.c)
    quarter = w_qkv.shape[2]
    loads = [
        pltpu.make_async_copy(w_qkv.at[c], w_3.at[(*me, slice(None), pl.ds(c * quarter, quarter))], local.at[c])
        for c in range(3)
    ]
    for k, (ref, full) in enumerate(((w_up, w_0), (w_down_t, w_1), (w_o_t, w_2))):
        loads.append(pltpu.make_async_copy(ref, full.at[me], local.at[3 + k]))
    loads.append(pltpu.make_async_copy(acts.at[place.x], x, local.at[6]))
    loads.append(pltpu.make_async_copy(cots.at[place.x], cot, local.at[7]))
    for load in loads:
        load.start()

    barrier = pltpu.get_barrier_semaphore()
    partners = [place.other(axis) for axis in "xyc"] + [place.along(hop)[0] for hop in range(1, count)]
    for device in partners:
        pl.semaphore_signal(barrier, inc=1, device_id=device, device_id_type=pl.DeviceIdType.MESH)

    rows = place_small(b_qv, b_up_t, out_bias, norm_gain, norm_bias, wide, place.x, lax.axis_index("dp"))
    rows = jnp.concatenate([*rows, jnp.zeros((16 - len(rows), wide), jnp.float32)])
    smalls[0] = rows.astype(jnp.bfloat16)
    pl.semaphore_wait(barrier, len(partners))

    gathers = [Gather(weights[part], part * GATHER_SEMS, wire, place) for part in range(4)]
    tiny = SmallSum(smalls, smalls_from, 4 * GATHER_SEMS, wire, place)
    base = 4 * GATHER_SEMS + SMALL_SEMS
    reduces = [
        Reduce(g_parts[part], *froms[4 * part : 4 * part + 4], base + part * REDUCE_SEMS, wire, place) for part in range(4)
    ]
    final = reduces[3]
    base += 4 * REDUCE_SEMS
    out_base, gx_base, small_base = base, base + 8, base + 16
    tiles = x.shape[0] // TILE

    def forward_rows(ref, first, tile):
        part = ref.at[place.x, tile_rows(tile)]
        return wire.copy(stage.at[tile_rows(tile)], part, first + tile, place.other("x"))

    def keep_rows(ref, first, tile):
        return pltpu.make_async_copy(stage.at[tile_rows(tile)], ref.at[place.x, tile_rows(tile)], local.at[first + tile])

    def send_out(tile):
        forward_rows(outs, out_base, tile).start()
        keep_rows(outs, 12, tile).start()

    def free_stage(tile):
        forward_rows(outs, out_base, tile).wait_send()
        keep_rows(outs, 12, tile).wait()

    def send_gx(tile):
        forward_rows(grads_x, gx_base, tile).start()
        keep_rows(grads_x, 16, tile).start()

    for load in loads[:3]:
        load.wait()
    for copy in tiny.z_copies():
        copy.start()
    gathers[3].start()
    for load in loads[3:]:
        load.wait()
    for copy in tiny.z_copies():
        copy.wait_recv()
    tiny.add_z()
    tiny.step("y").start()
    gathers[3].after_start()
    for part in range(3):
        gathers[part].start()
    tiny.step("y").wait_recv()
    tiny.add("y")
    tiny.step("x").start()
    gathers[3].after_second()
    x_label = chain_ids[pl.ds(place.x, 1), :]
    label = x_label.astype(jnp.float32)
    marks[0:1, :] = label
    marks[1:2, :] = jnp.where(key_keep[pl.ds(place.x, 1), :] == 1, label, -2.0)
    marks[2:8, :] = jnp.broadcast_to((x_label >= 0).astype(jnp.float32), (6, label.shape[1]))
    marks_col[...] = marks[...].T
    tiny.step("x").wait_recv()
    tiny.add("x")
    tiny.step("c").start()
    gathers[3].after_third()
    gathers[0].after_start()

    tiny.step("c").wait_recv()
    tiny.add("c")
    total = smalls[4].astype(jnp.float32)
    vecs[...] = total[0:8, :]
    for half in range(2):
        for k in range(2):
            row = 8 + half * 2 + k
            b_up[half : half + 1, k * wide : (k + 1) * wide] = total[row : row + 1, :]
    gathers[3].finish()

    keep = lambda tile, half: pltpu.make_async_copy(expos.at[half], kept.at[tile, half], local.at[8 + half])
    fetch = lambda tile, half: pltpu.make_async_copy(kept.at[tile, half], expos.at[half], local.at[10 + half])
    flat = [ref.reshape(2, wide, ref.shape[5]) for ref in weights]
    g_flat = [ref.reshape(2, wide, ref.shape[5]) for ref in g_parts]
    qkv_phase(x, flat[3], vecs, h1t, query_t, key, key_t, value, value_t)
    gathers[1].after_start()
    gathers[2].after_start()

    def up_second():
        gathers[0].after_second()

    def down_second():
        gathers[1].after_second()
        gathers[2].after_second()

    def up_third():
        gathers[0].after_third()

    attend_phase(query_t, key, value_t, marks, marks_col, bias, mixed_t, inverse_sum, expos, keep, ((0, up_second), (2, down_second), (5, up_third)))
    gathers[1].after_third()
    gathers[2].after_third()
    for part in range(3):
        gathers[part].finish()
    middle_phase(x, cot, marks_col, flat[0], flat[1], flat[2], vecs, b_up, mixed_t, inverse_sum, h2t, glowt, glow2t, act, gpre,
                 gmix_t, dots, stage, gres, sums, sums_up, send_out)
    for half in range(2):
        fetch(0, half).start()
    def step_on(part, step, *chunks):
        for chunk in chunks:
            reduces[part].take(step, chunk)
            reduces[part].send(step + 1, chunk)

    weight_phase(h2t, gpre, g_flat[0], lambda half: reduces[0].send(0, half))
    weight_phase(glowt, act, g_flat[1], lambda half: reduces[1].send(0, half))
    step_on(0, 0, 0, 1)
    turned_weight_phase(glow2t, mixed_t, g_flat[2], lambda half: reduces[2].send(0, half))
    step_on(1, 0, 0, 1)
    attend_back_phase(query_t, key_t, value, gmix_t, dots, expos, fetch, gq, wide_key, wide_value, (
        (0, lambda: step_on(2, 0, 0, 1)), (3, lambda: step_on(0, 1, 0)), (6, lambda: step_on(0, 1, 1)),
    ))
    round_phase(wide_key, gk)
    round_phase(wide_value, gv)
    qkv_weight_phase(h1t, gq, gk, gv, g_flat[3], lambda half: final.send(0, half))
    step_on(1, 1, 0)
    step_on(3, 0, 0, 1)
    input_phase(x, flat[3], vecs, gq, gk, gv, gres, sums, stage, free_stage, send_gx)
    small_tot[0:8, :] = sums[...]
    for half in range(2):
        for k in range(2):
            row = 8 + half * 2 + k
            small_tot[row : row + 1, :] = sums_up[half : half + 1, k * wide : (k + 1) * wide]
    small_tot[12:16, :] = jnp.zeros((4, wide), jnp.float32)

    def small_copy(number, axis):
        return wire.copy(small_tot, small_from.at[number], small_base + number, place.other(axis))

    def small_add(number, axis):
        small_copy(number, axis).wait()
        small_tot[...] += small_from[number]

    small_copy(0, "c").start()
    step_on(1, 1, 1)
    small_add(0, "c")
    small_copy(1, "y").start()
    for chunk in range(2):
        reduces[0].take(2, chunk)
    reduces[0].send_last()
    step_on(2, 1, 0, 1)
    step_on(3, 1, 0, 1)
    small_add(1, "y")
    last = [wire.copy(small_tot, small_from.at[2 + hop], small_base + 2 + hop, place.along(hop)[0]) for hop in range(1, count)]
    for copy in last:
        copy.start()
    for part in range(1, 4):
        for chunk in range(2):
            reduces[part].take(2, chunk)
        reduces[part].send_last()
    for copy in last:
        copy.wait()
    ordered = jnp.zeros(small_tot.shape, jnp.float32)
    for z in range(count):
        term = small_tot[...]
        for hop in range(1, count):
            term = jnp.where(lax.rem(place.z + count - hop, count) == z, small_from[2 + hop], term)
        ordered += term
    small_tot[...] = ordered
    small_copy(2, "x").start()
    for part, ref in enumerate((g_up, g_down, g_out)):
        ref[...] = reduces[part].result()
    small_add(2, "x")
    small_sum[...] = small_tot[...]
    mine = final.result()
    for c in range(3):
        g_qkv[c] = mine[:, c * quarter : (c + 1) * quarter]

    def land(tile, _):
        forward_rows(outs, out_base, tile).wait_recv()
        forward_rows(grads_x, gx_base, tile).wait()
        keep_rows(grads_x, 16, tile).wait()
        return 0

    for gather in gathers:
        gather.drain()
    for copy in tiny.z_copies():
        copy.wait_send()
    for axis in "yxc":
        tiny.step(axis).wait_send()
    for reduce in reduces:
        reduce.drain()
    lax.fori_loop(0, tiles, land, 0)


def whole(operands, count):
    acts, w_up, w_qkv = operands[0], operands[4], operands[7]
    slots, width = acts.shape[1], acts.shape[2]
    rows, columns = w_up.shape
    quarter = w_qkv.shape[2]
    bf, f32 = jnp.bfloat16, jnp.float32
    V = pltpu.VMEM
    half = (2, slots, width // 2)
    turned = V((width, slots), bf)
    any_space = pl.BlockSpec(memory_space=pl.ANY)
    sems = 4 * GATHER_SEMS + SMALL_SEMS + 4 * REDUCE_SEMS + 16 + 8
    out_shape = [
        jax.ShapeDtypeStruct((2, slots, width), bf),
        jax.ShapeDtypeStruct((2, slots, width), bf),
        jax.ShapeDtypeStruct((rows, columns), f32),
        jax.ShapeDtypeStruct((rows, columns), f32),
        jax.ShapeDtypeStruct((rows, quarter), f32),
        jax.ShapeDtypeStruct((3, rows, quarter), f32),
        jax.ShapeDtypeStruct((16, width), f32),
        jax.ShapeDtypeStruct((slots // TILE, 2, width // 128, slots, TILE), bf),
    ]
    sizes = (columns, columns, quarter, 3 * quarter)
    fulls = [V((2, count, 2, 2, rows, size), bf) for size in sizes]
    scratch = [
        *fulls, V((5, 16, width), bf), V((count + 2, 16, width), bf),
        V((slots, width), bf), V((slots, width), bf), V((8, width), f32), V((2, columns), f32),
        V((8, slots), f32), V((slots, 8), f32), V((8, width), f32), V((2, columns), f32),
        turned, turned, V(half, bf), turned, V(half, bf), V((width // 64, 80, slots), bf), V((slots, TILE), f32),
        turned, V((width // 64, 1, slots), f32), V((2, width // 128, slots, TILE), bf), turned, turned, turned,
        V((2, slots, columns), bf), V((2, slots, columns), bf), turned, V((width // 64, 1, slots), f32),
        V((slots, width), f32), V((width, slots), f32), V((width, slots), f32), V((slots, width), bf), *fulls,
    ]
    for size in sizes:
        scratch += [
            V((2, count, 2, rows, size), bf), V((2, count, rows, size), bf),
            V((2, count - 1, rows, size), bf), V((rows, size), bf),
        ]
    scratch += [
        V((count + 2, 16, width), f32), V((16, width), f32),
        pltpu.SemaphoreType.DMA((20,)), pltpu.SemaphoreType.DMA((sems,)), pltpu.SemaphoreType.DMA((sems,)),
    ]
    return pl.pallas_call(
        whole_kernel,
        out_shape=out_shape,
        in_specs=[any_space] * 2 + [FULL] * 2 + [any_space] * 4 + [FULL] * 5,
        out_specs=[any_space] * 2 + [FULL] * 5 + [any_space],
        scratch_shapes=scratch,
        compiler_params=pltpu.CompilerParams(
            vmem_limit_bytes=67043328, collective_id=0, has_side_effects=True
        ),
    )(*operands)


def finish_kernel(out, grad_x, up, down, o_t, qkv, total, r_out, r_gx, r_qkv, r_o, r_up, r_down, r_qv, r_bup, r_bias, r_gain, r_shift):
    r_out[...] = out[...].astype(jnp.float32)
    r_gx[...] = grad_x[...].astype(jnp.float32)

    @pl.when(pl.program_id(0) == 0)
    def _():
        r_qkv[...] = qkv[...]
        r_o[...] = o_t[...]
        r_up[...] = up[...]
        r_down[...] = down[...]
        pick_small(total, lax.axis_index("mp"), lax.axis_index("dp"), r_qv, r_bup, r_bias, r_gain, r_shift)


def finish(parts, qv_shape, up_shape, pair_shape):
    parts = parts[:7]
    out, grad_x = parts[0], parts[1]
    block = pl.BlockSpec((1, 512, out.shape[2]), lambda step: (step // 2, step % 2, 0))
    fixed = lambda shape: pl.BlockSpec(shape, lambda step: (0,) * len(shape))
    f32 = jnp.float32
    order = (5, 4, 2, 3)
    shapes = [parts[k].shape for k in order] + [qv_shape, up_shape, pair_shape, pair_shape, pair_shape]
    return pl.pallas_call(
        finish_kernel,
        grid=(2 * out.shape[1] // 512,),
        out_shape=[jax.ShapeDtypeStruct(out.shape, f32)] * 2 + [jax.ShapeDtypeStruct(shape, f32) for shape in shapes],
        in_specs=[block, block] + [fixed(part.shape) for part in parts[2:]],
        out_specs=[block, block] + [fixed(shape) for shape in shapes],
    )(*parts)


def product(left, right):
    return jnp.dot(left, right, preferred_element_type=jnp.float32)


def normalize(values, scale_row, shift_row):
    row_mean = jnp.mean(values, axis=-1, keepdims=True)
    centred = values - row_mean
    inverse = lax.rsqrt(jnp.mean(centred * centred, axis=-1, keepdims=True) + epsilon)
    scaled = centred * inverse
    return (scaled * scale_row + shift_row, scaled, inverse)


def normalize_back(grad_rows, scaled, inverse, scale_row):
    inner = grad_rows * scale_row
    return inverse * (
        inner
        - jnp.mean(inner, axis=-1, keepdims=True)
        - scaled * jnp.mean(inner * scaled, axis=-1, keepdims=True)
    )


def gelu_slope(values):
    normal_cdf = 0.5 * (1.0 + lax.erf(values * 0.7071067811865476))
    density = jnp.exp(-0.5 * values * values) * 0.3989422804014327
    return normal_cdf + values * density


def permitted(chain_rows, keep_rows):
    slot_count = chain_rows.shape[0]
    same_chain = chain_rows[:, None] == chain_rows[None, :]
    diagonal = lax.broadcasted_iota(jnp.int32, (slot_count, slot_count), 0) == lax.broadcasted_iota(
        jnp.int32, (slot_count, slot_count), 1
    )
    return same_chain & ((keep_rows[None, :] == 1) | diagonal)


def head_scores(query, key_rows, allowed, head_count, head_width):
    query_heads = query.reshape(-1, head_count, head_width)
    key_heads = key_rows.reshape(-1, head_count, head_width)
    scores = jnp.einsum(
        "qhd,khd->hqk", query_heads, key_heads, preferred_element_type=jnp.float32
    ) * (1.0 / math.sqrt(head_width))
    return jnp.where(allowed[None], scores, masked_value)


def forward(rows_in, chain_rows, keep_rows, weights, join=lambda a: a):
    qkv_full, out_full, up_full, down_full, bias_qv, bias_up, bias_out, gain_full, shift_full = (
        weights
    )
    head_count = bias_qv.shape[1]
    head_width = bias_qv.shape[2]
    row_count = rows_in.shape[0]
    bias_qv = bias_qv.astype(jnp.float32)
    bias_out = bias_out.astype(jnp.float32)
    gain_full = gain_full.astype(jnp.float32)
    shift_full = shift_full.astype(jnp.float32)
    allowed = permitted(chain_rows, keep_rows)
    normed_one, scaled_one, inverse_one = normalize(rows_in, gain_full[0], shift_full[0])
    hidden_one = normed_one.astype(jnp.bfloat16)
    query = (product(hidden_one, qkv_full[0]) + bias_qv[0].reshape(-1)).astype(jnp.bfloat16)
    key_rows = product(hidden_one, qkv_full[1]).astype(jnp.bfloat16)
    value_rows = (product(hidden_one, qkv_full[2]) + bias_qv[1].reshape(-1)).astype(jnp.bfloat16)
    scores = head_scores(query, key_rows, allowed, head_count, head_width)
    row_top = jnp.max(scores, axis=-1, keepdims=True)
    log_total = jnp.log(jnp.sum(jnp.exp(scores - row_top), axis=-1, keepdims=True)) + row_top
    probs_low = jnp.exp(scores - log_total).astype(jnp.bfloat16)
    mixed = jnp.einsum(
        "hqk,khd->qhd",
        probs_low,
        value_rows.reshape(row_count, head_count, head_width),
        preferred_element_type=jnp.float32,
    )
    mixed = mixed.reshape(row_count, -1).astype(jnp.bfloat16)
    partial_attn = product(mixed, out_full)
    resid = rows_in + join(partial_attn) + bias_out[0]
    normed_two, scaled_two, inverse_two = normalize(resid, gain_full[1], shift_full[1])
    hidden_two = normed_two.astype(jnp.bfloat16)
    pre = product(hidden_two, up_full) + bias_up.astype(jnp.float32).reshape(-1)
    act = jax.nn.gelu(pre, approximate=False).astype(jnp.bfloat16)
    partial_ffn = product(act, down_full)
    result = (
        resid + join(partial_ffn.astype(jnp.bfloat16)).astype(jnp.float32) + bias_out[1]
    )
    kept = (
        allowed,
        scaled_one,
        inverse_one,
        hidden_one,
        query,
        key_rows,
        value_rows,
        log_total,
        mixed,
        scaled_two,
        inverse_two,
        hidden_two,
        pre,
        act,
    )
    return (result, kept)


def backward(grad_out, result, kept, weights, join=lambda a: a):
    qkv_full, out_full, up_full, down_full, bias_qv, bias_up, bias_out, gain_full, shift_full = (
        weights
    )
    (
        allowed,
        scaled_one,
        inverse_one,
        hidden_one,
        query,
        key_rows,
        value_rows,
        log_total,
        mixed,
        scaled_two,
        inverse_two,
        hidden_two,
        pre,
        act,
    ) = kept
    head_count = bias_qv.shape[1]
    head_width = bias_qv.shape[2]
    row_count = grad_out.shape[0]
    gain_full = gain_full.astype(jnp.float32)
    grad_low = grad_out.astype(jnp.bfloat16)
    grad_down = product(act.T, grad_low)
    grad_pre = (product(grad_low, down_full.T) * gelu_slope(pre)).astype(jnp.bfloat16)
    grad_bup = jnp.sum(grad_pre, axis=0, dtype=jnp.float32).reshape(bias_up.shape)
    grad_up = product(hidden_two.T, grad_pre)
    partial_two = product(grad_pre, up_full.T)
    grad_two = join(partial_two.astype(jnp.bfloat16)).astype(jnp.float32)
    gain_two = jnp.sum(grad_two * scaled_two, axis=0)
    shift_two = jnp.sum(grad_two, axis=0)
    grad_resid = grad_out + normalize_back(grad_two, scaled_two, inverse_two, gain_full[1])
    resid_low = grad_resid.astype(jnp.bfloat16)
    grad_out_proj = product(mixed.T, resid_low)
    grad_mixed = (
        product(resid_low, out_full.T)
        .astype(jnp.bfloat16)
        .reshape(row_count, head_count, head_width)
    )
    scores = head_scores(query, key_rows, allowed, head_count, head_width)
    probs = jnp.exp(scores - log_total)
    probs_low = probs.astype(jnp.bfloat16)
    value_heads = value_rows.reshape(row_count, head_count, head_width)
    grad_value = jnp.einsum(
        "hqk,qhd->khd", probs_low, grad_mixed, preferred_element_type=jnp.float32
    ).astype(jnp.bfloat16)
    grad_probs = jnp.einsum(
        "qhd,khd->hqk", grad_mixed, value_heads, preferred_element_type=jnp.float32
    )
    grad_scores = (
        probs * (grad_probs - jnp.sum(grad_probs * probs, axis=-1, keepdims=True))
    ).astype(jnp.bfloat16)
    score_scale = 1.0 / math.sqrt(head_width)
    key_heads = key_rows.reshape(row_count, head_count, head_width)
    query_heads = query.reshape(row_count, head_count, head_width)
    grad_query = (
        jnp.einsum("hqk,khd->qhd", grad_scores, key_heads, preferred_element_type=jnp.float32)
        * score_scale
    ).astype(jnp.bfloat16)
    grad_key = (
        jnp.einsum("hqk,qhd->khd", grad_scores, query_heads, preferred_element_type=jnp.float32)
        * score_scale
    ).astype(jnp.bfloat16)
    stacked = jnp.stack(
        [
            grad_query.reshape(row_count, -1),
            grad_key.reshape(row_count, -1),
            grad_value.reshape(row_count, -1),
        ]
    )
    grad_qkv = jnp.einsum("rd,crk->cdk", hidden_one, stacked, preferred_element_type=jnp.float32)
    partial_one = jnp.einsum("crk,cdk->rd", stacked, qkv_full, preferred_element_type=jnp.float32)
    grad_one = join(partial_one.astype(jnp.bfloat16)).astype(jnp.float32)
    grad_bqv = jnp.stack(
        [
            jnp.sum(stacked[0], axis=0, dtype=jnp.float32),
            jnp.sum(stacked[2], axis=0, dtype=jnp.float32),
        ]
    ).reshape(2, head_count, head_width)
    gain_one = jnp.sum(grad_one * scaled_one, axis=0)
    shift_one = jnp.sum(grad_one, axis=0)
    grad_in = grad_resid + normalize_back(grad_one, scaled_one, inverse_one, gain_full[0])
    small_sums = jnp.stack(
        [
            jnp.sum(grad_resid, axis=0),
            jnp.sum(grad_out, axis=0),
            gain_one,
            gain_two,
            shift_one,
            shift_two,
        ]
    )
    local_grads = (
        grad_qkv,
        grad_out_proj,
        grad_up,
        grad_down,
        grad_bqv,
        grad_bup,
        small_sums[0:2],
        small_sums[2:4],
        small_sums[4:6],
    )
    return (result, grad_in, local_grads)


def body_generic(
    activations,
    cotangent,
    w_qkv,
    w_o,
    w_up,
    w_down,
    b_qv,
    b_up,
    out_bias,
    norm_gain,
    norm_bias,
    chain_ids,
    key_keep,
):
    batch_count = activations.shape[0]
    outputs = []
    input_grads = []
    running = None
    for batch_index in range(batch_count):
        weights = (
            lax.all_gather(w_qkv, "dp", axis=1, tiled=True),
            lax.all_gather(w_o, "dp", axis=1, tiled=True),
            lax.all_gather(w_up, "dp", axis=0, tiled=True),
            lax.all_gather(w_down, "dp", axis=1, tiled=True),
            lax.all_gather(b_qv, "dp", axis=2, tiled=True),
            lax.all_gather(b_up, "dp", axis=1, tiled=True),
            lax.all_gather(out_bias, "dp", axis=1, tiled=True),
            lax.all_gather(norm_gain, "dp", axis=1, tiled=True),
            lax.all_gather(norm_bias, "dp", axis=1, tiled=True),
        )
        result, kept = forward(
            activations[batch_index].astype(jnp.float32),
            chain_ids[batch_index],
            key_keep[batch_index],
            weights,
            lambda a: lax.psum(a, "mp"),
        )
        live_rows = (chain_ids[batch_index] >= 0).astype(jnp.float32)[:, None]
        output_rows, grad_in, local_grads = backward(
            cotangent[batch_index].astype(jnp.float32) * live_rows, result, kept, weights, lambda a: lax.psum(a, "mp")
        )
        outputs.append(output_rows)
        input_grads.append(grad_in)
        shares = (
            lax.psum_scatter(
                local_grads[0].astype(jnp.bfloat16), "dp", scatter_dimension=1, tiled=True
            ).astype(jnp.float32),
            lax.psum_scatter(
                local_grads[1].astype(jnp.bfloat16), "dp", scatter_dimension=1, tiled=True
            ).astype(jnp.float32),
            lax.psum_scatter(
                local_grads[2].astype(jnp.bfloat16), "dp", scatter_dimension=0, tiled=True
            ).astype(jnp.float32),
            lax.psum_scatter(
                local_grads[3].astype(jnp.bfloat16), "dp", scatter_dimension=1, tiled=True
            ).astype(jnp.float32),
            lax.psum_scatter(
                local_grads[4].astype(jnp.bfloat16), "dp", scatter_dimension=2, tiled=True
            ).astype(jnp.float32),
            lax.psum_scatter(
                local_grads[5].astype(jnp.bfloat16), "dp", scatter_dimension=1, tiled=True
            ).astype(jnp.float32),
            lax.psum_scatter(
                local_grads[6].astype(jnp.bfloat16), "dp", scatter_dimension=1, tiled=True
            ).astype(jnp.float32),
            lax.psum_scatter(
                local_grads[7].astype(jnp.bfloat16), "dp", scatter_dimension=1, tiled=True
            ).astype(jnp.float32),
            lax.psum_scatter(
                local_grads[8].astype(jnp.bfloat16), "dp", scatter_dimension=1, tiled=True
            ).astype(jnp.float32),
        )
        if running is None:
            running = tuple(shares)
        else:
            running = tuple(jax.tree.map(jnp.add, tuple(running), tuple(shares)))
    return (
        jnp.stack(outputs),
        jnp.stack(input_grads),
        running[0],
        running[1],
        running[2],
        running[3],
        running[4],
        running[5],
        running[6],
        running[7],
        running[8],
    )


def fits(mesh):
    return mesh.shape["mp"] == 2 and mesh.shape["dp"] == 16


def body_split(
    activations,
    cotangent,
    w_qkv,
    w_o,
    w_up,
    w_down,
    b_qv,
    b_up,
    out_bias,
    norm_gain,
    norm_bias,
    chain_ids,
    key_keep,
):
    parts = whole(
        (activations, cotangent, chain_ids, key_keep, w_up, w_down.T, w_o.T, w_qkv, b_qv, b_up.T, out_bias, norm_gain, norm_bias),
        lax.axis_size("dp") // 4,
    )
    out, grad_x, qkv, o_t, up, down_t, qv, bup_t, bias, gain, shift = finish(parts, b_qv.shape, b_up.shape[::-1], out_bias.shape)
    return (out, grad_x, qkv, o_t.T, up, down_t.T, qv, bup_t.T, bias, gain, shift)


def solution(mesh):
    placed = (
        P(None, "dp", None),
        P(None, "dp", None),
        P(None, "dp", "mp"),
        P("mp", "dp"),
        P("dp", "mp"),
        P("mp", "dp"),
        P(None, "mp", "dp"),
        P("mp", "dp"),
        P(None, "dp"),
        P(None, "dp"),
        P(None, "dp"),
        P(None, "dp"),
        P(None, "dp"),
    )
    body = body_split if fits(mesh) else body_generic
    return jax.shard_map(
        body,
        mesh=mesh,
        in_specs=placed,
        out_specs=(
            P(None, "dp", None),
            P(None, "dp", None),
            P(None, "dp", "mp"),
            P("mp", "dp"),
            P("dp", "mp"),
            P("mp", "dp"),
            P(None, "mp", "dp"),
            P("mp", "dp"),
            P(None, "dp"),
            P(None, "dp"),
            P(None, "dp"),
        ),
        check_vma=False,
    )
```
